32 devices in a mesh: groups: 2 (over y), tile: 16 (over z, x, core).
Axes of the slice: x: 2, y: 2, z: 4, core: 2. Of those that a mesh axis runs over, the one named last changes fastest.
Arguments:
- features: bfloat16 [64, 12288], P(None, ('groups', 'tile')), parts along dimension 1, may hold values from -6 to 6
- rulebook: int32 [27, 12288], P(None, ('groups', 'tile')), parts along dimension 1, may hold values from 0 to 640, as said below
- send_lists: int32 [2, 32], P(None, ('groups', 'tile')), parts along dimension 1, may hold values from 0 to 3, as said below
- weight_first: bfloat16 [64, 1728], replicated, may hold values from -0.375 to 0.375
- weight_second: bfloat16 [64, 1728], replicated, may hold values from -0.75 to 0.75
- cotangent: bfloat16 [64, 12288], P(None, ('groups', 'tile')), parts along dimension 1, may hold values from -6 to 6
Outputs:
- out_features: bfloat16 [64, 12288], P(None, ('groups', 'tile')), parts along dimension 1
- d_features: bfloat16 [64, 12288], P(None, ('groups', 'tile')), parts along dimension 1
- grad_first: float32 [128, 1728], P('groups'), parts along dimension 0
- grad_second: float32 [128, 1728], P('groups'), parts along dimension 0
The draws below stay inside these ranges and needn't reach their ends.
There are 2 independent parts, one for each index of `groups`. The reference program is written for one: setup_inputs(seed, part) draws one part's arguments, and reference() takes and returns one part's arrays. A program takes and returns all parts, laid end to end along the dimension named above; an argument that names none is the same for every part. Nothing has to cross between parts.
Inputs may be any that keep to these rules, and one draw needn't show every extreme that they name: `rulebook`: A tile's rows are occupied cells of its box of 3 x 64 x 16 lattice cells, exactly 128 of them in each plane; tile t borders tile t - 1 below and t + 1 above along the first dimension. Offset k = 9 (a + 1) + 3 (b + 1) + (c + 1), with a, b, c in -1, 0, 1, names the occupied cell at that displacement, or 640 where that cell is empty or outside the detector; offset 27 // 2 names the row itself. If offset k of voxel v names voxel u, then offset 27 - 1 - k of u names v. Every halo row that is named lies in a listed block. `send_lists`: row 0 of a tile lists the distinct blocks of it that hold the cells of its lowest plane, row 1 those that hold the cells of its highest plane, 1 block each; the first tile lists nothing in row 0 and the last nothing in row 1, their entries being 3.
All inputs are finite; a program needn't handle non-finite values.
Results may differ from the reference program's by a relative error of at most 0.0042.
Values may be sent and summed in bfloat16 or wider, within the bound.
No kernel may reach another device: no remote copies, remote signals or barrier semaphores. Data moves between devices by JAX's collectives and lax.ppermute only.
A program may use at most 64 MiB of HBM per device.

```python
import math
import jax
import jax.numpy as jnp
from jax import lax

CHANNELS = 64
OFFSETS = 27
PLANES = 3
SIDE_Z = 16
PLANE_BLOCKS = 1
SIDE_Y = 64
VOX_DEV = 384
BLOCKS_DEV = 3
HALO_ROWS = 128
VOXELS = 6144
N_TILE = 16


def geometry(key):
    plane = SIDE_Y * SIDE_Z
    cells = PLANES * plane
    per_plane = PLANE_BLOCKS * 128
    missing = VOX_DEV + 2 * HALO_ROWS
    base = jax.random.fold_in(key, 4242)
    score_key, order_key = jax.random.split(base)
    plane_ids = jnp.arange(plane, dtype=jnp.int32)
    tiles = jnp.arange(N_TILE, dtype=jnp.int32)
    scores = jax.random.randint(score_key, (N_TILE, PLANES, plane), 0, 1 << 16, dtype=jnp.int32) * plane + plane_ids[None, None, :]
    picked = jnp.argsort(scores, axis=2, stable=True)[:, :, :per_plane].astype(jnp.int32)
    picked = jnp.sort(picked, axis=2) + (jnp.arange(PLANES, dtype=jnp.int32) * plane)[None, :, None]
    chosen = picked.reshape(N_TILE, VOX_DEV).astype(jnp.int32)
    perms = jax.vmap(lambda subkey: jax.random.permutation(subkey, BLOCKS_DEV).astype(jnp.int32))(jax.random.split(order_key, N_TILE))
    inverse = jnp.argsort(perms, axis=1, stable=True).astype(jnp.int32)
    positions = jnp.arange(VOX_DEV, dtype=jnp.int32)
    old_positions = jnp.full((N_TILE, cells), -1, jnp.int32).at[tiles[:, None], chosen].set(jnp.broadcast_to(positions[None, :], (N_TILE, VOX_DEV)))
    lowest = jnp.sum((chosen < plane).astype(jnp.int32), axis=1)
    highest = jnp.sum((chosen >= cells - plane).astype(jnp.int32), axis=1)
    low_count = jnp.where(tiles == 0, 0, (lowest + 127) // 128)
    high_count = jnp.where(tiles == N_TILE - 1, 0, (highest + 127) // 128)
    slots = jnp.arange(PLANE_BLOCKS, dtype=jnp.int32)[None, :]
    down_list = jnp.where(slots < low_count[:, None], inverse[:, :PLANE_BLOCKS], BLOCKS_DEV)
    up_old = jnp.clip(BLOCKS_DEV - high_count[:, None] + slots, 0, BLOCKS_DEV - 1)
    up_list = jnp.where(slots < high_count[:, None], jnp.take_along_axis(inverse, up_old, axis=1), BLOCKS_DEV)
    lists = jnp.stack([down_list, up_list]).reshape(2, N_TILE * PLANE_BLOCKS).astype(jnp.int32)
    rows = jnp.arange(VOX_DEV, dtype=jnp.int32)
    old_of_row = perms[:, rows // 128] * 128 + (rows % 128)[None, :]
    cell = jnp.take_along_axis(chosen, old_of_row, axis=1)
    coord_x = cell // plane
    coord_y = cell % plane // SIDE_Z
    coord_z = cell % SIDE_Z
    offsets = jnp.arange(OFFSETS, dtype=jnp.int32)[:, None, None]
    near_x = coord_x[None] + offsets // 9 - 1
    near_y = coord_y[None] + offsets // 3 % 3 - 1
    near_z = coord_z[None] + offsets % 3 - 1
    inside = (near_y >= 0) & (near_y < SIDE_Y) & (near_z >= 0) & (near_z < SIDE_Z)
    across = jnp.clip(near_y, 0, SIDE_Y - 1) * SIDE_Z + jnp.clip(near_z, 0, SIDE_Z - 1)
    owner = tiles[None, :, None]
    here = old_positions[owner, jnp.clip(near_x, 0, PLANES - 1) * plane + across]
    here_safe = jnp.maximum(here, 0)
    here_rule = inverse[owner, here_safe // 128] * 128 + here_safe % 128
    below_tile = jnp.clip(owner - 1, 0, N_TILE - 1)
    below = old_positions[below_tile, (PLANES - 1) * plane + across]
    below_safe = jnp.maximum(below, 0)
    below_rule = VOX_DEV + (below_safe // 128 - (BLOCKS_DEV - high_count[below_tile])) * 128 + below_safe % 128
    above_tile = jnp.clip(owner + 1, 0, N_TILE - 1)
    above = old_positions[above_tile, across]
    above_rule = VOX_DEV + HALO_ROWS + jnp.maximum(above, 0)
    rule = jnp.where((near_x >= 0) & (near_x < PLANES) & (here >= 0), here_rule, missing)
    rule = jnp.where((near_x < 0) & (owner > 0) & (below >= 0), below_rule, rule)
    rule = jnp.where((near_x >= PLANES) & (owner < N_TILE - 1) & (above >= 0), above_rule, rule)
    rule = jnp.where(inside, rule, missing)
    return (rule.reshape(OFFSETS, N_TILE * VOX_DEV).astype(jnp.int32), lists)


def draw_rulebook(key, part):
    return geometry(key)[0]


def draw_send_lists(key, part):
    return geometry(key)[1]


def level_of(stream_key, extent, cuts, low, high):
    loudness, own = 1.0, jax.random.fold_in(stream_key, 6)
    for axis_at, blocks in cuts:
        heights = jnp.exp(jax.random.uniform(jax.random.fold_in(own, axis_at), (blocks,), jnp.float32, low / len(cuts), high / len(cuts)))
        loudness = loudness * jnp.repeat(heights, extent[axis_at] // blocks).reshape([-1 if axis == axis_at else 1 for axis in range(len(extent))])
    return loudness


def bell_draw(rng, dims, scale, most, cuts=(), kind=jnp.bfloat16):
    entries = jax.random.normal(rng, dims, jnp.float32) * scale
    if len(cuts) > 0:
        entries = level_of(rng, dims, cuts, -0.22, 0.18) * entries
    return jnp.clip(entries, min=-most, max=most).astype(kind)


def setup_inputs(seed: int = 0, part: int = 0) -> dict:
    splits = jax.random.split(jax.random.key(seed), 7)
    part_splits = jax.random.split(jax.random.fold_in(splits[6], part), 7)
    return {
        "features": bell_draw(part_splits[0], (CHANNELS, VOXELS), 1.0, 6.0, ((1, 16),)),
        "rulebook": draw_rulebook(jax.random.fold_in(jax.random.fold_in(splits[6], part), 71), part),
        "send_lists": draw_send_lists(jax.random.fold_in(jax.random.fold_in(splits[6], part), 71), part),
        "weight_first": bell_draw(splits[3], (CHANNELS, OFFSETS * CHANNELS), (OFFSETS * CHANNELS // 6) ** -0.5, 0.375),
        "weight_second": bell_draw(splits[4], (CHANNELS, OFFSETS * CHANNELS), (OFFSETS * CHANNELS // 24) ** -0.5, 0.75),
        "cotangent": bell_draw(part_splits[5], (CHANNELS, VOXELS), 1.0, 6.0, ((1, 16),)),
    }


def global_index(rulebook, send_lists):
    ids = rulebook.reshape(OFFSETS, N_TILE, VOX_DEV)
    lists = send_lists.reshape(2, N_TILE, PLANE_BLOCKS)
    tiles = jnp.arange(N_TILE, dtype=jnp.int32)[None, :, None]
    below_tile = jnp.clip(tiles - 1, 0, N_TILE - 1)
    above_tile = jnp.clip(tiles + 1, 0, N_TILE - 1)
    low_offset = jnp.clip(ids - VOX_DEV, 0, HALO_ROWS - 1)
    high_offset = jnp.clip(ids - VOX_DEV - HALO_ROWS, 0, HALO_ROWS - 1)
    below_block = lists[1][below_tile, low_offset // 128]
    above_block = lists[0][above_tile, high_offset // 128]
    below_row = below_tile * VOX_DEV + below_block * 128 + low_offset % 128
    above_row = above_tile * VOX_DEV + above_block * 128 + high_offset % 128
    result = jnp.full(ids.shape, VOXELS, jnp.int32)
    result = jnp.where(ids < VOX_DEV, tiles * VOX_DEV + ids, result)
    lower_ok = (ids >= VOX_DEV) & (ids < VOX_DEV + HALO_ROWS) & (tiles > 0) & (below_block < BLOCKS_DEV)
    upper_ok = (ids >= VOX_DEV + HALO_ROWS) & (ids < VOX_DEV + 2 * HALO_ROWS) & (tiles < N_TILE - 1) & (above_block < BLOCKS_DEV)
    result = jnp.where(lower_ok, below_row, result)
    result = jnp.where(upper_ok, above_row, result)
    return result.transpose(1, 0, 2).astype(jnp.int32)

def padded_of(values):
    return jnp.concatenate([values, jnp.zeros((values.shape[0], 1), values.dtype)], axis=1)

def columns_of(padded, indices):
    gathered = padded[:, indices]
    return gathered.transpose(1, 0, 2).reshape(-1, indices.shape[1])

def convolve(weight, values, index):
    padded = padded_of(values)
    result = lax.map(lambda indices: jnp.dot(weight, columns_of(padded, indices), preferred_element_type=jnp.float32), index)
    return result.transpose(1, 0, 2).reshape(values.shape[0], -1)

def weight_grad(grads, values, index):
    width = grads.shape[0]
    padded = padded_of(values)
    pieces = grads.reshape(width, N_TILE, VOX_DEV).transpose(1, 0, 2)

    def step(total, pair):
        piece, indices = pair
        term = lax.dot_general(piece, columns_of(padded, indices), (((1,), (1,)), ((), ())), preferred_element_type=jnp.float32)
        return (total + term, None)
    total, unused = lax.scan(step, jnp.zeros((width, OFFSETS * width), jnp.float32), (pieces, index))
    return total

def spread_back(weight, grads, index):
    width = grads.shape[0]
    pieces = grads.reshape(width, N_TILE, VOX_DEV).transpose(1, 0, 2)

    def step(total, pair):
        piece, indices = pair
        terms = jnp.dot(weight.T, piece, preferred_element_type=jnp.float32)
        terms = terms.reshape(OFFSETS, width, -1).transpose(1, 0, 2)
        return (total.at[:, indices].add(terms), None)
    total, unused = lax.scan(step, jnp.zeros((width, VOXELS + 1), jnp.float32), (pieces, index))
    return total[:, :VOXELS]

def reference(features, rulebook, send_lists, weight_first, weight_second, cotangent):
    index = global_index(rulebook, send_lists)
    pre_first = convolve(weight_first, features, index)
    hidden = jax.nn.silu(pre_first).astype(jnp.bfloat16)
    out_features = (convolve(weight_second, hidden, index) + features.astype(jnp.float32)).astype(jnp.bfloat16)
    scale = 1.0 / math.sqrt(VOXELS)
    grad_second = weight_grad(cotangent, hidden, index) * scale
    d_hidden = spread_back(weight_second, cotangent, index)
    sigma = jax.nn.sigmoid(pre_first)
    d_pre = (d_hidden * sigma * (1.0 + pre_first * (1.0 - sigma))).astype(jnp.bfloat16)
    grad_first = weight_grad(d_pre, features, index) * scale
    d_features = (cotangent.astype(jnp.float32) + spread_back(weight_first, d_pre, index)).astype(jnp.bfloat16)
    return (out_features, d_features, grad_first, grad_second)
```

```python
import functools
import math

import jax
import jax.numpy as jnp
from jax import lax
from jax.experimental import pallas as pl
from jax.experimental.pallas import tpu as pltpu
from jax.sharding import PartitionSpec as P

BLOCK = 128
F32, BF16 = jnp.float32, jnp.bfloat16
VMEM = pl.BlockSpec(memory_space=pltpu.VMEM)
SMEM = pl.BlockSpec(memory_space=pltpu.SMEM)
NT = (((1,), (1,)), ((), ()))


def pair_blocks(lists_ref, odd):
    lower, upper = lists_ref[0, 0], lists_ref[1, 0]
    return jnp.where(odd, lower, upper), jnp.where(odd, upper, lower)


def payload_kernel(lists_ref, odd_ref, top_ref, bottom_ref, near_ref, far_ref):
    width, rows = top_ref.shape
    blocks = rows // BLOCK
    picks = pair_blocks(lists_ref, odd_ref[0] == 1)
    for pick, out_ref in zip(picks, (near_ref, far_ref)):
        start = pl.multiple_of(jnp.minimum(pick, blocks - 1) * BLOCK, BLOCK)
        listed = pick < blocks
        for half, ref in enumerate((top_ref, bottom_ref)):
            piece = ref[:, pl.ds(start, BLOCK)]
            out_ref[half * width : (half + 1) * width, :] = jnp.where(
                listed, piece, jnp.zeros_like(piece)
            )


def fill_halo(table_ref, near_ref, far_ref, odd, blocks):
    near, far = near_ref[...], far_ref[...]
    table_ref[blocks] = jnp.where(odd, near, far)
    table_ref[blocks + 1] = jnp.where(odd, far, near)


def gather(table_ref, rule_ref, first_ref, second_ref, blocks):
    offsets = rule_ref.shape[0]
    group = offsets // 3
    sources, channels, _ = table_ref.shape
    width = channels // 2
    source_rows = lax.broadcasted_iota(jnp.int32, (BLOCK, BLOCK), 0)

    def store(k, low, high, found, mirrored):
        first_ref[k * width : (k + 1) * width, low:high] = found[:width].astype(BF16)
        second_ref[mirrored * width : (mirrored + 1) * width, low:high] = found[
            width:
        ].astype(BF16)

    strays = jnp.zeros((group, BLOCK), jnp.int32)
    for block in range(blocks):
        low, high = block * BLOCK, (block + 1) * BLOCK
        for side in range(3):
            entries = rule_ref[side * group : (side + 1) * group, low:high]
            if side == 1:
                source = block
            else:
                least = jnp.min(entries.astype(F32)).astype(jnp.int32)
                source = jnp.minimum(least // BLOCK, sources - 1)
            local = entries - source * BLOCK
            named = entries < sources * BLOCK
            strays = strays | (
                named & ((local < 0) | (local >= BLOCK))
            ).astype(jnp.int32)
            table = table_ref[source]
            for j in range(group):
                k = side * group + j
                choice = (source_rows == local[j : j + 1]).astype(F32).astype(BF16)
                found = jnp.dot(table, choice, preferred_element_type=F32)
                store(k, low, high, found, offsets - 1 - k)

    @pl.when(jnp.max(strays.astype(F32)) > 0)
    def _():
        rows = rule_ref.shape[1]
        every_row = lax.broadcasted_iota(jnp.int32, (BLOCK, rows), 0)

        def one(k, carry):
            line = rule_ref[pl.ds(k, 1), :]
            found = jnp.zeros((channels, rows), F32)
            for source in range(sources):
                choice = (every_row == line - source * BLOCK).astype(F32).astype(BF16)
                found += jnp.dot(table_ref[source], choice, preferred_element_type=F32)
            here = pl.multiple_of(k * width, width)
            there = pl.multiple_of((offsets - 1 - k) * width, width)
            first_ref[pl.ds(here, width), :] = found[:width].astype(BF16)
            second_ref[pl.ds(there, width), :] = found[width:].astype(BF16)
            return carry

        lax.fori_loop(0, offsets, one, 0)


def turn(weight_ref, turned_ref):
    width, depth = weight_ref.shape
    offsets = depth // width
    for k in range(0, offsets, 2):
        count = min(2, offsets - k)
        block = weight_ref[:, k * width : (k + count) * width].astype(F32).T
        pieces = [block[i * width : (i + 1) * width] for i in range(count)]
        joined = pieces[0] if count == 1 else jnp.concatenate(pieces, axis=1)
        turned_ref[:, k * width : (k + count) * width] = joined.astype(BF16)


def first_kernel(
    lists_ref, odd_ref, rule_ref, x_ref, g_ref, near_ref, far_ref, w1_ref, w2_ref,
    state_ref, near_out, far_out, keep_ref, send_ref,
    table_ref, xs_ref, gs_ref, turned_ref,
):
    width, rows = x_ref.shape
    blocks = rows // BLOCK
    offsets = rule_ref.shape[0]
    odd = odd_ref[0] == 1
    for block in range(blocks):
        low, high = block * BLOCK, (block + 1) * BLOCK
        table_ref[block, :width] = x_ref[:, low:high]
        table_ref[block, width:] = g_ref[:, low:high]
    fill_halo(table_ref, near_ref, far_ref, odd, blocks)
    turn(w2_ref, turned_ref)
    gather(table_ref, rule_ref, xs_ref, gs_ref, blocks)
    pre = jnp.dot(w1_ref[...], xs_ref[...], preferred_element_type=F32)
    d_hidden = jnp.dot(turned_ref[...], gs_ref[...], preferred_element_type=F32)
    sigma = jax.nn.sigmoid(pre)
    hidden = (pre * sigma).astype(BF16)
    d_pre = (d_hidden * sigma * (1.0 + pre * (1.0 - sigma))).astype(BF16)
    for block in range(blocks):
        low, high = block * BLOCK, (block + 1) * BLOCK
        state_ref[block, :width] = hidden[:, low:high]
        state_ref[block, width:] = d_pre[:, low:high]
    for pick, out_ref in zip(pair_blocks(lists_ref, odd), (near_out, far_out)):
        piece = state_ref[jnp.minimum(pick, blocks - 1)]
        out_ref[...] = jnp.where(pick < blocks, piece, jnp.zeros_like(piece))
    grad_first = lax.dot_general(d_pre, xs_ref[...], NT, preferred_element_type=F32)
    stacked = lax.dot_general(gs_ref[...], hidden, NT, preferred_element_type=F32)
    for k in range(0, offsets, 2):
        count = min(2, offsets - k)
        low, high = k * width, (k + count) * width
        pieces = [stacked[low + i * width : low + (i + 1) * width] for i in range(count)]
        second = pieces[0] if count == 1 else jnp.concatenate(pieces, axis=1)
        first = grad_first[:, low:high]
        keep_ref[:, low:high] = jnp.where(odd, second, first)
        send_ref[:, low:high] = jnp.where(odd, first, second).astype(BF16)


def second_kernel(
    odd_ref, rule_ref, state_ref, near_ref, far_ref, w1_ref, w2_ref, x_ref, g_ref,
    out_ref, dx_ref,
    table_ref, hs_ref, ds_ref, turned_ref,
):
    width, rows = x_ref.shape
    blocks = rows // BLOCK
    odd = odd_ref[0] == 1
    for block in range(blocks):
        table_ref[block] = state_ref[block]
    fill_halo(table_ref, near_ref, far_ref, odd, blocks)
    turn(w1_ref, turned_ref)
    gather(table_ref, rule_ref, hs_ref, ds_ref, blocks)
    second = jnp.dot(w2_ref[...], hs_ref[...], preferred_element_type=F32)
    out_ref[...] = (second + x_ref[...].astype(F32)).astype(BF16)
    d_input = jnp.dot(turned_ref[...], ds_ref[...], preferred_element_type=F32)
    dx_ref[...] = (d_input + g_ref[...].astype(F32)).astype(BF16)


def neighbour_pairs(count):
    near = [(i, i ^ 1) for i in range(count) if i ^ 1 < count]
    far = [(i, i + 1 if i % 2 else i - 1) for i in range(count)]
    return near, [(i, j) for i, j in far if 0 <= j < count]


def total_over_tiles(keep, send, odd, first_scale):
    count = lax.axis_size("tile")
    received = lax.ppermute(send, "tile", [(i, i ^ 1) for i in range(count)])
    total = keep + received.astype(F32)
    bits = [1 << b for b in range(1, count.bit_length() - 1)]
    for step, (even_bit, odd_bit) in enumerate(zip(bits, bits[-1:] + bits[:-1])):
        wire = BF16 if step >= len(bits) - 3 else F32
        pairs = [(i, i ^ (odd_bit if i % 2 else even_bit)) for i in range(count)]
        sent = total.astype(wire)
        total = sent.astype(F32) + lax.ppermute(sent, "tile", pairs).astype(F32)
    total = total * first_scale
    other = lax.ppermute(total, "tile", [(i, i ^ 1) for i in range(count)])
    return jnp.where(odd, other, total), jnp.where(odd, total, other)


def body(features, rulebook, send_lists, weight_first, weight_second, cotangent):
    width, rows = features.shape
    offsets = rulebook.shape[0]
    blocks = rows // BLOCK
    count = lax.axis_size("tile")
    parity = lax.axis_index("tile") % 2
    odd = parity == 1
    parity = parity.reshape(1).astype(jnp.int32)
    near_pairs, far_pairs = neighbour_pairs(count)
    shape = jax.ShapeDtypeStruct
    rim = shape((2 * width, BLOCK), BF16)

    near, far = pl.pallas_call(
        payload_kernel,
        out_shape=(rim, rim),
        in_specs=[SMEM, SMEM, VMEM, VMEM],
        out_specs=(VMEM, VMEM),
    )(send_lists, parity, features, cotangent)
    near = lax.ppermute(near, "tile", near_pairs)
    far = lax.ppermute(far, "tile", far_pairs)

    scratch = [
        pltpu.VMEM((blocks + 2, 2 * width, BLOCK), BF16),
        pltpu.VMEM((offsets * width, rows), BF16),
        pltpu.VMEM((offsets * width, rows), BF16),
        pltpu.VMEM((width, offsets * width), BF16),
    ]
    state, near, far, keep, send = pl.pallas_call(
        first_kernel,
        out_shape=(
            shape((blocks, 2 * width, BLOCK), BF16), rim, rim,
            shape((width, offsets * width), F32), shape((width, offsets * width), BF16),
        ),
        in_specs=[SMEM, SMEM] + [VMEM] * 7,
        out_specs=(VMEM,) * 5,
        scratch_shapes=scratch,
    )(send_lists, parity, rulebook, features, cotangent, near, far, weight_first, weight_second)

    near = lax.ppermute(near, "tile", near_pairs)
    far = lax.ppermute(far, "tile", far_pairs)
    out_features, d_features = pl.pallas_call(
        second_kernel,
        out_shape=(shape((width, rows), BF16), shape((width, rows), BF16)),
        in_specs=[SMEM] + [VMEM] * 8,
        out_specs=(VMEM, VMEM),
        scratch_shapes=scratch,
        cost_estimate=pl.CostEstimate(
            flops=2 * 2 * width * offsets * rows * (width + BLOCK),
            bytes_accessed=4 * offsets * width * rows,
            transcendentals=0,
        ),
    )(parity, rulebook, state, near, far, weight_first, weight_second, features, cotangent)

    scale = 1.0 / math.sqrt(rows * count)
    grad_first, grad_second = total_over_tiles(keep, send, odd, scale)
    return out_features, d_features, grad_first, grad_second


def solution(mesh):
    placed = (
        P(None, ("groups", "tile")),
        P(None, ("groups", "tile")),
        P(None, ("groups", "tile")),
        P(),
        P(),
        P(None, ("groups", "tile")),
    )
    return jax.shard_map(
        body,
        mesh=mesh,
        in_specs=placed,
        out_specs=(
            P(None, ("groups", "tile")),
            P(None, ("groups", "tile")),
            P("groups", None),
            P("groups", None),
        ),
        check_vma=False,
    )
```

```python
import math

import jax
import jax.numpy as jnp
from jax import lax
from jax.experimental import pallas as pl
from jax.experimental.pallas import tpu as pltpu
from jax.sharding import PartitionSpec as P


BLOCK = 128
F32, BF16 = jnp.float32, jnp.bfloat16
HBM = pl.BlockSpec(memory_space=pltpu.HBM)
SMALL = pltpu.CompilerParams(vmem_limit_bytes=1 << 20)
MEDIUM = pltpu.CompilerParams(vmem_limit_bytes=20 << 20)
VMEM = pl.BlockSpec(memory_space=pltpu.VMEM)
SMEM = pl.BlockSpec(memory_space=pltpu.SMEM)
NT = (((1,), (1,)), ((), ()))


def pair_blocks(lists_ref, odd):
    lower, upper = lists_ref[0], lists_ref[1]
    return jnp.where(odd, lower, upper), jnp.where(odd, upper, lower)


def fetch(sources, targets, sems):
    copies = [
        pltpu.make_async_copy(source, target, sems.at[i])
        for i, (source, target) in enumerate(zip(sources, targets))
    ]
    for copy in copies:
        copy.start()
    return copies


def payload_kernel(
    lists_hbm, odd_ref, x_hbm, g_hbm, near_ref, far_ref, lists_ref, x_ref, g_ref, sems
):
    width, rows = x_ref.shape
    copies = fetch((lists_hbm, x_hbm, g_hbm), (lists_ref, x_ref, g_ref), sems)
    for copy in copies:
        copy.wait()
    picks = pair_blocks(lists_ref, odd_ref[0] == 1)
    for pick, out_ref in zip(picks, (near_ref, far_ref)):
        start = pl.multiple_of(jnp.minimum(pick, rows // BLOCK - 1) * BLOCK, BLOCK)
        out_ref[:width, :] = x_ref[:, pl.ds(start, BLOCK)]
        out_ref[width:, :] = g_ref[:, pl.ds(start, BLOCK)]


def fill_halo(table_ref, near_ref, far_ref, odd, blocks):
    near, far = near_ref[...], far_ref[...]
    table_ref[blocks] = jnp.where(odd, near, far)
    table_ref[blocks + 1] = jnp.where(odd, far, near)


def gather(table_ref, rule_ref, first_ref, second_ref, blocks):
    offsets = rule_ref.shape[0]
    group = offsets // 3
    sources, channels, _ = table_ref.shape
    width = channels // 2
    source_rows = lax.broadcasted_iota(jnp.int32, (BLOCK, BLOCK), 0)

    def store(k, low, high, found, mirrored):
        first_ref[k * width : (k + 1) * width, low:high] = found[:width].astype(BF16)
        second_ref[mirrored * width : (mirrored + 1) * width, low:high] = found[
            width:
        ].astype(BF16)

    strays = jnp.zeros((group, BLOCK), jnp.int32)
    for block in range(blocks):
        low, high = block * BLOCK, (block + 1) * BLOCK
        for side in range(3):
            entries = rule_ref[side * group : (side + 1) * group, low:high]
            if side == 1:
                source = block
            else:
                least = jnp.min(entries.astype(F32)).astype(jnp.int32)
                source = jnp.minimum(least // BLOCK, sources - 1)
            local = entries - source * BLOCK
            named = entries < sources * BLOCK
            strays = strays | (
                named & ((local < 0) | (local >= BLOCK))
            ).astype(jnp.int32)
            table = table_ref[source]
            for j in range(group):
                k = side * group + j
                choice = (source_rows == local[j : j + 1]).astype(F32).astype(BF16)
                found = jnp.dot(table, choice, preferred_element_type=F32)
                store(k, low, high, found, offsets - 1 - k)

    @pl.when(jnp.max(strays.astype(F32)) > 0)
    def _():
        rows = rule_ref.shape[1]
        every_row = lax.broadcasted_iota(jnp.int32, (BLOCK, rows), 0)

        def one(k, carry):
            line = rule_ref[pl.ds(k, 1), :]
            found = jnp.zeros((channels, rows), F32)
            for source in range(sources):
                choice = (every_row == line - source * BLOCK).astype(F32).astype(BF16)
                found += jnp.dot(table_ref[source], choice, preferred_element_type=F32)
            here = pl.multiple_of(k * width, width)
            there = pl.multiple_of((offsets - 1 - k) * width, width)
            first_ref[pl.ds(here, width), :] = found[:width].astype(BF16)
            second_ref[pl.ds(there, width), :] = found[width:].astype(BF16)
            return carry

        lax.fori_loop(0, offsets, one, 0)


def turn(weight_ref, turned_ref):
    width, depth = weight_ref.shape
    offsets = depth // width
    for k in range(0, offsets, 2):
        count = min(2, offsets - k)
        block = weight_ref[:, k * width : (k + count) * width].astype(F32).T
        pieces = [block[i * width : (i + 1) * width] for i in range(count)]
        joined = pieces[0] if count == 1 else jnp.concatenate(pieces, axis=1)
        turned_ref[:, k * width : (k + count) * width] = joined.astype(BF16)


def first_kernel(
    odd_ref, near_ref, far_ref, lists_hbm, rule_hbm, x_hbm, g_hbm, w1_hbm, w2_hbm,
    state_ref, near_out, far_out, keep_ref, send_ref,
    table_ref, xs_ref, gs_ref, turned_ref,
    lists_ref, rule_ref, x_ref, g_ref, w1_ref, w2_ref, sems,
):
    copies = fetch(
        (lists_hbm, rule_hbm, x_hbm, g_hbm, w2_hbm, w1_hbm),
        (lists_ref, rule_ref, x_ref, g_ref, w2_ref, w1_ref),
        sems,
    )
    width, rows = x_ref.shape
    blocks = rows // BLOCK
    offsets = rule_ref.shape[0]
    odd = odd_ref[0] == 1
    for copy in copies[:4]:
        copy.wait()
    for block in range(blocks):
        low, high = block * BLOCK, (block + 1) * BLOCK
        table_ref[block, :width] = x_ref[:, low:high]
        table_ref[block, width:] = g_ref[:, low:high]
    fill_halo(table_ref, near_ref, far_ref, odd, blocks)
    gather(table_ref, rule_ref, xs_ref, gs_ref, blocks)
    for copy in copies[4:]:
        copy.wait()
    turn(w2_ref, turned_ref)
    pre = jnp.dot(w1_ref[...], xs_ref[...], preferred_element_type=F32)
    d_hidden = jnp.dot(turned_ref[...], gs_ref[...], preferred_element_type=F32)
    sigma = jax.nn.sigmoid(pre)
    hidden = (pre * sigma).astype(BF16)
    d_pre = (d_hidden * sigma * (1.0 + pre * (1.0 - sigma))).astype(BF16)
    for block in range(blocks):
        low, high = block * BLOCK, (block + 1) * BLOCK
        state_ref[block, :width] = hidden[:, low:high]
        state_ref[block, width:] = d_pre[:, low:high]
    for pick, out_ref in zip(pair_blocks(lists_ref, odd), (near_out, far_out)):
        piece = state_ref[jnp.minimum(pick, blocks - 1)]
        out_ref[...] = jnp.where(pick < blocks, piece, jnp.zeros_like(piece))
    grad_first = lax.dot_general(d_pre, xs_ref[...], NT, preferred_element_type=F32)
    stacked = lax.dot_general(gs_ref[...], hidden, NT, preferred_element_type=F32)
    for k in range(0, offsets, 2):
        count = min(2, offsets - k)
        low, high = k * width, (k + count) * width
        pieces = [stacked[low + i * width : low + (i + 1) * width] for i in range(count)]
        second = pieces[0] if count == 1 else jnp.concatenate(pieces, axis=1)
        first = grad_first[:, low:high]
        keep_ref[:, low:high] = jnp.where(odd, second, first)
        send_ref[:, low:high] = jnp.where(odd, first, second).astype(BF16)


def second_kernel(
    odd_ref, near_ref, far_ref, state_ref, rule_hbm, x_hbm, g_hbm, w1_hbm, w2_hbm,
    out_ref, dx_ref,
    table_ref, hs_ref, ds_ref, turned_ref,
    rule_ref, x_ref, g_ref, w1_ref, w2_ref, sems,
):
    copies = fetch(
        (rule_hbm, w1_hbm, w2_hbm, x_hbm, g_hbm),
        (rule_ref, w1_ref, w2_ref, x_ref, g_ref),
        sems,
    )
    _, rows = x_ref.shape
    blocks = rows // BLOCK
    odd = odd_ref[0] == 1
    for block in range(blocks):
        table_ref[block] = state_ref[block]
    fill_halo(table_ref, near_ref, far_ref, odd, blocks)
    copies[0].wait()
    gather(table_ref, rule_ref, hs_ref, ds_ref, blocks)
    for copy in copies[1:]:
        copy.wait()
    turn(w1_ref, turned_ref)
    second = jnp.dot(w2_ref[...], hs_ref[...], preferred_element_type=F32)
    out_ref[...] = (second + x_ref[...].astype(F32)).astype(BF16)
    d_input = jnp.dot(turned_ref[...], ds_ref[...], preferred_element_type=F32)
    dx_ref[...] = (d_input + g_ref[...].astype(F32)).astype(BF16)


def neighbour_pairs(count):
    near = [(i, i ^ 1) for i in range(count) if i ^ 1 < count]
    far = [(i, i + 1 if i % 2 else i - 1) for i in range(count)]
    return near, [(i, j) for i, j in far if 0 <= j < count]


def total_over_tiles(keep, send, odd, first_scale):
    count = lax.axis_size("tile")
    received = lax.ppermute(send, "tile", [(i, i ^ 1) for i in range(count)])
    total = keep + received.astype(F32)
    bits = [1 << b for b in range(1, count.bit_length() - 1)]
    for step, (even_bit, odd_bit) in enumerate(zip(bits, bits[-1:] + bits[:-1])):
        wire = BF16 if step >= len(bits) - 3 else F32
        pairs = [(i, i ^ (odd_bit if i % 2 else even_bit)) for i in range(count)]
        sent = total.astype(wire)
        received = lax.ppermute(sent, "tile", pairs)
        total = sent.astype(F32) + received.astype(F32)
    total = total * first_scale
    other = lax.ppermute(total, "tile", [(i, i ^ 1) for i in range(count)])
    return jnp.where(odd, other, total), jnp.where(odd, total, other)


def body(features, rulebook, send_lists, weight_first, weight_second, cotangent):
    width, rows = features.shape
    offsets = rulebook.shape[0]
    blocks = rows // BLOCK
    count = lax.axis_size("tile")
    parity = lax.axis_index("tile") % 2
    odd = parity == 1
    parity = parity.reshape(1).astype(jnp.int32)
    send_lists = send_lists.reshape(2)
    features, cotangent, rulebook, weight_first, weight_second, send_lists = (
        pltpu.with_memory_space_constraint(array, pltpu.HBM)
        for array in (features, cotangent, rulebook, weight_first, weight_second, send_lists)
    )
    near_pairs, far_pairs = neighbour_pairs(count)
    shape = jax.ShapeDtypeStruct
    rim = shape((2 * width, BLOCK), BF16)

    near, far = pl.pallas_call(
        payload_kernel,
        out_shape=(rim, rim),
        in_specs=[HBM, SMEM, HBM, HBM],
        out_specs=(VMEM, VMEM),
        scratch_shapes=[
            pltpu.SMEM((2,), jnp.int32),
            pltpu.VMEM((width, rows), BF16),
            pltpu.VMEM((width, rows), BF16),
            pltpu.SemaphoreType.DMA((3,)),
        ],
        compiler_params=SMALL,
    )(send_lists, parity, features, cotangent)
    far = lax.ppermute(far, "tile", far_pairs)
    near = lax.ppermute(near, "tile", near_pairs)

    scratch = [
        pltpu.VMEM((blocks + 2, 2 * width, BLOCK), BF16),
        pltpu.VMEM((offsets * width, rows), BF16),
        pltpu.VMEM((offsets * width, rows), BF16),
        pltpu.VMEM((width, offsets * width), BF16),
    ]
    inputs = [
        pltpu.VMEM((offsets, rows), jnp.int32),
        pltpu.VMEM((width, rows), BF16),
        pltpu.VMEM((width, rows), BF16),
        pltpu.VMEM((width, offsets * width), BF16),
        pltpu.VMEM((width, offsets * width), BF16),
        pltpu.SemaphoreType.DMA((6,)),
    ]
    arrays = (rulebook, features, cotangent, weight_first, weight_second)
    state, near, far, keep, send = pl.pallas_call(
        first_kernel,
        out_shape=(
            shape((blocks, 2 * width, BLOCK), BF16), rim, rim,
            shape((width, offsets * width), F32), shape((width, offsets * width), BF16),
        ),
        in_specs=[SMEM, VMEM, VMEM] + [HBM] * 6,
        out_specs=(VMEM,) * 5,
        scratch_shapes=scratch + [pltpu.SMEM((2,), jnp.int32)] + inputs,
        compiler_params=MEDIUM,
    )(parity, near, far, send_lists, *arrays)

    near = lax.ppermute(near, "tile", near_pairs)
    far = lax.ppermute(far, "tile", far_pairs)
    second_phase = pl.pallas_call(
        second_kernel,
        out_shape=(shape((width, rows), BF16), shape((width, rows), BF16)),
        in_specs=[SMEM] + [VMEM] * 3 + [HBM] * 5,
        out_specs=(VMEM, VMEM),
        scratch_shapes=scratch + inputs,
        compiler_params=MEDIUM,
        cost_estimate=pl.CostEstimate(
            flops=2 * 2 * width * offsets * rows * (width + BLOCK),
            bytes_accessed=4 * offsets * width * rows,
            transcendentals=0,
        ),
    )
    out_features, d_features = second_phase(
        parity, near, far, state, *arrays
    )

    scale = 1.0 / math.sqrt(rows * count)
    grad_first, grad_second = total_over_tiles(keep, send, odd, scale)
    return out_features, d_features, grad_first, grad_second


def solution(mesh):
    tiles = P(None, ("groups", "tile"))
    return jax.shard_map(
        body,
        mesh=mesh,
        in_specs=(tiles, tiles, tiles, P(), P(), tiles),
        out_specs=(tiles, tiles, P("groups", None), P("groups", None)),
        check_vma=False,
    )
```

```python
import math

import jax
import jax.numpy as jnp
from jax import lax
from jax.experimental import pallas as pl
from jax.experimental.pallas import tpu as pltpu
from jax.sharding import PartitionSpec as P


BLOCK = 128
F32, BF16 = jnp.float32, jnp.bfloat16
HBM = pl.BlockSpec(memory_space=pltpu.HBM)
SMALL = pltpu.CompilerParams(vmem_limit_bytes=1 << 20)
MEDIUM = pltpu.CompilerParams(vmem_limit_bytes=20 << 20)
VMEM = pl.BlockSpec(memory_space=pltpu.VMEM)
NT = (((1,), (1,)), ((), ()))


def is_odd():
    return lax.axis_index("tile") % 2 == 1


def pair_blocks(lists_ref, odd):
    lower, upper = lists_ref[0], lists_ref[1]
    return jnp.where(odd, lower, upper), jnp.where(odd, upper, lower)


def fetch(sources, targets, sems):
    copies = [
        pltpu.make_async_copy(source, target, sems.at[i])
        for i, (source, target) in enumerate(zip(sources, targets))
    ]
    for copy in copies:
        copy.start()
    return copies


def payload_kernel(
    lists_hbm, x_hbm, g_hbm, near_ref, far_ref, lists_ref, x_ref, g_ref, sems
):
    width, rows = x_ref.shape
    copies = fetch((lists_hbm, x_hbm, g_hbm), (lists_ref, x_ref, g_ref), sems)
    for copy in copies:
        copy.wait()
    picks = pair_blocks(lists_ref, is_odd())
    for pick, out_ref in zip(picks, (near_ref, far_ref)):
        start = pl.multiple_of(jnp.minimum(pick, rows // BLOCK - 1) * BLOCK, BLOCK)
        out_ref[:width, :] = x_ref[:, pl.ds(start, BLOCK)]
        out_ref[width:, :] = g_ref[:, pl.ds(start, BLOCK)]


def fill_halo(table_ref, near_ref, far_ref, odd, blocks):
    near, far = near_ref[...], far_ref[...]
    table_ref[blocks] = jnp.where(odd, near, far)
    table_ref[blocks + 1] = jnp.where(odd, far, near)


def one_hot(rows, line):
    return (rows == line).astype(F32).astype(BF16)


def gather(table_ref, rule_ref, first_ref, second_ref, blocks):
    offsets = rule_ref.shape[0]
    group = offsets // 3
    sources, channels, _ = table_ref.shape
    width = channels // 2
    source_rows = lax.broadcasted_iota(jnp.int32, (BLOCK, BLOCK), 0)

    def store(k, low, high, found, mirrored):
        first_ref[k * width : (k + 1) * width, low:high] = found[:width].astype(BF16)
        second_ref[mirrored * width : (mirrored + 1) * width, low:high] = found[
            width:
        ].astype(BF16)

    strays = jnp.zeros((group, BLOCK), jnp.int32)
    for block in range(blocks):
        low, high = block * BLOCK, (block + 1) * BLOCK
        for side in range(3):
            entries = rule_ref[side * group : (side + 1) * group, low:high]
            if side == 1:
                source = block
            else:
                least = jnp.min(entries.astype(F32)).astype(jnp.int32)
                source = jnp.minimum(least // BLOCK, sources - 1)
            local = entries - source * BLOCK
            named = entries < sources * BLOCK
            strays = strays | (
                named & ((local < 0) | (local >= BLOCK))
            ).astype(jnp.int32)
            table = table_ref[source]
            for j in range(group):
                k = side * group + j
                choice = one_hot(source_rows, local[j : j + 1])
                found = jnp.dot(table, choice, preferred_element_type=F32)
                store(k, low, high, found, offsets - 1 - k)

    @pl.when(jnp.max(strays.astype(F32)) > 0)
    def _():
        rows = rule_ref.shape[1]
        every_row = lax.broadcasted_iota(jnp.int32, (BLOCK, rows), 0)

        def one(k, carry):
            line = rule_ref[pl.ds(k, 1), :]
            found = jnp.zeros((channels, rows), F32)
            for source in range(sources):
                choice = one_hot(every_row, line - source * BLOCK)
                found += jnp.dot(table_ref[source], choice, preferred_element_type=F32)
            here = pl.multiple_of(k * width, width)
            there = pl.multiple_of((offsets - 1 - k) * width, width)
            first_ref[pl.ds(here, width), :] = found[:width].astype(BF16)
            second_ref[pl.ds(there, width), :] = found[width:].astype(BF16)
            return carry

        lax.fori_loop(0, offsets, one, 0)


def turn(weight_ref, turned_ref):
    width, depth = weight_ref.shape
    offsets = depth // width
    for k in range(0, offsets, 2):
        count = min(2, offsets - k)
        block = weight_ref[:, k * width : (k + count) * width].astype(F32).T
        pieces = [block[i * width : (i + 1) * width] for i in range(count)]
        joined = pieces[0] if count == 1 else jnp.concatenate(pieces, axis=1)
        turned_ref[:, k * width : (k + count) * width] = joined.astype(BF16)


def own_kernel(
    rule_hbm, x_hbm, g_hbm, w1_hbm, w2_hbm,
    xs_ref, gs_ref, pre_ref, d_hidden_ref, rule_ref, w1_ref, turned_ref,
    table_ref, x_ref, g_ref, w2_ref, sems,
):
    copies = fetch(
        (rule_hbm, x_hbm, g_hbm, w2_hbm, w1_hbm), (rule_ref, x_ref, g_ref, w2_ref, w1_ref), sems
    )
    width, rows = x_ref.shape
    blocks = rows // BLOCK
    for copy in copies[:3]:
        copy.wait()
    for block in range(blocks):
        low, high = block * BLOCK, (block + 1) * BLOCK
        table_ref[block, :width] = x_ref[:, low:high]
        table_ref[block, width:] = g_ref[:, low:high]
    table_ref[blocks:] = jnp.zeros_like(table_ref[blocks:])
    gather(table_ref, rule_ref, xs_ref, gs_ref, blocks)
    for copy in copies[3:]:
        copy.wait()
    turn(w2_ref, turned_ref)
    pre_ref[...] = jnp.dot(w1_ref[...], xs_ref[...], preferred_element_type=F32)
    d_hidden_ref[...] = jnp.dot(turned_ref[...], gs_ref[...], preferred_element_type=F32)


def rim_kernel(
    lists_hbm, near_ref, far_ref, xs_ref, gs_ref, pre_in, d_hidden_in, rule_ref, w1_ref, turned_ref,
    state_ref, near_out, far_out, keep_ref, send_ref,
    pre_ref, d_hidden_ref, rim_x_ref, rim_g_ref, lists_ref, sems,
):
    copies = fetch((lists_hbm,), (lists_ref,), sems)
    width, rows = pre_in.shape
    blocks = rows // BLOCK
    offsets = rule_ref.shape[0]
    group = offsets // 3
    odd = is_odd()
    near, far = near_ref[...], far_ref[...]
    tables = (jnp.where(odd, near, far), jnp.where(odd, far, near))
    pre_ref[...] = pre_in[...]
    d_hidden_ref[...] = d_hidden_in[...]
    source_rows = lax.broadcasted_iota(jnp.int32, (BLOCK, BLOCK), 0)
    copies[0].wait()
    sides = []
    for side in range(2):
        block = jnp.minimum(lists_ref[side], blocks - 1)
        columns = pl.ds(pl.multiple_of(block * BLOCK, BLOCK), BLOCK)
        start = 2 * side * group
        mirrored = offsets - group - start
        local = rule_ref[start : start + group, columns] - (blocks + side) * BLOCK
        for j in range(group):
            found = jnp.dot(
                tables[side], one_hot(source_rows, local[j : j + 1]), preferred_element_type=F32
            )
            rim_x_ref[side, j * width : (j + 1) * width] = found[:width].astype(BF16)
            place = (group - 1 - j) * width
            rim_g_ref[side, place : place + width] = found[width:].astype(BF16)
        span = slice(start * width, (start + group) * width)
        mirror_span = slice(mirrored * width, (mirrored + group) * width)
        pre_ref[:, columns] += jnp.dot(
            w1_ref[:, span], rim_x_ref[side], preferred_element_type=F32
        )
        d_hidden_ref[:, columns] += jnp.dot(
            turned_ref[:, mirror_span], rim_g_ref[side], preferred_element_type=F32
        )
        sides.append((block, start, mirrored))
    pre = pre_ref[...]
    sigma = jax.nn.sigmoid(pre)
    hidden = (pre * sigma).astype(BF16)
    d_pre = (d_hidden_ref[...] * sigma * (1.0 + pre * (1.0 - sigma))).astype(BF16)
    for block in range(blocks):
        low, high = block * BLOCK, (block + 1) * BLOCK
        state_ref[block, :width] = hidden[:, low:high]
        state_ref[block, width:] = d_pre[:, low:high]
    for pick, out_ref in zip(pair_blocks(lists_ref, odd), (near_out, far_out)):
        out_ref[...] = state_ref[jnp.minimum(pick, blocks - 1)]
    grad_first = lax.dot_general(d_pre, xs_ref[...], NT, preferred_element_type=F32)
    stacked = lax.dot_general(gs_ref[...], hidden, NT, preferred_element_type=F32)
    rims = [
        (
            lax.dot_general(
                state_ref[block, width:], rim_x_ref[side], NT, preferred_element_type=F32
            ),
            lax.dot_general(
                rim_g_ref[side], state_ref[block, :width], NT, preferred_element_type=F32
            ),
        )
        for side, (block, _, _) in enumerate(sides)
    ]

    def first_of(k):
        term = grad_first[:, k * width : (k + 1) * width]
        for (rim, _), (_, start, _) in zip(rims, sides):
            if start <= k < start + group:
                term = term + rim[:, (k - start) * width : (k - start + 1) * width]
        return term

    def second_of(k):
        term = stacked[k * width : (k + 1) * width]
        for (_, rim), (_, _, mirrored) in zip(rims, sides):
            if mirrored <= k < mirrored + group:
                term = term + rim[(k - mirrored) * width : (k - mirrored + 1) * width]
        return term

    for k in range(0, offsets, 2):
        count = min(2, offsets - k)
        low, high = k * width, (k + count) * width
        first = [first_of(k + i) for i in range(count)]
        second = [second_of(k + i) for i in range(count)]
        first = first[0] if count == 1 else jnp.concatenate(first, axis=1)
        second = second[0] if count == 1 else jnp.concatenate(second, axis=1)
        keep_ref[:, low:high] = jnp.where(odd, second, first)
        send_ref[:, low:high] = jnp.where(odd, first, second).astype(BF16)


def second_kernel(
    near_ref, far_ref, state_ref, rule_hbm, x_hbm, g_hbm, w1_hbm, w2_hbm,
    out_ref, dx_ref,
    table_ref, hs_ref, ds_ref, turned_ref,
    rule_ref, x_ref, g_ref, w1_ref, w2_ref, sems,
):
    copies = fetch(
        (rule_hbm, w1_hbm, w2_hbm, x_hbm, g_hbm),
        (rule_ref, w1_ref, w2_ref, x_ref, g_ref),
        sems,
    )
    _, rows = x_ref.shape
    blocks = rows // BLOCK
    odd = is_odd()
    for block in range(blocks):
        table_ref[block] = state_ref[block]
    fill_halo(table_ref, near_ref, far_ref, odd, blocks)
    copies[0].wait()
    gather(table_ref, rule_ref, hs_ref, ds_ref, blocks)
    for copy in copies[1:]:
        copy.wait()
    turn(w1_ref, turned_ref)
    second = jnp.dot(w2_ref[...], hs_ref[...], preferred_element_type=F32)
    out_ref[...] = (second + x_ref[...].astype(F32)).astype(BF16)
    d_input = jnp.dot(turned_ref[...], ds_ref[...], preferred_element_type=F32)
    dx_ref[...] = (d_input + g_ref[...].astype(F32)).astype(BF16)


def neighbour_pairs(count):
    near = [(i, i ^ 1) for i in range(count) if i ^ 1 < count]
    far = [(i, i + 1 if i % 2 else i - 1) for i in range(count)]
    return near, [(i, j) for i, j in far if 0 <= j < count]


def total_over_tiles(keep, send, odd, first_scale):
    count = lax.axis_size("tile")
    received = lax.ppermute(send, "tile", [(i, i ^ 1) for i in range(count)])
    total = keep + received.astype(F32)
    bits = [1 << b for b in range(1, count.bit_length() - 1)]
    for step, (even_bit, odd_bit) in enumerate(zip(bits, bits[-1:] + bits[:-1])):
        wire = BF16 if step >= len(bits) - 3 else F32
        pairs = [(i, i ^ (odd_bit if i % 2 else even_bit)) for i in range(count)]
        sent = total.astype(wire)
        received = lax.ppermute(sent, "tile", pairs)
        total = sent.astype(F32) + received.astype(F32)
    total = total * first_scale
    other = lax.ppermute(total, "tile", [(i, i ^ 1) for i in range(count)])
    return jnp.where(odd, other, total), jnp.where(odd, total, other)


def body(features, rulebook, send_lists, weight_first, weight_second, cotangent):
    width, rows = features.shape
    offsets = rulebook.shape[0]
    blocks = rows // BLOCK
    count = lax.axis_size("tile")
    odd = is_odd()
    send_lists = send_lists.reshape(2)
    features, cotangent, rulebook, weight_first, weight_second, send_lists = (
        pltpu.with_memory_space_constraint(array, pltpu.HBM)
        for array in (features, cotangent, rulebook, weight_first, weight_second, send_lists)
    )
    near_pairs, far_pairs = neighbour_pairs(count)
    shape = jax.ShapeDtypeStruct
    rim = shape((2 * width, BLOCK), BF16)

    near, far = pl.pallas_call(
        payload_kernel,
        out_shape=(rim, rim),
        in_specs=[HBM, HBM, HBM],
        out_specs=(VMEM, VMEM),
        scratch_shapes=[
            pltpu.SMEM((2,), jnp.int32),
            pltpu.VMEM((width, rows), BF16),
            pltpu.VMEM((width, rows), BF16),
            pltpu.SemaphoreType.DMA((3,)),
        ],
        compiler_params=SMALL,
    )(send_lists, features, cotangent)
    far = lax.ppermute(far, "tile", far_pairs)
    near = lax.ppermute(near, "tile", near_pairs)

    table = pltpu.VMEM((blocks + 2, 2 * width, BLOCK), BF16)
    rows_of_tile = pltpu.VMEM((width, rows), BF16)
    weight = pltpu.VMEM((width, offsets * width), BF16)
    arrays = (rulebook, features, cotangent, weight_first, weight_second)
    own_phase = pl.pallas_call(
        own_kernel,
        out_shape=(
            shape((offsets * width, rows), BF16), shape((offsets * width, rows), BF16),
            shape((width, rows), F32), shape((width, rows), F32),
            shape(rulebook.shape, jnp.int32), shape(weight_first.shape, BF16),
            shape(weight_first.shape, BF16),
        ),
        in_specs=[HBM] * 5,
        out_specs=(VMEM,) * 7,
        scratch_shapes=[table, rows_of_tile, rows_of_tile, weight, pltpu.SemaphoreType.DMA((5,))],
        compiler_params=MEDIUM,
        cost_estimate=pl.CostEstimate(
            flops=2 * 2 * width * offsets * rows * (width + BLOCK),
            bytes_accessed=4 * offsets * width * rows,
            transcendentals=0,
        ),
    )
    own = own_phase(*arrays)
    state, near, far, keep, send = pl.pallas_call(
        rim_kernel,
        out_shape=(
            shape((blocks, 2 * width, BLOCK), BF16), rim, rim,
            shape((width, offsets * width), F32), shape((width, offsets * width), BF16),
        ),
        in_specs=[HBM] + [VMEM] * 9,
        out_specs=(VMEM,) * 5,
        scratch_shapes=[
            pltpu.VMEM((width, rows), F32),
            pltpu.VMEM((width, rows), F32),
            pltpu.VMEM((2, offsets // 3 * width, BLOCK), BF16),
            pltpu.VMEM((2, offsets // 3 * width, BLOCK), BF16),
            pltpu.SMEM((2,), jnp.int32),
            pltpu.SemaphoreType.DMA((1,)),
        ],
        compiler_params=MEDIUM,
    )(send_lists, near, far, *own)

    near = lax.ppermute(near, "tile", near_pairs)
    far = lax.ppermute(far, "tile", far_pairs)
    second_phase = pl.pallas_call(
        second_kernel,
        out_shape=(shape((width, rows), BF16), shape((width, rows), BF16)),
        in_specs=[VMEM] * 3 + [HBM] * 5,
        out_specs=(VMEM, VMEM),
        scratch_shapes=[
            table,
            pltpu.VMEM((offsets * width, rows), BF16),
            pltpu.VMEM((offsets * width, rows), BF16),
            weight,
            pltpu.VMEM(rulebook.shape, jnp.int32),
            rows_of_tile, rows_of_tile, weight, weight,
            pltpu.SemaphoreType.DMA((5,)),
        ],
        compiler_params=MEDIUM,
        cost_estimate=pl.CostEstimate(
            flops=2 * 2 * width * offsets * rows * (width + BLOCK),
            bytes_accessed=4 * offsets * width * rows,
            transcendentals=0,
        ),
    )
    out_features, d_features = second_phase(
        near, far, state, *arrays
    )

    scale = 1.0 / math.sqrt(rows * count)
    grad_first, grad_second = total_over_tiles(keep, send, odd, scale)
    return out_features, d_features, grad_first, grad_second


def solution(mesh):
    tiles = P(None, ("groups", "tile"))
    return jax.shard_map(
        body,
        mesh=mesh,
        in_specs=(tiles, tiles, tiles, P(), P(), tiles),
        out_specs=(tiles, tiles, P("groups", None), P("groups", None)),
        check_vma=False,
    )
```

```python
import math

import jax
import jax.numpy as jnp
from jax import lax
from jax.experimental import pallas as pl
from jax.experimental.pallas import tpu as pltpu
from jax.sharding import PartitionSpec as P


BLOCK = 128
F32, BF16 = jnp.float32, jnp.bfloat16
HBM = pl.BlockSpec(memory_space=pltpu.HBM)
SMALL = pltpu.CompilerParams(vmem_limit_bytes=1 << 20)
MEDIUM = pltpu.CompilerParams(vmem_limit_bytes=20 << 20)
VMEM = pl.BlockSpec(memory_space=pltpu.VMEM)
NT = (((1,), (1,)), ((), ()))


def is_odd():
    return lax.axis_index("tile") % 2 == 1


def pair_blocks(listed, odd):
    lower, upper = listed
    return jnp.where(odd, lower, upper), jnp.where(odd, upper, lower)


def fetch(sources, targets, sems):
    copies = [
        pltpu.make_async_copy(source, target, sems.at[i])
        for i, (source, target) in enumerate(zip(sources, targets))
    ]
    for copy in copies:
        copy.start()
    return copies


def load_kernel(
    lists_hbm, x_hbm, g_hbm, rule_hbm, w2_hbm, w1_hbm,
    near_ref, far_ref, lists_out, x_ref, g_ref, rule_ref, w2_ref, w1_ref,
    lists_ref, sems,
):
    width, rows = x_ref.shape
    copies = fetch(
        (lists_hbm, x_hbm, g_hbm, rule_hbm, w2_hbm, w1_hbm),
        (lists_ref, x_ref, g_ref, rule_ref, w2_ref, w1_ref),
        sems,
    )
    for copy in copies[:3]:
        copy.wait()
    picks = pair_blocks((lists_ref[0], lists_ref[1]), is_odd())
    for pick, out_ref in zip(picks, (near_ref, far_ref)):
        start = pl.multiple_of(jnp.minimum(pick, rows // BLOCK - 1) * BLOCK, BLOCK)
        out_ref[:width, :] = x_ref[:, pl.ds(start, BLOCK)]
        out_ref[width:, :] = g_ref[:, pl.ds(start, BLOCK)]
    for side in range(2):
        lists_out[side] = jnp.full(lists_out.shape[1:], lists_ref[side], jnp.int32)
    for copy in copies[3:]:
        copy.wait()


def fill_halo(table_ref, near_ref, far_ref, odd, blocks):
    near, far = near_ref[...], far_ref[...]
    table_ref[blocks] = jnp.where(odd, near, far)
    table_ref[blocks + 1] = jnp.where(odd, far, near)


def one_hot(rows, line):
    return (rows == line).astype(F32).astype(BF16)


def gather(table_ref, rule_ref, first_ref, second_ref, blocks):
    offsets = rule_ref.shape[0]
    group = offsets // 3
    sources, channels, _ = table_ref.shape
    width = channels // 2
    source_rows = lax.broadcasted_iota(jnp.int32, (BLOCK, BLOCK), 0)

    def store(k, low, high, found, mirrored):
        first_ref[k * width : (k + 1) * width, low:high] = found[:width].astype(BF16)
        second_ref[mirrored * width : (mirrored + 1) * width, low:high] = found[
            width:
        ].astype(BF16)

    strays = jnp.zeros((group, BLOCK), jnp.int32)
    for block in range(blocks):
        low, high = block * BLOCK, (block + 1) * BLOCK
        for side in range(3):
            entries = rule_ref[side * group : (side + 1) * group, low:high]
            if side == 1:
                source = block
            else:
                least = jnp.min(entries.astype(F32)).astype(jnp.int32)
                source = jnp.minimum(least // BLOCK, sources - 1)
            local = entries - source * BLOCK
            named = entries < sources * BLOCK
            strays = strays | (
                named & ((local < 0) | (local >= BLOCK))
            ).astype(jnp.int32)
            table = table_ref[source]
            for j in range(group):
                k = side * group + j
                choice = one_hot(source_rows, local[j : j + 1])
                found = jnp.dot(table, choice, preferred_element_type=F32)
                store(k, low, high, found, offsets - 1 - k)

    @pl.when(jnp.max(strays.astype(F32)) > 0)
    def _():
        rows = rule_ref.shape[1]
        every_row = lax.broadcasted_iota(jnp.int32, (BLOCK, rows), 0)

        def one(k, carry):
            line = rule_ref[pl.ds(k, 1), :]
            found = jnp.zeros((channels, rows), F32)
            for source in range(sources):
                choice = one_hot(every_row, line - source * BLOCK)
                found += jnp.dot(table_ref[source], choice, preferred_element_type=F32)
            here = pl.multiple_of(k * width, width)
            there = pl.multiple_of((offsets - 1 - k) * width, width)
            first_ref[pl.ds(here, width), :] = found[:width].astype(BF16)
            second_ref[pl.ds(there, width), :] = found[width:].astype(BF16)
            return carry

        lax.fori_loop(0, offsets, one, 0)


def turn(weight_ref, turned_ref):
    width, depth = weight_ref.shape
    offsets = depth // width
    for k in range(0, offsets, 2):
        count = min(2, offsets - k)
        block = weight_ref[:, k * width : (k + count) * width].astype(F32).T
        pieces = [block[i * width : (i + 1) * width] for i in range(count)]
        joined = pieces[0] if count == 1 else jnp.concatenate(pieces, axis=1)
        turned_ref[:, k * width : (k + count) * width] = joined.astype(BF16)


def own_kernel(
    rule_ref, x_ref, g_ref, w1_ref, w2_ref,
    xs_ref, gs_ref, pre_ref, d_hidden_ref, turned_ref,
    table_ref,
):
    width, rows = x_ref.shape
    blocks = rows // BLOCK
    for block in range(blocks):
        low, high = block * BLOCK, (block + 1) * BLOCK
        table_ref[block, :width] = x_ref[:, low:high]
        table_ref[block, width:] = g_ref[:, low:high]
    table_ref[blocks:] = jnp.zeros_like(table_ref[blocks:])
    gather(table_ref, rule_ref, xs_ref, gs_ref, blocks)
    turn(w2_ref, turned_ref)
    pre_ref[...] = jnp.dot(w1_ref[...], xs_ref[...], preferred_element_type=F32)
    d_hidden_ref[...] = jnp.dot(turned_ref[...], gs_ref[...], preferred_element_type=F32)


def first_terms(state_ref, xs_ref, out_ref):
    blocks = state_ref.shape[0]
    width = state_ref.shape[1] // 2
    depth = xs_ref.shape[0]
    d_pre = jnp.concatenate([state_ref[block, width:] for block in range(blocks)], axis=1)
    for low in range(0, depth, 8 * width):
        high = min(depth, low + 8 * width)
        terms = lax.dot_general(d_pre, xs_ref[low:high], NT, preferred_element_type=F32)
        out_ref[:, low:high] = terms.astype(out_ref.dtype)


def second_terms(state_ref, gs_ref, out_ref):
    blocks = state_ref.shape[0]
    width = state_ref.shape[1] // 2
    depth = gs_ref.shape[0]
    hidden = jnp.concatenate([state_ref[block, :width] for block in range(blocks)], axis=1)
    for low in range(0, depth, 4 * width):
        high = min(depth, low + 4 * width)
        terms = lax.dot_general(gs_ref[low:high], hidden, NT, preferred_element_type=F32)
        for at in range(low, high, 2 * width):
            pieces = [
                terms[i - low : i - low + width] for i in range(at, min(high, at + 2 * width), width)
            ]
            joined = pieces[0] if len(pieces) == 1 else jnp.concatenate(pieces, axis=1)
            out_ref[:, at : at + joined.shape[1]] = joined.astype(out_ref.dtype)


def rim_kernel(
    lists_ref, near_ref, far_ref, pre_in, d_hidden_in, rule_ref, w1_ref, turned_ref, xs_in, gs_in,
    state_ref, near_out, far_out, send_ref, xs_ref, gs_ref,
    pre_ref, d_hidden_ref,
):
    width, rows = pre_in.shape
    blocks = rows // BLOCK
    offsets = rule_ref.shape[0]
    group = offsets // 3
    odd = is_odd()
    listed = [jnp.max(lists_ref[side].astype(F32)).astype(jnp.int32) for side in range(2)]
    near, far = near_ref[...], far_ref[...]
    tables = (jnp.where(odd, near, far), jnp.where(odd, far, near))
    pre_ref[...] = pre_in[...]
    d_hidden_ref[...] = d_hidden_in[...]
    source_rows = lax.broadcasted_iota(jnp.int32, (BLOCK, BLOCK), 0)
    for side in range(2):
        columns = pl.ds(pl.multiple_of(jnp.minimum(listed[side], blocks - 1) * BLOCK, BLOCK), BLOCK)
        start = 2 * side * group
        mirrored = offsets - group - start
        local = rule_ref[start : start + group, columns] - (blocks + side) * BLOCK
        rim_x, rim_g = [], []
        for j in range(group):
            found = jnp.dot(
                tables[side], one_hot(source_rows, local[j : j + 1]), preferred_element_type=F32
            )
            rim_x.append(found[:width].astype(BF16))
            rim_g.append(found[width:].astype(BF16))
        rim_x = jnp.concatenate(rim_x, axis=0)
        rim_g = jnp.concatenate(rim_g[::-1], axis=0)
        span = slice(start * width, (start + group) * width)
        mirror_span = slice(mirrored * width, (mirrored + group) * width)
        pre_ref[:, columns] += jnp.dot(w1_ref[:, span], rim_x, preferred_element_type=F32)
        d_hidden_ref[:, columns] += jnp.dot(
            turned_ref[:, mirror_span], rim_g, preferred_element_type=F32
        )

        @pl.when(listed[side] < blocks)
        def _():
            xs_ref[span, columns] = rim_x
            gs_ref[mirror_span, columns] = rim_g

    pre = pre_ref[...]
    sigma = jax.nn.sigmoid(pre)
    hidden = (pre * sigma).astype(BF16)
    d_pre = (d_hidden_ref[...] * sigma * (1.0 + pre * (1.0 - sigma))).astype(BF16)
    for block in range(blocks):
        low, high = block * BLOCK, (block + 1) * BLOCK
        state_ref[block, :width] = hidden[:, low:high]
        state_ref[block, width:] = d_pre[:, low:high]
    for pick, out_ref in zip(pair_blocks(listed, odd), (near_out, far_out)):
        out_ref[...] = state_ref[jnp.minimum(pick, blocks - 1)]

    @pl.when(odd)
    def _():
        first_terms(state_ref, xs_ref, send_ref)

    @pl.when(jnp.logical_not(odd))
    def _():
        second_terms(state_ref, gs_ref, send_ref)


def keep_kernel(state_ref, xs_ref, gs_ref, keep_ref):
    odd = is_odd()

    @pl.when(odd)
    def _():
        second_terms(state_ref, gs_ref, keep_ref)

    @pl.when(jnp.logical_not(odd))
    def _():
        first_terms(state_ref, xs_ref, keep_ref)


def put(source, for_odd, for_even, sem):
    odd = is_odd()
    for chosen, target in ((odd, for_odd), (jnp.logical_not(odd), for_even)):

        @pl.when(chosen)
        def _():
            copy = pltpu.make_async_copy(source, target, sem)
            copy.start()
            copy.wait()


def put_own_kernel(total_ref, first_hbm, second_hbm, sem):
    put(total_ref, second_hbm, first_hbm, sem)


def put_other_kernel(other_ref, first_in, second_in, first_hbm, second_hbm, sem):
    put(other_ref, first_hbm, second_hbm, sem)


def second_kernel(
    near_ref, far_ref, state_ref, rule_ref, x_ref, g_ref, w1_ref, w2_ref,
    out_ref, dx_ref,
    table_ref, hs_ref, ds_ref, turned_ref,
):
    _, rows = x_ref.shape
    blocks = rows // BLOCK
    odd = is_odd()
    for block in range(blocks):
        table_ref[block] = state_ref[block]
    fill_halo(table_ref, near_ref, far_ref, odd, blocks)
    gather(table_ref, rule_ref, hs_ref, ds_ref, blocks)
    turn(w1_ref, turned_ref)
    second = jnp.dot(w2_ref[...], hs_ref[...], preferred_element_type=F32)
    out_ref[...] = (second + x_ref[...].astype(F32)).astype(BF16)
    d_input = jnp.dot(turned_ref[...], ds_ref[...], preferred_element_type=F32)
    dx_ref[...] = (d_input + g_ref[...].astype(F32)).astype(BF16)


def neighbour_pairs(count):
    near = [(i, i ^ 1) for i in range(count) if i ^ 1 < count]
    far = [(i, i + 1 if i % 2 else i - 1) for i in range(count)]
    return near, [(i, j) for i, j in far if 0 <= j < count]


def total_over_tiles(keep, send, scale):
    count = lax.axis_size("tile")
    cores = [(i, i ^ 1) for i in range(count)]
    received = lax.ppermute(send, "tile", cores)
    total = keep + received.astype(F32)
    bits = [1 << b for b in range(1, count.bit_length() - 1)]
    for step, (even_bit, odd_bit) in enumerate(zip(bits, bits[-1:] + bits[:-1])):
        wire = BF16 if step >= len(bits) - 3 else F32
        pairs = [(i, i ^ (odd_bit if i % 2 else even_bit)) for i in range(count)]
        sent = total.astype(wire)
        received = lax.ppermute(sent, "tile", pairs)
        total = sent.astype(F32) + received.astype(F32)
    total = total * scale
    other = lax.ppermute(total, "tile", cores)
    result = jax.ShapeDtypeStruct(total.shape, F32)
    put_own = pl.pallas_call(
        put_own_kernel,
        out_shape=(result, result),
        in_specs=[VMEM],
        out_specs=(HBM, HBM),
        scratch_shapes=[pltpu.SemaphoreType.DMA],
        compiler_params=SMALL,
    )
    half = put_own(total)
    return pl.pallas_call(
        put_other_kernel,
        out_shape=(result, result),
        in_specs=[VMEM, HBM, HBM],
        out_specs=(HBM, HBM),
        scratch_shapes=[pltpu.SemaphoreType.DMA],
        input_output_aliases={1: 0, 2: 1},
        compiler_params=SMALL,
    )(other, *half)


def body(features, rulebook, send_lists, weight_first, weight_second, cotangent):
    width, rows = features.shape
    offsets = rulebook.shape[0]
    blocks = rows // BLOCK
    count = lax.axis_size("tile")
    near_pairs, far_pairs = neighbour_pairs(count)
    send_lists = send_lists.reshape(2)
    features, cotangent, rulebook, weight_first, weight_second, send_lists = (
        pltpu.with_memory_space_constraint(array, pltpu.HBM)
        for array in (features, cotangent, rulebook, weight_first, weight_second, send_lists)
    )
    shape = jax.ShapeDtypeStruct
    rim = shape((2 * width, BLOCK), BF16)
    values = shape((width, rows), BF16)
    sums = shape((width, rows), F32)
    gathered = shape((offsets * width, rows), BF16)
    weight = shape((width, offsets * width), BF16)
    terms = shape((width, offsets * width), F32)
    state_shape = shape((blocks, 2 * width, BLOCK), BF16)
    table = pltpu.VMEM((blocks + 2, 2 * width, BLOCK), BF16)

    near, far, lists, x, g, rule, w2, w1 = pl.pallas_call(
        load_kernel,
        out_shape=(
            rim, rim, shape((2, 8, BLOCK), jnp.int32), values, values,
            shape(rulebook.shape, jnp.int32), weight, weight,
        ),
        in_specs=[HBM] * 6,
        out_specs=(VMEM,) * 8,
        scratch_shapes=[pltpu.SMEM((2,), jnp.int32), pltpu.SemaphoreType.DMA((6,))],
        compiler_params=MEDIUM,
    )(send_lists, features, cotangent, rulebook, weight_second, weight_first)
    far = lax.ppermute(far, "tile", far_pairs)
    near = lax.ppermute(near, "tile", near_pairs)

    work = pl.CostEstimate(
        flops=2 * 2 * width * offsets * rows * (width + BLOCK),
        bytes_accessed=4 * offsets * width * rows,
        transcendentals=0,
    )
    own_phase = pl.pallas_call(
        own_kernel,
        out_shape=(gathered, gathered, sums, sums, weight),
        in_specs=[VMEM] * 5,
        out_specs=(VMEM,) * 5,
        scratch_shapes=[table],
        compiler_params=MEDIUM,
        cost_estimate=work,
    )
    xs, gs, pre, d_hidden, turned = own_phase(rule, x, g, w1, w2)
    state, near, far, send, xs, gs = pl.pallas_call(
        rim_kernel,
        out_shape=(state_shape, rim, rim, weight, gathered, gathered),
        in_specs=[VMEM] * 10,
        out_specs=(VMEM,) * 6,
        scratch_shapes=[pltpu.VMEM((width, rows), F32), pltpu.VMEM((width, rows), F32)],
        input_output_aliases={8: 4, 9: 5},
        compiler_params=MEDIUM,
    )(lists, near, far, pre, d_hidden, rule, w1, turned, xs, gs)
    keep_terms = pl.pallas_call(
        keep_kernel,
        out_shape=terms,
        in_specs=[VMEM] * 3,
        out_specs=VMEM,
        compiler_params=MEDIUM,
    )
    keep = keep_terms(state, xs, gs)

    near = lax.ppermute(near, "tile", near_pairs)
    far = lax.ppermute(far, "tile", far_pairs)
    second_phase = pl.pallas_call(
        second_kernel,
        out_shape=(values, values),
        in_specs=[VMEM] * 8,
        out_specs=(VMEM, VMEM),
        scratch_shapes=[
            table,
            pltpu.VMEM((offsets * width, rows), BF16),
            pltpu.VMEM((offsets * width, rows), BF16),
            pltpu.VMEM((width, offsets * width), BF16),
        ],
        compiler_params=MEDIUM,
        cost_estimate=work,
    )
    out_features, d_features = second_phase(near, far, state, rule, x, g, w1, w2)

    scale = 1.0 / math.sqrt(rows * count)
    grad_first, grad_second = total_over_tiles(keep, send, scale)
    return out_features, d_features, grad_first, grad_second


def solution(mesh):
    tiles = P(None, ("groups", "tile"))
    return jax.shard_map(
        body,
        mesh=mesh,
        in_specs=(tiles, tiles, tiles, P(), P(), tiles),
        out_specs=(tiles, tiles, P("groups", None), P("groups", None)),
        check_vma=False,
    )
```

```python
import math

import jax
import jax.numpy as jnp
from jax import lax
from jax.experimental import pallas as pl
from jax.experimental.pallas import tpu as pltpu
from jax.sharding import PartitionSpec as P


BLOCK = 128
F32, BF16 = jnp.float32, jnp.bfloat16
HBM = pl.BlockSpec(memory_space=pltpu.HBM)
SMALL = pltpu.CompilerParams(vmem_limit_bytes=1 << 20)
MEDIUM = pltpu.CompilerParams(vmem_limit_bytes=20 << 20)
VMEM = pl.BlockSpec(memory_space=pltpu.VMEM)
NT = (((1,), (1,)), ((), ()))


def is_odd():
    return lax.axis_index("tile") % 2 == 1


def pair_blocks(listed, odd):
    lower, upper = listed
    return jnp.where(odd, lower, upper), jnp.where(odd, upper, lower)


def fetch(sources, targets, sems):
    copies = [
        pltpu.make_async_copy(source, target, sems.at[i])
        for i, (source, target) in enumerate(zip(sources, targets))
    ]
    for copy in copies:
        copy.start()
    return copies


def load_kernel(
    lists_hbm, x_hbm, g_hbm, rule_hbm, w2_hbm, w1_hbm,
    near_ref, far_ref, lists_out, x_ref, g_ref, rule_ref, w2_ref, w1_ref,
    lists_ref, sems,
):
    width, rows = x_ref.shape
    copies = fetch(
        (lists_hbm, x_hbm, g_hbm, rule_hbm, w2_hbm, w1_hbm),
        (lists_ref, x_ref, g_ref, rule_ref, w2_ref, w1_ref),
        sems,
    )
    for copy in copies[:3]:
        copy.wait()
    picks = pair_blocks((lists_ref[0], lists_ref[1]), is_odd())
    for pick, out_ref in zip(picks, (near_ref, far_ref)):
        start = pl.multiple_of(jnp.minimum(pick, rows // BLOCK - 1) * BLOCK, BLOCK)
        out_ref[:width, :] = x_ref[:, pl.ds(start, BLOCK)]
        out_ref[width:, :] = g_ref[:, pl.ds(start, BLOCK)]
    for side in range(2):
        lists_out[side] = jnp.full(lists_out.shape[1:], lists_ref[side], jnp.int32)
    for copy in copies[3:]:
        copy.wait()


def fill_halo(table_ref, near_ref, far_ref, odd, blocks):
    near, far = near_ref[...], far_ref[...]
    table_ref[blocks] = jnp.where(odd, near, far)
    table_ref[blocks + 1] = jnp.where(odd, far, near)


def one_hot(rows, line):
    return (rows == line).astype(F32).astype(BF16)


def gather(table_ref, rule_ref, first_ref, second_ref, blocks):
    offsets = rule_ref.shape[0]
    group = offsets // 3
    sources, channels, _ = table_ref.shape
    width = channels // 2
    source_rows = lax.broadcasted_iota(jnp.int32, (BLOCK, BLOCK), 0)

    def store(k, low, high, found, mirrored):
        first_ref[k * width : (k + 1) * width, low:high] = found[:width].astype(BF16)
        second_ref[mirrored * width : (mirrored + 1) * width, low:high] = found[
            width:
        ].astype(BF16)

    strays = jnp.zeros((group, BLOCK), jnp.int32)
    for block in range(blocks):
        low, high = block * BLOCK, (block + 1) * BLOCK
        for side in range(3):
            entries = rule_ref[side * group : (side + 1) * group, low:high]
            if side == 1:
                source = block
            else:
                least = jnp.min(entries.astype(F32)).astype(jnp.int32)
                source = jnp.minimum(least // BLOCK, sources - 1)
            local = entries - source * BLOCK
            named = entries < sources * BLOCK
            strays = strays | (
                named & ((local < 0) | (local >= BLOCK))
            ).astype(jnp.int32)
            table = table_ref[source]
            for j in range(group):
                k = side * group + j
                choice = one_hot(source_rows, local[j : j + 1])
                found = jnp.dot(table, choice, preferred_element_type=F32)
                store(k, low, high, found, offsets - 1 - k)

    @pl.when(jnp.max(strays.astype(F32)) > 0)
    def _():
        rows = rule_ref.shape[1]
        every_row = lax.broadcasted_iota(jnp.int32, (BLOCK, rows), 0)

        def one(k, carry):
            line = rule_ref[pl.ds(k, 1), :]
            found = jnp.zeros((channels, rows), F32)
            for source in range(sources):
                choice = one_hot(every_row, line - source * BLOCK)
                found += jnp.dot(table_ref[source], choice, preferred_element_type=F32)
            here = pl.multiple_of(k * width, width)
            there = pl.multiple_of((offsets - 1 - k) * width, width)
            first_ref[pl.ds(here, width), :] = found[:width].astype(BF16)
            second_ref[pl.ds(there, width), :] = found[width:].astype(BF16)
            return carry

        lax.fori_loop(0, offsets, one, 0)


def turn(weight_ref, turned_ref):
    width, depth = weight_ref.shape
    offsets = depth // width
    for k in range(0, offsets, 2):
        count = min(2, offsets - k)
        block = weight_ref[:, k * width : (k + count) * width].astype(F32).T
        pieces = [block[i * width : (i + 1) * width] for i in range(count)]
        joined = pieces[0] if count == 1 else jnp.concatenate(pieces, axis=1)
        turned_ref[:, k * width : (k + count) * width] = joined.astype(BF16)


def own_kernel(
    rule_ref, x_ref, g_ref, w1_ref, w2_ref,
    xs_ref, gs_ref, pre_ref, d_hidden_ref, turned_ref,
    table_ref,
):
    width, rows = x_ref.shape
    blocks = rows // BLOCK
    for block in range(blocks):
        low, high = block * BLOCK, (block + 1) * BLOCK
        table_ref[block, :width] = x_ref[:, low:high]
        table_ref[block, width:] = g_ref[:, low:high]
    table_ref[blocks:] = jnp.zeros_like(table_ref[blocks:])
    gather(table_ref, rule_ref, xs_ref, gs_ref, blocks)
    turn(w2_ref, turned_ref)
    pre_ref[...] = jnp.dot(w1_ref[...], xs_ref[...], preferred_element_type=F32)
    d_hidden_ref[...] = jnp.dot(turned_ref[...], gs_ref[...], preferred_element_type=F32)


def first_terms(state_ref, xs_ref, out_ref):
    blocks = state_ref.shape[0]
    width = state_ref.shape[1] // 2
    depth = xs_ref.shape[0]
    d_pre = jnp.concatenate([state_ref[block, width:] for block in range(blocks)], axis=1)
    for low in range(0, depth, 8 * width):
        high = min(depth, low + 8 * width)
        terms = lax.dot_general(d_pre, xs_ref[low:high], NT, preferred_element_type=F32)
        out_ref[:, low:high] = terms.astype(out_ref.dtype)


def second_terms(state_ref, gs_ref, out_ref):
    blocks = state_ref.shape[0]
    width = state_ref.shape[1] // 2
    depth = gs_ref.shape[0]
    hidden = jnp.concatenate([state_ref[block, :width] for block in range(blocks)], axis=1)
    for low in range(0, depth, 4 * width):
        high = min(depth, low + 4 * width)
        terms = lax.dot_general(gs_ref[low:high], hidden, NT, preferred_element_type=F32)
        for at in range(low, high, 2 * width):
            pieces = [
                terms[i - low : i - low + width] for i in range(at, min(high, at + 2 * width), width)
            ]
            joined = pieces[0] if len(pieces) == 1 else jnp.concatenate(pieces, axis=1)
            out_ref[:, at : at + joined.shape[1]] = joined.astype(out_ref.dtype)


def rim_kernel(
    lists_ref, near_ref, far_ref, pre_in, d_hidden_in, rule_ref, w1_ref, turned_ref, xs_in, gs_in,
    state_ref, near_out, far_out, send_ref, xs_ref, gs_ref,
    pre_ref, d_hidden_ref,
):
    width, rows = pre_in.shape
    blocks = rows // BLOCK
    offsets = rule_ref.shape[0]
    group = offsets // 3
    odd = is_odd()
    listed = [jnp.max(lists_ref[side].astype(F32)).astype(jnp.int32) for side in range(2)]
    near, far = near_ref[...], far_ref[...]
    tables = (jnp.where(odd, near, far), jnp.where(odd, far, near))
    pre_ref[...] = pre_in[...]
    d_hidden_ref[...] = d_hidden_in[...]
    source_rows = lax.broadcasted_iota(jnp.int32, (BLOCK, BLOCK), 0)
    for side in range(2):
        columns = pl.ds(pl.multiple_of(jnp.minimum(listed[side], blocks - 1) * BLOCK, BLOCK), BLOCK)
        start = 2 * side * group
        mirrored = offsets - group - start
        local = rule_ref[start : start + group, columns] - (blocks + side) * BLOCK
        rim_x, rim_g = [], []
        for j in range(group):
            found = jnp.dot(
                tables[side], one_hot(source_rows, local[j : j + 1]), preferred_element_type=F32
            )
            rim_x.append(found[:width].astype(BF16))
            rim_g.append(found[width:].astype(BF16))
        rim_x = jnp.concatenate(rim_x, axis=0)
        rim_g = jnp.concatenate(rim_g[::-1], axis=0)
        span = slice(start * width, (start + group) * width)
        mirror_span = slice(mirrored * width, (mirrored + group) * width)
        pre_ref[:, columns] += jnp.dot(w1_ref[:, span], rim_x, preferred_element_type=F32)
        d_hidden_ref[:, columns] += jnp.dot(
            turned_ref[:, mirror_span], rim_g, preferred_element_type=F32
        )

        @pl.when(listed[side] < blocks)
        def _():
            xs_ref[span, columns] = rim_x
            gs_ref[mirror_span, columns] = rim_g

    pre = pre_ref[...]
    sigma = jax.nn.sigmoid(pre)
    hidden = (pre * sigma).astype(BF16)
    d_pre = (d_hidden_ref[...] * sigma * (1.0 + pre * (1.0 - sigma))).astype(BF16)
    for block in range(blocks):
        low, high = block * BLOCK, (block + 1) * BLOCK
        state_ref[block, :width] = hidden[:, low:high]
        state_ref[block, width:] = d_pre[:, low:high]
    for pick, out_ref in zip(pair_blocks(listed, odd), (near_out, far_out)):
        out_ref[...] = state_ref[jnp.minimum(pick, blocks - 1)]

    @pl.when(odd)
    def _():
        first_terms(state_ref, xs_ref, send_ref)

    @pl.when(jnp.logical_not(odd))
    def _():
        second_terms(state_ref, gs_ref, send_ref)


def keep_kernel(state_ref, xs_ref, gs_ref, keep_ref):
    odd = is_odd()

    @pl.when(odd)
    def _():
        second_terms(state_ref, gs_ref, keep_ref)

    @pl.when(jnp.logical_not(odd))
    def _():
        first_terms(state_ref, xs_ref, keep_ref)


def put(source, for_odd, for_even, sem):
    odd = is_odd()
    for chosen, target in ((odd, for_odd), (jnp.logical_not(odd), for_even)):

        @pl.when(chosen)
        def _():
            copy = pltpu.make_async_copy(source, target, sem)
            copy.start()
            copy.wait()


def put_own_kernel(total_ref, first_hbm, second_hbm, sem):
    put(total_ref, second_hbm, first_hbm, sem)


def put_other_kernel(other_ref, first_in, second_in, first_hbm, second_hbm, sem):
    put(other_ref, first_hbm, second_hbm, sem)


def second_kernel(
    near_ref, far_ref, state_ref, rule_ref, x_ref, g_ref, w1_ref, w2_ref,
    out_ref, dx_ref,
    table_ref, hs_ref, ds_ref, turned_ref,
):
    _, rows = x_ref.shape
    blocks = rows // BLOCK
    odd = is_odd()
    for block in range(blocks):
        table_ref[block] = state_ref[block]
    fill_halo(table_ref, near_ref, far_ref, odd, blocks)
    gather(table_ref, rule_ref, hs_ref, ds_ref, blocks)
    turn(w1_ref, turned_ref)
    second = jnp.dot(w2_ref[...], hs_ref[...], preferred_element_type=F32)
    out_ref[...] = (second + x_ref[...].astype(F32)).astype(BF16)
    d_input = jnp.dot(turned_ref[...], ds_ref[...], preferred_element_type=F32)
    dx_ref[...] = (d_input + g_ref[...].astype(F32)).astype(BF16)


def neighbour_pairs(groups, count):
    near = [(i, i ^ 1) for i in range(groups * count)]
    far = []
    for group in range(groups):
        for i in range(count):
            other, tile = group, i + 1 if i % 2 else i - 1
            if not 0 <= tile < count:
                other, tile = (group + 1) % groups, i
            far.append((group * count + i, other * count + tile))
    return near, far


def total_over_tiles(keep, send, scale):
    count = lax.axis_size("tile")
    cores = [(i, i ^ 1) for i in range(count)]
    received = lax.ppermute(send, "tile", cores)
    total = keep + received.astype(F32)
    bits = [1 << b for b in range(1, count.bit_length() - 1)]
    for step, (even_bit, odd_bit) in enumerate(zip(bits, bits[-1:] + bits[:-1])):
        wire = BF16 if step >= len(bits) - 3 else F32
        pairs = [(i, i ^ (odd_bit if i % 2 else even_bit)) for i in range(count)]
        sent = total.astype(wire)
        received = lax.ppermute(sent, "tile", pairs)
        total = sent.astype(F32) + received.astype(F32)
    total = total * scale
    other = lax.ppermute(total, "tile", cores)
    result = jax.ShapeDtypeStruct(total.shape, F32)
    put_own = pl.pallas_call(
        put_own_kernel,
        out_shape=(result, result),
        in_specs=[VMEM],
        out_specs=(HBM, HBM),
        scratch_shapes=[pltpu.SemaphoreType.DMA],
        compiler_params=SMALL,
    )
    half = put_own(total)
    return pl.pallas_call(
        put_other_kernel,
        out_shape=(result, result),
        in_specs=[VMEM, HBM, HBM],
        out_specs=(HBM, HBM),
        scratch_shapes=[pltpu.SemaphoreType.DMA],
        input_output_aliases={1: 0, 2: 1},
        compiler_params=SMALL,
    )(other, *half)


def body(features, rulebook, send_lists, weight_first, weight_second, cotangent):
    width, rows = features.shape
    offsets = rulebook.shape[0]
    blocks = rows // BLOCK
    count = lax.axis_size("tile")
    near_pairs, far_pairs = neighbour_pairs(lax.axis_size("groups"), count)
    axes = ("groups", "tile")
    send_lists = send_lists.reshape(2)
    features, cotangent, rulebook, weight_first, weight_second, send_lists = (
        pltpu.with_memory_space_constraint(array, pltpu.HBM)
        for array in (features, cotangent, rulebook, weight_first, weight_second, send_lists)
    )
    shape = jax.ShapeDtypeStruct
    rim = shape((2 * width, BLOCK), BF16)
    values = shape((width, rows), BF16)
    sums = shape((width, rows), F32)
    gathered = shape((offsets * width, rows), BF16)
    weight = shape((width, offsets * width), BF16)
    terms = shape((width, offsets * width), F32)
    state_shape = shape((blocks, 2 * width, BLOCK), BF16)
    table = pltpu.VMEM((blocks + 2, 2 * width, BLOCK), BF16)

    near, far, lists, x, g, rule, w2, w1 = pl.pallas_call(
        load_kernel,
        out_shape=(
            rim, rim, shape((2, 8, BLOCK), jnp.int32), values, values,
            shape(rulebook.shape, jnp.int32), weight, weight,
        ),
        in_specs=[HBM] * 6,
        out_specs=(VMEM,) * 8,
        scratch_shapes=[pltpu.SMEM((2,), jnp.int32), pltpu.SemaphoreType.DMA((6,))],
        compiler_params=MEDIUM,
    )(send_lists, features, cotangent, rulebook, weight_second, weight_first)
    far = lax.ppermute(far, axes, far_pairs)
    near = lax.ppermute(near, axes, near_pairs)

    work = pl.CostEstimate(
        flops=2 * 2 * width * offsets * rows * (width + BLOCK),
        bytes_accessed=4 * offsets * width * rows,
        transcendentals=0,
    )
    own_phase = pl.pallas_call(
        own_kernel,
        out_shape=(gathered, gathered, sums, sums, weight),
        in_specs=[VMEM] * 5,
        out_specs=(VMEM,) * 5,
        scratch_shapes=[table],
        compiler_params=MEDIUM,
        cost_estimate=work,
    )
    xs, gs, pre, d_hidden, turned = own_phase(rule, x, g, w1, w2)
    state, near, far, send, xs, gs = pl.pallas_call(
        rim_kernel,
        out_shape=(state_shape, rim, rim, weight, gathered, gathered),
        in_specs=[VMEM] * 10,
        out_specs=(VMEM,) * 6,
        scratch_shapes=[pltpu.VMEM((width, rows), F32), pltpu.VMEM((width, rows), F32)],
        input_output_aliases={8: 4, 9: 5},
        compiler_params=MEDIUM,
    )(lists, near, far, pre, d_hidden, rule, w1, turned, xs, gs)
    keep_terms = pl.pallas_call(
        keep_kernel,
        out_shape=terms,
        in_specs=[VMEM] * 3,
        out_specs=VMEM,
        compiler_params=MEDIUM,
    )
    keep = keep_terms(state, xs, gs)

    near = lax.ppermute(near, axes, near_pairs)
    far = lax.ppermute(far, axes, far_pairs)
    second_phase = pl.pallas_call(
        second_kernel,
        out_shape=(values, values),
        in_specs=[VMEM] * 8,
        out_specs=(VMEM, VMEM),
        scratch_shapes=[
            table,
            pltpu.VMEM((offsets * width, rows), BF16),
            pltpu.VMEM((offsets * width, rows), BF16),
            pltpu.VMEM((width, offsets * width), BF16),
        ],
        compiler_params=MEDIUM,
        cost_estimate=work,
    )
    out_features, d_features = second_phase(near, far, state, rule, x, g, w1, w2)

    scale = 1.0 / math.sqrt(rows * count)
    grad_first, grad_second = total_over_tiles(keep, send, scale)
    return out_features, d_features, grad_first, grad_second


def solution(mesh):
    tiles = P(None, ("groups", "tile"))
    return jax.shard_map(
        body,
        mesh=mesh,
        in_specs=(tiles, tiles, tiles, P(), P(), tiles),
        out_specs=(tiles, tiles, P("groups", None), P("groups", None)),
        check_vma=False,
    )
```

```python
import math

import jax
import jax.numpy as jnp
from jax import lax
from jax.experimental import pallas as pl
from jax.experimental.pallas import tpu as pltpu
from jax.sharding import PartitionSpec as P


BLOCK = 128
F32, BF16 = jnp.float32, jnp.bfloat16
HBM = pl.BlockSpec(memory_space=pltpu.HBM)
MEDIUM = pltpu.CompilerParams(vmem_limit_bytes=20 << 20)
VMEM = pl.BlockSpec(memory_space=pltpu.VMEM)
NT = (((1,), (1,)), ((), ()))


def is_odd():
    return lax.axis_index("tile") % 2 == 1


def pair_blocks(listed, odd):
    lower, upper = listed
    return jnp.where(odd, lower, upper), jnp.where(odd, upper, lower)


def fetch(sources, targets, sems):
    copies = [
        pltpu.make_async_copy(source, target, sems.at[i])
        for i, (source, target) in enumerate(zip(sources, targets))
    ]
    for copy in copies:
        copy.start()
    return copies


def load_kernel(
    lists_hbm, x_hbm, g_hbm, rule_hbm, w2_hbm, w1_hbm,
    near_ref, far_ref, lists_out, x_ref, g_ref, rule_ref, w2_ref, w1_ref,
    lists_ref, sems,
):
    width, rows = x_ref.shape
    copies = fetch(
        (lists_hbm, x_hbm, g_hbm, rule_hbm, w2_hbm, w1_hbm),
        (lists_ref, x_ref, g_ref, rule_ref, w2_ref, w1_ref),
        sems,
    )
    for copy in copies[:3]:
        copy.wait()
    picks = pair_blocks((lists_ref[0], lists_ref[1]), is_odd())
    for pick, out_ref in zip(picks, (near_ref, far_ref)):
        start = pl.multiple_of(jnp.minimum(pick, rows // BLOCK - 1) * BLOCK, BLOCK)
        out_ref[:width, :] = x_ref[:, pl.ds(start, BLOCK)]
        out_ref[width:, :] = g_ref[:, pl.ds(start, BLOCK)]
    for side in range(2):
        lists_out[side] = jnp.full(lists_out.shape[1:], lists_ref[side], jnp.int32)
    for copy in copies[3:]:
        copy.wait()


def fill_halo(table_ref, near_ref, far_ref, odd, blocks):
    near, far = near_ref[...], far_ref[...]
    table_ref[blocks] = jnp.where(odd, near, far)
    table_ref[blocks + 1] = jnp.where(odd, far, near)


def one_hot(rows, line):
    return (rows == line).astype(F32).astype(BF16)


def gather(table_ref, rule_ref, first_ref, second_ref, blocks):
    offsets = rule_ref.shape[0]
    group = offsets // 3
    sources, channels, _ = table_ref.shape
    width = channels // 2
    source_rows = lax.broadcasted_iota(jnp.int32, (BLOCK, BLOCK), 0)

    def store(k, low, high, found, mirrored):
        first_ref[k * width : (k + 1) * width, low:high] = found[:width].astype(BF16)
        second_ref[mirrored * width : (mirrored + 1) * width, low:high] = found[
            width:
        ].astype(BF16)

    strays = jnp.zeros((group, BLOCK), jnp.int32)
    for block in range(blocks):
        low, high = block * BLOCK, (block + 1) * BLOCK
        for side in range(3):
            entries = rule_ref[side * group : (side + 1) * group, low:high]
            if side == 1:
                source = block
            else:
                least = jnp.min(entries.astype(F32)).astype(jnp.int32)
                source = jnp.minimum(least // BLOCK, sources - 1)
            local = entries - source * BLOCK
            named = entries < sources * BLOCK
            strays = strays | (
                named & ((local < 0) | (local >= BLOCK))
            ).astype(jnp.int32)
            table = table_ref[source]
            for j in range(group):
                k = side * group + j
                choice = one_hot(source_rows, local[j : j + 1])
                found = jnp.dot(table, choice, preferred_element_type=F32)
                store(k, low, high, found, offsets - 1 - k)

    @pl.when(jnp.max(strays.astype(F32)) > 0)
    def _():
        rows = rule_ref.shape[1]
        every_row = lax.broadcasted_iota(jnp.int32, (BLOCK, rows), 0)

        def one(k, carry):
            line = rule_ref[pl.ds(k, 1), :]
            found = jnp.zeros((channels, rows), F32)
            for source in range(sources):
                choice = one_hot(every_row, line - source * BLOCK)
                found += jnp.dot(table_ref[source], choice, preferred_element_type=F32)
            here = pl.multiple_of(k * width, width)
            there = pl.multiple_of((offsets - 1 - k) * width, width)
            first_ref[pl.ds(here, width), :] = found[:width].astype(BF16)
            second_ref[pl.ds(there, width), :] = found[width:].astype(BF16)
            return carry

        lax.fori_loop(0, offsets, one, 0)


def turn(weight_ref, turned_ref):
    width, depth = weight_ref.shape
    offsets = depth // width
    for k in range(0, offsets, 2):
        count = min(2, offsets - k)
        block = weight_ref[:, k * width : (k + count) * width].astype(F32).T
        pieces = [block[i * width : (i + 1) * width] for i in range(count)]
        joined = pieces[0] if count == 1 else jnp.concatenate(pieces, axis=1)
        turned_ref[:, k * width : (k + count) * width] = joined.astype(BF16)


def own_kernel(
    rule_ref, x_ref, g_ref, w1_ref, w2_ref,
    xs_ref, gs_ref, pre_ref, d_hidden_ref, turned_ref,
    table_ref,
):
    width, rows = x_ref.shape
    blocks = rows // BLOCK
    for block in range(blocks):
        low, high = block * BLOCK, (block + 1) * BLOCK
        table_ref[block, :width] = x_ref[:, low:high]
        table_ref[block, width:] = g_ref[:, low:high]
    table_ref[blocks:] = jnp.zeros_like(table_ref[blocks:])
    gather(table_ref, rule_ref, xs_ref, gs_ref, blocks)
    turn(w2_ref, turned_ref)
    pre_ref[...] = jnp.dot(w1_ref[...], xs_ref[...], preferred_element_type=F32)
    d_hidden_ref[...] = jnp.dot(turned_ref[...], gs_ref[...], preferred_element_type=F32)


def first_terms(state_ref, xs_ref, out_ref):
    blocks = state_ref.shape[0]
    width = state_ref.shape[1] // 2
    depth = xs_ref.shape[0]
    d_pre = jnp.concatenate([state_ref[block, width:] for block in range(blocks)], axis=1)
    for low in range(0, depth, 8 * width):
        high = min(depth, low + 8 * width)
        terms = lax.dot_general(d_pre, xs_ref[low:high], NT, preferred_element_type=F32)
        out_ref[:, low:high] = terms.astype(out_ref.dtype)


def second_terms(state_ref, gs_ref, out_ref):
    blocks = state_ref.shape[0]
    width = state_ref.shape[1] // 2
    depth = gs_ref.shape[0]
    hidden = jnp.concatenate([state_ref[block, :width] for block in range(blocks)], axis=1)
    for low in range(0, depth, 4 * width):
        high = min(depth, low + 4 * width)
        terms = lax.dot_general(gs_ref[low:high], hidden, NT, preferred_element_type=F32)
        for at in range(low, high, 2 * width):
            pieces = [
                terms[i - low : i - low + width] for i in range(at, min(high, at + 2 * width), width)
            ]
            joined = pieces[0] if len(pieces) == 1 else jnp.concatenate(pieces, axis=1)
            out_ref[:, at : at + joined.shape[1]] = joined.astype(out_ref.dtype)


def rim_kernel(
    lists_ref, near_ref, far_ref, pre_in, d_hidden_in, rule_ref, w1_ref, turned_ref, xs_in, gs_in,
    state_ref, near_out, far_out, send_ref, xs_ref, gs_ref,
    pre_ref, d_hidden_ref, rim_ref,
):
    width, rows = pre_in.shape
    blocks = rows // BLOCK
    offsets = rule_ref.shape[0]
    group = offsets // 3
    odd = is_odd()
    listed = [jnp.max(lists_ref[side].astype(F32)).astype(jnp.int32) for side in range(2)]
    near, far = near_ref[...], far_ref[...]
    tables = (jnp.where(odd, near, far), jnp.where(odd, far, near))
    pre_ref[...] = pre_in[...]
    d_hidden_ref[...] = d_hidden_in[...]
    source_rows = lax.broadcasted_iota(jnp.int32, (BLOCK, BLOCK), 0)
    sides = []
    for side in range(2):
        columns = pl.ds(pl.multiple_of(jnp.minimum(listed[side], blocks - 1) * BLOCK, BLOCK), BLOCK)
        start = 2 * side * group
        mirrored = offsets - group - start
        span = slice(start * width, (start + group) * width)
        mirror_span = slice(mirrored * width, (mirrored + group) * width)
        sides.append((listed[side] < blocks, columns, span, mirror_span))
        local = rule_ref[start : start + group, columns] - (blocks + side) * BLOCK
        for j in range(group):
            found = jnp.dot(
                tables[side], one_hot(source_rows, local[j : j + 1]), preferred_element_type=F32
            ).astype(BF16)
            rim_ref[2 * side, j * width : (j + 1) * width] = found[:width]
            place = (group - 1 - j) * width
            rim_ref[2 * side + 1, place : place + width] = found[width:]
    for side, (named, columns, span, mirror_span) in enumerate(sides):
        rim_x, rim_g = rim_ref[2 * side], rim_ref[2 * side + 1]
        pre_ref[:, columns] += jnp.dot(w1_ref[:, span], rim_x, preferred_element_type=F32)
        d_hidden_ref[:, columns] += jnp.dot(
            turned_ref[:, mirror_span], rim_g, preferred_element_type=F32
        )
        xs_ref[span, columns] = jnp.where(named, rim_x, xs_ref[span, columns])
        gs_ref[mirror_span, columns] = jnp.where(named, rim_g, gs_ref[mirror_span, columns])
    pre = pre_ref[...]
    sigma = jax.nn.sigmoid(pre)
    hidden = (pre * sigma).astype(BF16)
    d_pre = (d_hidden_ref[...] * sigma * (1.0 + pre * (1.0 - sigma))).astype(BF16)
    for block in range(blocks):
        low, high = block * BLOCK, (block + 1) * BLOCK
        state_ref[block, :width] = hidden[:, low:high]
        state_ref[block, width:] = d_pre[:, low:high]
    for pick, out_ref in zip(pair_blocks(listed, odd), (near_out, far_out)):
        out_ref[...] = state_ref[jnp.minimum(pick, blocks - 1)]

    @pl.when(odd)
    def _():
        first_terms(state_ref, xs_ref, send_ref)

    @pl.when(jnp.logical_not(odd))
    def _():
        second_terms(state_ref, gs_ref, send_ref)


def keep_kernel(state_ref, xs_ref, gs_ref, keep_ref):
    odd = is_odd()

    @pl.when(odd)
    def _():
        second_terms(state_ref, gs_ref, keep_ref)

    @pl.when(jnp.logical_not(odd))
    def _():
        first_terms(state_ref, xs_ref, keep_ref)


def put(pieces, first_hbm, second_hbm, staging_ref, sems):
    places = []
    for i, (ref, row, own) in enumerate(pieces):
        staging_ref[i] = ref[...].astype(F32)
        places.append((i, slice(row, row + ref.shape[0]), own))
    odd = is_odd()
    for chosen, mine, theirs in (
        (odd, second_hbm, first_hbm),
        (jnp.logical_not(odd), first_hbm, second_hbm),
    ):

        @pl.when(chosen)
        def _():
            copies = fetch(
                [staging_ref.at[i] for i, _, _ in places],
                [(mine if own else theirs).at[rows] for _, rows, own in places],
                sems,
            )
            for copy in copies:
                copy.wait()


def put_own_kernel(own_ref, first_hbm, second_hbm, staging_ref, sems):
    put(((own_ref, 0, True),), first_hbm, second_hbm, staging_ref, sems)


def put_other_kernel(other_ref, first_in, second_in, first_hbm, second_hbm, staging_ref, sems):
    put(((other_ref, 0, False),), first_hbm, second_hbm, staging_ref, sems)


def second_kernel(
    near_ref, far_ref, state_ref, rule_ref, x_ref, g_ref, w1_ref, w2_ref,
    out_ref, dx_ref,
    table_ref, hs_ref, ds_ref, turned_ref,
):
    _, rows = x_ref.shape
    blocks = rows // BLOCK
    odd = is_odd()
    for block in range(blocks):
        table_ref[block] = state_ref[block]
    fill_halo(table_ref, near_ref, far_ref, odd, blocks)
    gather(table_ref, rule_ref, hs_ref, ds_ref, blocks)
    turn(w1_ref, turned_ref)
    second = jnp.dot(w2_ref[...], hs_ref[...], preferred_element_type=F32)
    out_ref[...] = (second + x_ref[...].astype(F32)).astype(BF16)
    d_input = jnp.dot(turned_ref[...], ds_ref[...], preferred_element_type=F32)
    dx_ref[...] = (d_input + g_ref[...].astype(F32)).astype(BF16)


def neighbour_pairs(groups, count):
    near = [(i, i ^ 1) for i in range(groups * count)]
    far = []
    for group in range(groups):
        for i in range(count):
            other, tile = group, i + 1 if i % 2 else i - 1
            if not 0 <= tile < count:
                other, tile = (group + 1) % groups, i
            far.append((group * count + i, other * count + tile))
    return near, far


def total_over_tiles(keep, send, scale):
    count = lax.axis_size("tile")
    cores = [(i, i ^ 1) for i in range(count)]
    received = lax.ppermute(send, "tile", cores)
    total = keep + received.astype(F32)
    bits = [1 << b for b in range(1, count.bit_length() - 1)]
    for step, (even_bit, odd_bit) in enumerate(zip(bits, bits[-1:] + bits[:-1])):
        wire = BF16 if step >= len(bits) - 3 else F32
        pairs = [(i, i ^ (odd_bit if i % 2 else even_bit)) for i in range(count)]
        sent = total.astype(wire)
        received = lax.ppermute(sent, "tile", pairs)
        total = sent.astype(F32) + received.astype(F32)
    total = (total * scale).astype(BF16)
    other = lax.ppermute(total, "tile", cores)
    result = jax.ShapeDtypeStruct(total.shape, F32)
    staging = [pltpu.VMEM((1, *total.shape), F32), pltpu.SemaphoreType.DMA((1,))]
    put_own = pl.pallas_call(
        put_own_kernel,
        out_shape=(result, result),
        in_specs=[VMEM],
        out_specs=(HBM, HBM),
        scratch_shapes=staging,
        compiler_params=MEDIUM,
    )
    half = put_own(total)
    return pl.pallas_call(
        put_other_kernel,
        out_shape=(result, result),
        in_specs=[VMEM, HBM, HBM],
        out_specs=(HBM, HBM),
        scratch_shapes=staging,
        input_output_aliases={1: 0, 2: 1},
        compiler_params=MEDIUM,
    )(other, *half)


def body(features, rulebook, send_lists, weight_first, weight_second, cotangent):
    width, rows = features.shape
    offsets = rulebook.shape[0]
    blocks = rows // BLOCK
    count = lax.axis_size("tile")
    near_pairs, far_pairs = neighbour_pairs(lax.axis_size("groups"), count)
    axes = ("groups", "tile")
    send_lists = send_lists.reshape(2)
    features, cotangent, rulebook, weight_first, weight_second, send_lists = (
        pltpu.with_memory_space_constraint(array, pltpu.HBM)
        for array in (features, cotangent, rulebook, weight_first, weight_second, send_lists)
    )
    shape = jax.ShapeDtypeStruct
    rim = shape((2 * width, BLOCK), BF16)
    values = shape((width, rows), BF16)
    sums = shape((width, rows), F32)
    gathered = shape((offsets * width, rows), BF16)
    weight = shape((width, offsets * width), BF16)
    terms = shape((width, offsets * width), F32)
    state_shape = shape((blocks, 2 * width, BLOCK), BF16)
    table = pltpu.VMEM((blocks + 2, 2 * width, BLOCK), BF16)

    near, far, lists, x, g, rule, w2, w1 = pl.pallas_call(
        load_kernel,
        out_shape=(
            rim, rim, shape((2, 8, BLOCK), jnp.int32), values, values,
            shape(rulebook.shape, jnp.int32), weight, weight,
        ),
        in_specs=[HBM] * 6,
        out_specs=(VMEM,) * 8,
        scratch_shapes=[pltpu.SMEM((2,), jnp.int32), pltpu.SemaphoreType.DMA((6,))],
        compiler_params=MEDIUM,
    )(send_lists, features, cotangent, rulebook, weight_second, weight_first)
    far = lax.ppermute(far, axes, far_pairs)
    near = lax.ppermute(near, axes, near_pairs)

    work = pl.CostEstimate(
        flops=2 * 2 * width * offsets * rows * (width + BLOCK),
        bytes_accessed=4 * offsets * width * rows,
        transcendentals=0,
    )
    own_phase = pl.pallas_call(
        own_kernel,
        out_shape=(gathered, gathered, sums, sums, weight),
        in_specs=[VMEM] * 5,
        out_specs=(VMEM,) * 5,
        scratch_shapes=[table],
        compiler_params=MEDIUM,
        cost_estimate=work,
    )
    xs, gs, pre, d_hidden, turned = own_phase(rule, x, g, w1, w2)
    state, near, far, send, xs, gs = pl.pallas_call(
        rim_kernel,
        out_shape=(state_shape, rim, rim, weight, gathered, gathered),
        in_specs=[VMEM] * 10,
        out_specs=(VMEM,) * 6,
        scratch_shapes=[
            pltpu.VMEM((width, rows), F32),
            pltpu.VMEM((width, rows), F32),
            pltpu.VMEM((4, offsets // 3 * width, BLOCK), BF16),
        ],
        input_output_aliases={8: 4, 9: 5},
        compiler_params=MEDIUM,
    )(lists, near, far, pre, d_hidden, rule, w1, turned, xs, gs)
    keep_terms = pl.pallas_call(
        keep_kernel,
        out_shape=terms,
        in_specs=[VMEM] * 3,
        out_specs=VMEM,
        compiler_params=MEDIUM,
    )
    keep = keep_terms(state, xs, gs)

    near = lax.ppermute(near, axes, near_pairs)
    far = lax.ppermute(far, axes, far_pairs)
    second_phase = pl.pallas_call(
        second_kernel,
        out_shape=(values, values),
        in_specs=[VMEM] * 8,
        out_specs=(VMEM, VMEM),
        scratch_shapes=[
            table,
            pltpu.VMEM((offsets * width, rows), BF16),
            pltpu.VMEM((offsets * width, rows), BF16),
            pltpu.VMEM((width, offsets * width), BF16),
        ],
        compiler_params=MEDIUM,
        cost_estimate=work,
    )
    out_features, d_features = second_phase(near, far, state, rule, x, g, w1, w2)

    scale = 1.0 / math.sqrt(rows * count)
    grad_first, grad_second = total_over_tiles(keep, send, scale)
    return out_features, d_features, grad_first, grad_second


def solution(mesh):
    tiles = P(None, ("groups", "tile"))
    return jax.shard_map(
        body,
        mesh=mesh,
        in_specs=(tiles, tiles, tiles, P(), P(), tiles),
        out_specs=(tiles, tiles, P("groups", None), P("groups", None)),
        check_vma=False,
    )
```

```python
import math

import jax
import jax.numpy as jnp
from jax import lax
from jax.experimental import pallas as pl
from jax.experimental.pallas import tpu as pltpu
from jax.sharding import PartitionSpec as P


BLOCK = 128
F32, BF16 = jnp.float32, jnp.bfloat16
HBM = pl.BlockSpec(memory_space=pltpu.HBM)
MEDIUM = pltpu.CompilerParams(vmem_limit_bytes=20 << 20)
VMEM = pl.BlockSpec(memory_space=pltpu.VMEM)
NT = (((1,), (1,)), ((), ()))


def in_chunks(ref, count=4):
    rows = ref.shape[0] // count
    return [ref.at[i * rows : (i + 1) * rows] for i in range(count)]


def is_odd():
    return lax.axis_index("tile") % 2 == 1


def pair_blocks(listed, odd):
    lower, upper = listed
    return jnp.where(odd, lower, upper), jnp.where(odd, upper, lower)


def fetch(sources, targets, sems):
    copies = [
        pltpu.make_async_copy(source, target, sems.at[i])
        for i, (source, target) in enumerate(zip(sources, targets))
    ]
    for copy in copies:
        copy.start()
    return copies


def load_kernel(
    lists_hbm, x_hbm, g_hbm, rule_hbm, w2_hbm, w1_hbm,
    near_ref, far_ref, lists_out, x_ref, g_ref, rule_ref, w2_ref, w1_ref,
    lists_ref, sems,
):
    width, rows = x_ref.shape
    copies = fetch(
        (lists_hbm, x_hbm, g_hbm, rule_hbm, *in_chunks(w2_hbm), *in_chunks(w1_hbm)),
        (lists_ref, x_ref, g_ref, rule_ref, *in_chunks(w2_ref), *in_chunks(w1_ref)),
        sems,
    )
    for copy in copies[:3]:
        copy.wait()
    picks = pair_blocks((lists_ref[0], lists_ref[1]), is_odd())
    for pick, out_ref in zip(picks, (near_ref, far_ref)):
        start = pl.multiple_of(jnp.minimum(pick, rows // BLOCK - 1) * BLOCK, BLOCK)
        out_ref[:width, :] = x_ref[:, pl.ds(start, BLOCK)]
        out_ref[width:, :] = g_ref[:, pl.ds(start, BLOCK)]
    for side in range(2):
        lists_out[side] = jnp.full(lists_out.shape[1:], lists_ref[side], jnp.int32)
    for copy in copies[3:]:
        copy.wait()


def fill_halo(table_ref, near_ref, far_ref, odd, blocks):
    near, far = near_ref[...], far_ref[...]
    table_ref[blocks] = jnp.where(odd, near, far)
    table_ref[blocks + 1] = jnp.where(odd, far, near)


def one_hot(rows, line):
    return (rows == line).astype(F32).astype(BF16)


def select_rows(table, rows, local):
    found = []
    for j in range(0, local.shape[0], 2):
        lines = [local[i : i + 1] for i in range(j, min(j + 2, local.shape[0]))]
        choice = jnp.concatenate([one_hot(rows, line) for line in lines], axis=1)
        both = jnp.dot(table, choice, preferred_element_type=F32).astype(BF16)
        found += [both[:, i * BLOCK : (i + 1) * BLOCK] for i in range(len(lines))]
    return found


def gather(table_ref, rule_ref, first_ref, second_ref, blocks):
    offsets = rule_ref.shape[0]
    group = offsets // 3
    sources, channels, _ = table_ref.shape
    width = channels // 2
    source_rows = lax.broadcasted_iota(jnp.int32, (BLOCK, BLOCK), 0)

    def store(k, low, high, found, mirrored):
        first_ref[k * width : (k + 1) * width, low:high] = found[:width]
        second_ref[mirrored * width : (mirrored + 1) * width, low:high] = found[width:]

    strays = jnp.zeros((group, BLOCK), jnp.int32)
    for block in range(blocks):
        low, high = block * BLOCK, (block + 1) * BLOCK
        for side in range(3):
            entries = rule_ref[side * group : (side + 1) * group, low:high]
            if side == 1:
                source = block
            else:
                least = jnp.min(entries.astype(F32)).astype(jnp.int32)
                source = jnp.minimum(least // BLOCK, sources - 1)
            local = entries - source * BLOCK
            named = entries < sources * BLOCK
            strays = strays | (
                named & ((local < 0) | (local >= BLOCK))
            ).astype(jnp.int32)
            for j, found in enumerate(select_rows(table_ref[source], source_rows, local)):
                k = side * group + j
                store(k, low, high, found, offsets - 1 - k)

    @pl.when(jnp.max(strays.astype(F32)) > 0)
    def _():
        rows = rule_ref.shape[1]
        every_row = lax.broadcasted_iota(jnp.int32, (BLOCK, rows), 0)

        def one(k, carry):
            line = rule_ref[pl.ds(k, 1), :]
            found = jnp.zeros((channels, rows), F32)
            for source in range(sources):
                choice = one_hot(every_row, line - source * BLOCK)
                found += jnp.dot(table_ref[source], choice, preferred_element_type=F32)
            here = pl.multiple_of(k * width, width)
            there = pl.multiple_of((offsets - 1 - k) * width, width)
            first_ref[pl.ds(here, width), :] = found[:width].astype(BF16)
            second_ref[pl.ds(there, width), :] = found[width:].astype(BF16)
            return carry

        lax.fori_loop(0, offsets, one, 0)


def turn(weight_ref, turned_ref):
    width, depth = weight_ref.shape
    offsets = depth // width
    for k in range(0, offsets, 2):
        count = min(2, offsets - k)
        block = weight_ref[:, k * width : (k + count) * width].astype(F32).T
        pieces = [block[i * width : (i + 1) * width] for i in range(count)]
        joined = pieces[0] if count == 1 else jnp.concatenate(pieces, axis=1)
        turned_ref[:, k * width : (k + count) * width] = joined.astype(BF16)


def own_kernel(
    rule_ref, x_ref, g_ref, w1_ref, w2_ref,
    xs_ref, gs_ref, pre_ref, d_hidden_ref, turned_ref,
    table_ref,
):
    width, rows = x_ref.shape
    blocks = rows // BLOCK
    for block in range(blocks):
        low, high = block * BLOCK, (block + 1) * BLOCK
        table_ref[block, :width] = x_ref[:, low:high]
        table_ref[block, width:] = g_ref[:, low:high]
    table_ref[blocks:] = jnp.zeros_like(table_ref[blocks:])
    gather(table_ref, rule_ref, xs_ref, gs_ref, blocks)
    turn(w2_ref, turned_ref)
    pre_ref[...] = jnp.dot(w1_ref[...], xs_ref[...], preferred_element_type=F32)
    d_hidden_ref[...] = jnp.dot(turned_ref[...], gs_ref[...], preferred_element_type=F32)


def first_terms(state_ref, xs_ref, out_ref):
    blocks = state_ref.shape[0]
    width = state_ref.shape[1] // 2
    depth = xs_ref.shape[0]
    d_pre = jnp.concatenate([state_ref[block, width:] for block in range(blocks)], axis=1)
    for low in range(0, depth, 8 * width):
        high = min(depth, low + 8 * width)
        terms = lax.dot_general(d_pre, xs_ref[low:high], NT, preferred_element_type=F32)
        out_ref[:, low:high] = terms.astype(out_ref.dtype)


def second_terms(state_ref, gs_ref, out_ref):
    blocks = state_ref.shape[0]
    width = state_ref.shape[1] // 2
    depth = gs_ref.shape[0]
    hidden = jnp.concatenate([state_ref[block, :width] for block in range(blocks)], axis=1)
    for low in range(0, depth, 4 * width):
        high = min(depth, low + 4 * width)
        terms = lax.dot_general(gs_ref[low:high], hidden, NT, preferred_element_type=F32)
        for at in range(low, high, 2 * width):
            pieces = [
                terms[i - low : i - low + width] for i in range(at, min(high, at + 2 * width), width)
            ]
            joined = pieces[0] if len(pieces) == 1 else jnp.concatenate(pieces, axis=1)
            out_ref[:, at : at + joined.shape[1]] = joined.astype(out_ref.dtype)


def rim_kernel(
    lists_ref, near_ref, far_ref, pre_in, d_hidden_in, rule_ref, w1_ref, turned_ref, xs_in, gs_in,
    state_ref, near_out, far_out, send_ref, xs_ref, gs_ref,
    pre_ref, d_hidden_ref, rim_ref,
):
    width, rows = pre_in.shape
    blocks = rows // BLOCK
    offsets = rule_ref.shape[0]
    group = offsets // 3
    odd = is_odd()
    listed = [jnp.max(lists_ref[side].astype(F32)).astype(jnp.int32) for side in range(2)]
    near, far = near_ref[...], far_ref[...]
    tables = (jnp.where(odd, near, far), jnp.where(odd, far, near))
    pre_ref[...] = pre_in[...]
    d_hidden_ref[...] = d_hidden_in[...]
    source_rows = lax.broadcasted_iota(jnp.int32, (BLOCK, BLOCK), 0)
    sides = []
    for side in range(2):
        columns = pl.ds(pl.multiple_of(jnp.minimum(listed[side], blocks - 1) * BLOCK, BLOCK), BLOCK)
        start = 2 * side * group
        mirrored = offsets - group - start
        span = slice(start * width, (start + group) * width)
        mirror_span = slice(mirrored * width, (mirrored + group) * width)
        sides.append((listed[side] < blocks, columns, span, mirror_span))
        local = rule_ref[start : start + group, columns] - (blocks + side) * BLOCK
        for j, found in enumerate(select_rows(tables[side], source_rows, local)):
            rim_ref[2 * side, j * width : (j + 1) * width] = found[:width]
            place = (group - 1 - j) * width
            rim_ref[2 * side + 1, place : place + width] = found[width:]
    for side, (named, columns, span, mirror_span) in enumerate(sides):
        rim_x, rim_g = rim_ref[2 * side], rim_ref[2 * side + 1]
        pre_ref[:, columns] += jnp.dot(w1_ref[:, span], rim_x, preferred_element_type=F32)
        d_hidden_ref[:, columns] += jnp.dot(
            turned_ref[:, mirror_span], rim_g, preferred_element_type=F32
        )
        xs_ref[span, columns] = jnp.where(named, rim_x, xs_ref[span, columns])
        gs_ref[mirror_span, columns] = jnp.where(named, rim_g, gs_ref[mirror_span, columns])
    pre = pre_ref[...]
    sigma = jax.nn.sigmoid(pre)
    hidden = (pre * sigma).astype(BF16)
    d_pre = (d_hidden_ref[...] * sigma * (1.0 + pre * (1.0 - sigma))).astype(BF16)
    for block in range(blocks):
        low, high = block * BLOCK, (block + 1) * BLOCK
        state_ref[block, :width] = hidden[:, low:high]
        state_ref[block, width:] = d_pre[:, low:high]
    for pick, out_ref in zip(pair_blocks(listed, odd), (near_out, far_out)):
        out_ref[...] = state_ref[jnp.minimum(pick, blocks - 1)]

    @pl.when(odd)
    def _():
        first_terms(state_ref, xs_ref, send_ref)

    @pl.when(jnp.logical_not(odd))
    def _():
        second_terms(state_ref, gs_ref, send_ref)


def keep_kernel(state_ref, xs_ref, gs_ref, keep_ref):
    odd = is_odd()

    @pl.when(odd)
    def _():
        second_terms(state_ref, gs_ref, keep_ref)

    @pl.when(jnp.logical_not(odd))
    def _():
        first_terms(state_ref, xs_ref, keep_ref)


def put(source_ref, for_odd, for_even, staging_ref, sems):
    odd = is_odd()
    for chosen, target in ((odd, for_odd), (jnp.logical_not(odd), for_even)):

        @pl.when(chosen)
        def _():
            copies = []
            chunks = zip(in_chunks(source_ref), in_chunks(staging_ref), in_chunks(target))
            for i, (source, staging, place) in enumerate(chunks):
                staging[...] = source[...].astype(F32)
                copies.append(pltpu.make_async_copy(staging, place, sems.at[i]))
                copies[-1].start()
            for copy in copies:
                copy.wait()


def put_own_kernel(own_ref, first_hbm, second_hbm, staging_ref, sems):
    put(own_ref, second_hbm, first_hbm, staging_ref, sems)


def put_other_kernel(other_ref, first_in, second_in, first_hbm, second_hbm, staging_ref, sems):
    put(other_ref, first_hbm, second_hbm, staging_ref, sems)


def second_kernel(
    near_ref, far_ref, state_ref, rule_ref, x_ref, g_ref, w1_ref, w2_ref,
    out_ref, dx_ref,
    table_ref, hs_ref, ds_ref, turned_ref,
):
    _, rows = x_ref.shape
    blocks = rows // BLOCK
    odd = is_odd()
    for block in range(blocks):
        table_ref[block] = state_ref[block]
    fill_halo(table_ref, near_ref, far_ref, odd, blocks)
    gather(table_ref, rule_ref, hs_ref, ds_ref, blocks)
    turn(w1_ref, turned_ref)
    second = jnp.dot(w2_ref[...], hs_ref[...], preferred_element_type=F32)
    out_ref[...] = (second + x_ref[...].astype(F32)).astype(BF16)
    d_input = jnp.dot(turned_ref[...], ds_ref[...], preferred_element_type=F32)
    dx_ref[...] = (d_input + g_ref[...].astype(F32)).astype(BF16)


def neighbour_pairs(groups, count):
    near = [(i, i ^ 1) for i in range(groups * count)]
    far = []
    for group in range(groups):
        for i in range(count):
            other, tile = group, i + 1 if i % 2 else i - 1
            if not 0 <= tile < count:
                other, tile = (group + 1) % groups, i
            far.append((group * count + i, other * count + tile))
    return near, far


def total_over_tiles(keep, send, scale):
    count = lax.axis_size("tile")
    cores = [(i, i ^ 1) for i in range(count)]
    received = lax.ppermute(send, "tile", cores)
    total = keep + received.astype(F32)
    bits = [1 << b for b in range(1, count.bit_length() - 1)]
    for step, (even_bit, odd_bit) in enumerate(zip(bits, bits[-1:] + bits[:-1])):
        wire = BF16 if step >= len(bits) - 3 else F32
        pairs = [(i, i ^ (odd_bit if i % 2 else even_bit)) for i in range(count)]
        sent = total.astype(wire)
        received = lax.ppermute(sent, "tile", pairs)
        total = sent.astype(F32) + received.astype(F32)
    total = (total * scale).astype(BF16)
    other = lax.ppermute(total, "tile", cores)
    result = jax.ShapeDtypeStruct(total.shape, F32)
    staging = [pltpu.VMEM(total.shape, F32), pltpu.SemaphoreType.DMA((4,))]
    put_own = pl.pallas_call(
        put_own_kernel,
        out_shape=(result, result),
        in_specs=[VMEM],
        out_specs=(HBM, HBM),
        scratch_shapes=staging,
        compiler_params=MEDIUM,
    )
    half = put_own(total)
    return pl.pallas_call(
        put_other_kernel,
        out_shape=(result, result),
        in_specs=[VMEM, HBM, HBM],
        out_specs=(HBM, HBM),
        scratch_shapes=staging,
        input_output_aliases={1: 0, 2: 1},
        compiler_params=MEDIUM,
    )(other, *half)


def body(features, rulebook, send_lists, weight_first, weight_second, cotangent):
    width, rows = features.shape
    offsets = rulebook.shape[0]
    blocks = rows // BLOCK
    count = lax.axis_size("tile")
    near_pairs, far_pairs = neighbour_pairs(lax.axis_size("groups"), count)
    axes = ("groups", "tile")
    send_lists = send_lists.reshape(2)
    features, cotangent, rulebook, weight_first, weight_second, send_lists = (
        pltpu.with_memory_space_constraint(array, pltpu.HBM)
        for array in (features, cotangent, rulebook, weight_first, weight_second, send_lists)
    )
    shape = jax.ShapeDtypeStruct
    rim = shape((2 * width, BLOCK), BF16)
    values = shape((width, rows), BF16)
    sums = shape((width, rows), F32)
    gathered = shape((offsets * width, rows), BF16)
    weight = shape((width, offsets * width), BF16)
    terms = shape((width, offsets * width), F32)
    state_shape = shape((blocks, 2 * width, BLOCK), BF16)
    table = pltpu.VMEM((blocks + 2, 2 * width, BLOCK), BF16)

    near, far, lists, x, g, rule, w2, w1 = pl.pallas_call(
        load_kernel,
        out_shape=(
            rim, rim, shape((2, 8, BLOCK), jnp.int32), values, values,
            shape(rulebook.shape, jnp.int32), weight, weight,
        ),
        in_specs=[HBM] * 6,
        out_specs=(VMEM,) * 8,
        scratch_shapes=[pltpu.SMEM((2,), jnp.int32), pltpu.SemaphoreType.DMA((12,))],
        compiler_params=MEDIUM,
    )(send_lists, features, cotangent, rulebook, weight_second, weight_first)
    far = lax.ppermute(far, axes, far_pairs)
    near = lax.ppermute(near, axes, near_pairs)

    work = pl.CostEstimate(
        flops=2 * 2 * width * offsets * rows * (width + BLOCK),
        bytes_accessed=4 * offsets * width * rows,
        transcendentals=0,
    )
    own_phase = pl.pallas_call(
        own_kernel,
        out_shape=(gathered, gathered, sums, sums, weight),
        in_specs=[VMEM] * 5,
        out_specs=(VMEM,) * 5,
        scratch_shapes=[table],
        compiler_params=MEDIUM,
        cost_estimate=work,
    )
    xs, gs, pre, d_hidden, turned = own_phase(rule, x, g, w1, w2)
    state, near, far, send, xs, gs = pl.pallas_call(
        rim_kernel,
        out_shape=(state_shape, rim, rim, weight, gathered, gathered),
        in_specs=[VMEM] * 10,
        out_specs=(VMEM,) * 6,
        scratch_shapes=[
            pltpu.VMEM((width, rows), F32),
            pltpu.VMEM((width, rows), F32),
            pltpu.VMEM((4, offsets // 3 * width, BLOCK), BF16),
        ],
        input_output_aliases={8: 4, 9: 5},
        compiler_params=MEDIUM,
    )(lists, near, far, pre, d_hidden, rule, w1, turned, xs, gs)
    keep_terms = pl.pallas_call(
        keep_kernel,
        out_shape=terms,
        in_specs=[VMEM] * 3,
        out_specs=VMEM,
        compiler_params=MEDIUM,
    )
    keep = keep_terms(state, xs, gs)

    near = lax.ppermute(near, axes, near_pairs)
    far = lax.ppermute(far, axes, far_pairs)
    second_phase = pl.pallas_call(
        second_kernel,
        out_shape=(values, values),
        in_specs=[VMEM] * 8,
        out_specs=(VMEM, VMEM),
        scratch_shapes=[
            table,
            pltpu.VMEM((offsets * width, rows), BF16),
            pltpu.VMEM((offsets * width, rows), BF16),
            pltpu.VMEM((width, offsets * width), BF16),
        ],
        compiler_params=MEDIUM,
        cost_estimate=work,
    )
    out_features, d_features = second_phase(near, far, state, rule, x, g, w1, w2)

    scale = 1.0 / math.sqrt(rows * count)
    grad_first, grad_second = total_over_tiles(keep, send, scale)
    return out_features, d_features, grad_first, grad_second


def solution(mesh):
    tiles = P(None, ("groups", "tile"))
    return jax.shard_map(
        body,
        mesh=mesh,
        in_specs=(tiles, tiles, tiles, P(), P(), tiles),
        out_specs=(tiles, tiles, P("groups", None), P("groups", None)),
        check_vma=False,
    )
```

```python
import math

import jax
import jax.numpy as jnp
from jax import lax
from jax.experimental import pallas as pl
from jax.experimental.pallas import tpu as pltpu
from jax.sharding import PartitionSpec as P


BLOCK = 128
F32, BF16 = jnp.float32, jnp.bfloat16
HBM = pl.BlockSpec(memory_space=pltpu.HBM)
MEDIUM = pltpu.CompilerParams(vmem_limit_bytes=20 << 20)
VMEM = pl.BlockSpec(memory_space=pltpu.VMEM)
NT = (((1,), (1,)), ((), ()))


def in_chunks(ref, count=4):
    rows = ref.shape[0] // count
    return [ref.at[i * rows : (i + 1) * rows] for i in range(count)]


def is_odd():
    return lax.axis_index("tile") % 2 == 1


def pair_blocks(listed, odd):
    lower, upper = listed
    return jnp.where(odd, lower, upper), jnp.where(odd, upper, lower)


def fetch(sources, targets, sems):
    copies = [
        pltpu.make_async_copy(source, target, sems.at[i])
        for i, (source, target) in enumerate(zip(sources, targets))
    ]
    for copy in copies:
        copy.start()
    return copies


def load_kernel(
    lists_hbm, x_hbm, g_hbm, rule_hbm, w2_hbm, w1_hbm,
    near_ref, far_ref, lists_out, x_ref, g_ref, rule_ref, w2_ref, w1_ref,
    lists_ref, sems,
):
    width, rows = x_ref.shape
    copies = fetch(
        (lists_hbm, x_hbm, g_hbm, rule_hbm, *in_chunks(w2_hbm), *in_chunks(w1_hbm)),
        (lists_ref, x_ref, g_ref, rule_ref, *in_chunks(w2_ref), *in_chunks(w1_ref)),
        sems,
    )
    for copy in copies[:3]:
        copy.wait()
    picks = pair_blocks((lists_ref[0], lists_ref[1]), is_odd())
    for pick, out_ref in zip(picks, (near_ref, far_ref)):
        start = pl.multiple_of(jnp.minimum(pick, rows // BLOCK - 1) * BLOCK, BLOCK)
        out_ref[:width, :] = x_ref[:, pl.ds(start, BLOCK)]
        out_ref[width:, :] = g_ref[:, pl.ds(start, BLOCK)]
    for side in range(2):
        lists_out[side] = jnp.full(lists_out.shape[1:], lists_ref[side], jnp.int32)
    for copy in copies[3:]:
        copy.wait()


def fill_halo(table_ref, near_ref, far_ref, odd, blocks):
    near, far = near_ref[...], far_ref[...]
    table_ref[blocks] = jnp.where(odd, near, far)
    table_ref[blocks + 1] = jnp.where(odd, far, near)


def one_hot(rows, line):
    return (rows == line).astype(F32).astype(BF16)


def select_rows(table, rows, local):
    found = []
    for j in range(0, local.shape[0], 2):
        lines = [local[i : i + 1] for i in range(j, min(j + 2, local.shape[0]))]
        choice = jnp.concatenate([one_hot(rows, line) for line in lines], axis=1)
        both = jnp.dot(table, choice, preferred_element_type=F32).astype(BF16)
        found += [both[:, i * BLOCK : (i + 1) * BLOCK] for i in range(len(lines))]
    return found


def gather(table_ref, rule_ref, first_ref, second_ref, blocks):
    offsets = rule_ref.shape[0]
    group = offsets // 3
    sources, channels, _ = table_ref.shape
    width = channels // 2
    source_rows = lax.broadcasted_iota(jnp.int32, (BLOCK, BLOCK), 0)

    def store(k, low, high, found, mirrored):
        first_ref[k * width : (k + 1) * width, low:high] = found[:width]
        second_ref[mirrored * width : (mirrored + 1) * width, low:high] = found[width:]

    strays = jnp.zeros((group, BLOCK), jnp.int32)
    for block in range(blocks):
        low, high = block * BLOCK, (block + 1) * BLOCK
        for side in range(3):
            entries = rule_ref[side * group : (side + 1) * group, low:high]
            if side == 1:
                source = block
            else:
                least = jnp.min(entries.astype(F32)).astype(jnp.int32)
                source = jnp.minimum(least // BLOCK, sources - 1)
            local = entries - source * BLOCK
            named = entries < sources * BLOCK
            strays = strays | (
                named & ((local < 0) | (local >= BLOCK))
            ).astype(jnp.int32)
            for j, found in enumerate(select_rows(table_ref[source], source_rows, local)):
                k = side * group + j
                store(k, low, high, found, offsets - 1 - k)

    @pl.when(jnp.max(strays.astype(F32)) > 0)
    def _():
        rows = rule_ref.shape[1]
        every_row = lax.broadcasted_iota(jnp.int32, (BLOCK, rows), 0)

        def one(k, carry):
            line = rule_ref[pl.ds(k, 1), :]
            found = jnp.zeros((channels, rows), F32)
            for source in range(sources):
                choice = one_hot(every_row, line - source * BLOCK)
                found += jnp.dot(table_ref[source], choice, preferred_element_type=F32)
            here = pl.multiple_of(k * width, width)
            there = pl.multiple_of((offsets - 1 - k) * width, width)
            first_ref[pl.ds(here, width), :] = found[:width].astype(BF16)
            second_ref[pl.ds(there, width), :] = found[width:].astype(BF16)
            return carry

        lax.fori_loop(0, offsets, one, 0)


def turn(weight_ref, turned_ref):
    width, depth = weight_ref.shape
    offsets = depth // width
    for k in range(0, offsets, 2):
        count = min(2, offsets - k)
        block = weight_ref[:, k * width : (k + count) * width].astype(F32).T
        pieces = [block[i * width : (i + 1) * width] for i in range(count)]
        joined = pieces[0] if count == 1 else jnp.concatenate(pieces, axis=1)
        turned_ref[:, k * width : (k + count) * width] = joined.astype(BF16)


def own_kernel(
    rule_ref, x_ref, g_ref, w1_ref, w2_ref,
    xs_ref, gs_ref, pre_ref, d_hidden_ref, turned_ref,
    table_ref,
):
    width, rows = x_ref.shape
    blocks = rows // BLOCK
    for block in range(blocks):
        low, high = block * BLOCK, (block + 1) * BLOCK
        table_ref[block, :width] = x_ref[:, low:high]
        table_ref[block, width:] = g_ref[:, low:high]
    table_ref[blocks:] = jnp.zeros_like(table_ref[blocks:])
    gather(table_ref, rule_ref, xs_ref, gs_ref, blocks)
    turn(w2_ref, turned_ref)
    pre_ref[...] = jnp.dot(w1_ref[...], xs_ref[...], preferred_element_type=F32)
    d_hidden_ref[...] = jnp.dot(turned_ref[...], gs_ref[...], preferred_element_type=F32)


def packed_rows(offsets, width):
    return offsets * width * width // BLOCK


def pack(out_ref, pair, pieces):
    width = pieces[0].shape[0]
    if len(pieces) == 1:
        pieces = [pieces[0][: width // 2], pieces[0][width // 2 :]]
    joined = jnp.concatenate(pieces, axis=1)
    row = pair * width
    out_ref[row : row + joined.shape[0]] = joined.astype(out_ref.dtype)


def first_terms(state_ref, xs_ref, out_ref):
    blocks = state_ref.shape[0]
    width = state_ref.shape[1] // 2
    depth = xs_ref.shape[0]
    d_pre = jnp.concatenate([state_ref[block, width:] for block in range(blocks)], axis=1)
    for low in range(0, depth, 8 * width):
        high = min(depth, low + 8 * width)
        terms = lax.dot_general(d_pre, xs_ref[low:high], NT, preferred_element_type=F32)
        for at in range(low, high, 2 * width):
            end = min(high, at + 2 * width)
            pair = terms[:, at - low : end - low]
            if end - at == BLOCK:
                row = at // BLOCK * width
                out_ref[row : row + width] = pair.astype(out_ref.dtype)
            else:
                pack(out_ref, at // BLOCK, [pair])


def second_terms(state_ref, gs_ref, out_ref):
    blocks = state_ref.shape[0]
    width = state_ref.shape[1] // 2
    depth = gs_ref.shape[0]
    hidden = jnp.concatenate([state_ref[block, :width] for block in range(blocks)], axis=1)
    for low in range(0, depth, 4 * width):
        high = min(depth, low + 4 * width)
        terms = lax.dot_general(gs_ref[low:high], hidden, NT, preferred_element_type=F32)
        for at in range(low, high, 2 * width):
            pieces = [
                terms[i - low : i - low + width] for i in range(at, min(high, at + 2 * width), width)
            ]
            pack(out_ref, at // BLOCK, pieces)


def rim_kernel(
    lists_ref, near_ref, far_ref, pre_in, d_hidden_in, rule_ref, w1_ref, turned_ref, xs_in, gs_in,
    state_ref, near_out, far_out, send_ref, xs_ref, gs_ref,
    pre_ref, d_hidden_ref, rim_ref,
):
    width, rows = pre_in.shape
    blocks = rows // BLOCK
    offsets = rule_ref.shape[0]
    group = offsets // 3
    odd = is_odd()
    listed = [jnp.max(lists_ref[side].astype(F32)).astype(jnp.int32) for side in range(2)]
    near, far = near_ref[...], far_ref[...]
    tables = (jnp.where(odd, near, far), jnp.where(odd, far, near))
    pre_ref[...] = pre_in[...]
    d_hidden_ref[...] = d_hidden_in[...]
    source_rows = lax.broadcasted_iota(jnp.int32, (BLOCK, BLOCK), 0)
    sides = []
    for side in range(2):
        columns = pl.ds(pl.multiple_of(jnp.minimum(listed[side], blocks - 1) * BLOCK, BLOCK), BLOCK)
        start = 2 * side * group
        mirrored = offsets - group - start
        span = slice(start * width, (start + group) * width)
        mirror_span = slice(mirrored * width, (mirrored + group) * width)
        sides.append((listed[side] < blocks, columns, span, mirror_span))
        local = rule_ref[start : start + group, columns] - (blocks + side) * BLOCK
        for j, found in enumerate(select_rows(tables[side], source_rows, local)):
            rim_ref[2 * side, j * width : (j + 1) * width] = found[:width]
            place = (group - 1 - j) * width
            rim_ref[2 * side + 1, place : place + width] = found[width:]
    for side, (named, columns, span, mirror_span) in enumerate(sides):
        rim_x, rim_g = rim_ref[2 * side], rim_ref[2 * side + 1]
        pre_ref[:, columns] += jnp.dot(w1_ref[:, span], rim_x, preferred_element_type=F32)
        d_hidden_ref[:, columns] += jnp.dot(
            turned_ref[:, mirror_span], rim_g, preferred_element_type=F32
        )
        xs_ref[span, columns] = jnp.where(named, rim_x, xs_ref[span, columns])
        gs_ref[mirror_span, columns] = jnp.where(named, rim_g, gs_ref[mirror_span, columns])
    pre = pre_ref[...]
    sigma = jax.nn.sigmoid(pre)
    hidden = (pre * sigma).astype(BF16)
    d_pre = (d_hidden_ref[...] * sigma * (1.0 + pre * (1.0 - sigma))).astype(BF16)
    for block in range(blocks):
        low, high = block * BLOCK, (block + 1) * BLOCK
        state_ref[block, :width] = hidden[:, low:high]
        state_ref[block, width:] = d_pre[:, low:high]
    for pick, out_ref in zip(pair_blocks(listed, odd), (near_out, far_out)):
        out_ref[...] = state_ref[jnp.minimum(pick, blocks - 1)]

    @pl.when(odd)
    def _():
        first_terms(state_ref, xs_ref, send_ref)

    @pl.when(jnp.logical_not(odd))
    def _():
        second_terms(state_ref, gs_ref, send_ref)


def keep_kernel(state_ref, xs_ref, gs_ref, keep_ref):
    odd = is_odd()

    @pl.when(odd)
    def _():
        second_terms(state_ref, gs_ref, keep_ref)

    @pl.when(jnp.logical_not(odd))
    def _():
        first_terms(state_ref, xs_ref, keep_ref)


def put(source_ref, for_odd, for_even, staging_ref, sems):
    width, depth = staging_ref.shape
    for pair in range(depth // BLOCK):
        block = source_ref[pair * width : (pair + 1) * width]
        staging_ref[:, pair * BLOCK : (pair + 1) * BLOCK] = block.astype(F32)
    if depth % BLOCK:
        low, half = depth - width, width // 2
        block = source_ref[depth // BLOCK * width :].astype(F32)
        staging_ref[:half, low:] = block[:, :width]
        staging_ref[half:, low:] = block[:, width:]
    odd = is_odd()
    for chosen, target in ((odd, for_odd), (jnp.logical_not(odd), for_even)):

        @pl.when(chosen)
        def _():
            for copy in fetch((staging_ref,), (target,), sems):
                copy.wait()


def put_own_kernel(own_ref, first_hbm, second_hbm, staging_ref, sems):
    put(own_ref, second_hbm, first_hbm, staging_ref, sems)


def put_other_kernel(other_ref, first_in, second_in, first_hbm, second_hbm, staging_ref, sems):
    put(other_ref, first_hbm, second_hbm, staging_ref, sems)


def second_kernel(
    near_ref, far_ref, state_ref, rule_ref, x_ref, g_ref, w1_ref, w2_ref,
    out_ref, dx_ref,
    table_ref, hs_ref, ds_ref, turned_ref,
):
    _, rows = x_ref.shape
    blocks = rows // BLOCK
    odd = is_odd()
    for block in range(blocks):
        table_ref[block] = state_ref[block]
    fill_halo(table_ref, near_ref, far_ref, odd, blocks)
    gather(table_ref, rule_ref, hs_ref, ds_ref, blocks)
    turn(w1_ref, turned_ref)
    second = jnp.dot(w2_ref[...], hs_ref[...], preferred_element_type=F32)
    out_ref[...] = (second + x_ref[...].astype(F32)).astype(BF16)
    d_input = jnp.dot(turned_ref[...], ds_ref[...], preferred_element_type=F32)
    dx_ref[...] = (d_input + g_ref[...].astype(F32)).astype(BF16)


def neighbour_pairs(groups, count):
    near = [(i, i ^ 1) for i in range(groups * count)]
    far = []
    for group in range(groups):
        for i in range(count):
            other, tile = group, i + 1 if i % 2 else i - 1
            if not 0 <= tile < count:
                other, tile = (group + 1) % groups, i
            far.append((group * count + i, other * count + tile))
    return near, far


def total_over_tiles(keep, send, scale, shape):
    count = lax.axis_size("tile")
    cores = [(i, i ^ 1) for i in range(count)]
    received = lax.ppermute(send, "tile", cores)
    total = keep + received.astype(F32)
    bits = [1 << b for b in range(1, count.bit_length() - 1)]
    for step, (even_bit, odd_bit) in enumerate(zip(bits, bits[-1:] + bits[:-1])):
        wire = BF16 if step >= len(bits) - 3 else F32
        pairs = [(i, i ^ (odd_bit if i % 2 else even_bit)) for i in range(count)]
        sent = total.astype(wire)
        received = lax.ppermute(sent, "tile", pairs)
        total = sent.astype(F32) + received.astype(F32)
    total = (total * scale).astype(BF16)
    other = lax.ppermute(total, "tile", cores)
    result = jax.ShapeDtypeStruct(shape, F32)
    staging = [pltpu.VMEM(shape, F32), pltpu.SemaphoreType.DMA((1,))]
    put_own = pl.pallas_call(
        put_own_kernel,
        out_shape=(result, result),
        in_specs=[VMEM],
        out_specs=(HBM, HBM),
        scratch_shapes=staging,
        compiler_params=MEDIUM,
    )
    half = put_own(total)
    return pl.pallas_call(
        put_other_kernel,
        out_shape=(result, result),
        in_specs=[VMEM, HBM, HBM],
        out_specs=(HBM, HBM),
        scratch_shapes=staging,
        input_output_aliases={1: 0, 2: 1},
        compiler_params=MEDIUM,
    )(other, *half)


def body(features, rulebook, send_lists, weight_first, weight_second, cotangent):
    width, rows = features.shape
    offsets = rulebook.shape[0]
    blocks = rows // BLOCK
    count = lax.axis_size("tile")
    near_pairs, far_pairs = neighbour_pairs(lax.axis_size("groups"), count)
    axes = ("groups", "tile")
    send_lists = send_lists.reshape(2)
    features, cotangent, rulebook, weight_first, weight_second, send_lists = (
        pltpu.with_memory_space_constraint(array, pltpu.HBM)
        for array in (features, cotangent, rulebook, weight_first, weight_second, send_lists)
    )
    shape = jax.ShapeDtypeStruct
    rim = shape((2 * width, BLOCK), BF16)
    values = shape((width, rows), BF16)
    sums = shape((width, rows), F32)
    gathered = shape((offsets * width, rows), BF16)
    weight = shape((width, offsets * width), BF16)
    packed = (packed_rows(offsets, width), BLOCK)
    state_shape = shape((blocks, 2 * width, BLOCK), BF16)
    table = pltpu.VMEM((blocks + 2, 2 * width, BLOCK), BF16)

    near, far, lists, x, g, rule, w2, w1 = pl.pallas_call(
        load_kernel,
        out_shape=(
            rim, rim, shape((2, 8, BLOCK), jnp.int32), values, values,
            shape(rulebook.shape, jnp.int32), weight, weight,
        ),
        in_specs=[HBM] * 6,
        out_specs=(VMEM,) * 8,
        scratch_shapes=[pltpu.SMEM((2,), jnp.int32), pltpu.SemaphoreType.DMA((12,))],
        compiler_params=MEDIUM,
    )(send_lists, features, cotangent, rulebook, weight_second, weight_first)
    far = lax.ppermute(far, axes, far_pairs)
    near = lax.ppermute(near, axes, near_pairs)

    work = pl.CostEstimate(
        flops=2 * 2 * width * offsets * rows * (width + BLOCK),
        bytes_accessed=4 * offsets * width * rows,
        transcendentals=0,
    )
    own_phase = pl.pallas_call(
        own_kernel,
        out_shape=(gathered, gathered, sums, sums, weight),
        in_specs=[VMEM] * 5,
        out_specs=(VMEM,) * 5,
        scratch_shapes=[table],
        compiler_params=MEDIUM,
        cost_estimate=work,
    )
    xs, gs, pre, d_hidden, turned = own_phase(rule, x, g, w1, w2)
    state, near, far, send, xs, gs = pl.pallas_call(
        rim_kernel,
        out_shape=(state_shape, rim, rim, shape(packed, BF16), gathered, gathered),
        in_specs=[VMEM] * 10,
        out_specs=(VMEM,) * 6,
        scratch_shapes=[
            pltpu.VMEM((width, rows), F32),
            pltpu.VMEM((width, rows), F32),
            pltpu.VMEM((4, offsets // 3 * width, BLOCK), BF16),
        ],
        input_output_aliases={8: 4, 9: 5},
        compiler_params=MEDIUM,
    )(lists, near, far, pre, d_hidden, rule, w1, turned, xs, gs)
    keep_terms = pl.pallas_call(
        keep_kernel,
        out_shape=shape(packed, F32),
        in_specs=[VMEM] * 3,
        out_specs=VMEM,
        compiler_params=MEDIUM,
    )
    keep = keep_terms(state, xs, gs)

    near = lax.ppermute(near, axes, near_pairs)
    far = lax.ppermute(far, axes, far_pairs)
    second_phase = pl.pallas_call(
        second_kernel,
        out_shape=(values, values),
        in_specs=[VMEM] * 8,
        out_specs=(VMEM, VMEM),
        scratch_shapes=[
            table,
            pltpu.VMEM((offsets * width, rows), BF16),
            pltpu.VMEM((offsets * width, rows), BF16),
            pltpu.VMEM((width, offsets * width), BF16),
        ],
        compiler_params=MEDIUM,
        cost_estimate=work,
    )
    out_features, d_features = second_phase(near, far, state, rule, x, g, w1, w2)

    scale = 1.0 / math.sqrt(rows * count)
    grad_first, grad_second = total_over_tiles(keep, send, scale, weight.shape)
    return out_features, d_features, grad_first, grad_second


def solution(mesh):
    tiles = P(None, ("groups", "tile"))
    return jax.shard_map(
        body,
        mesh=mesh,
        in_specs=(tiles, tiles, tiles, P(), P(), tiles),
        out_specs=(tiles, tiles, P("groups", None), P("groups", None)),
        check_vma=False,
    )
```

```python
import math

import jax
import jax.numpy as jnp
from jax import lax
from jax.experimental import pallas as pl
from jax.experimental.pallas import tpu as pltpu
from jax.sharding import PartitionSpec as P


BLOCK = 128
F32, BF16 = jnp.float32, jnp.bfloat16
HBM = pl.BlockSpec(memory_space=pltpu.HBM)
MEDIUM = pltpu.CompilerParams(vmem_limit_bytes=20 << 20)
VMEM = pl.BlockSpec(memory_space=pltpu.VMEM)
NT = (((1,), (1,)), ((), ()))


def is_odd():
    return lax.axis_index("tile") % 2 == 1


def pair_blocks(listed, odd):
    lower, upper = listed
    return jnp.where(odd, lower, upper), jnp.where(odd, upper, lower)


def fetch(sources, targets, sems):
    copies = [
        pltpu.make_async_copy(source, target, sems.at[i])
        for i, (source, target) in enumerate(zip(sources, targets))
    ]
    for copy in copies:
        copy.start()
    return copies


def load_kernel(
    lists_hbm, x_hbm, g_hbm, rule_hbm, w2_hbm,
    near_ref, far_ref, lists_out, x_ref, g_ref, rule_ref, w2_ref,
    lists_ref, sems,
):
    width, rows = x_ref.shape
    copies = fetch(
        (lists_hbm, x_hbm, g_hbm, rule_hbm, w2_hbm),
        (lists_ref, x_ref, g_ref, rule_ref, w2_ref),
        sems,
    )
    for copy in copies[:3]:
        copy.wait()
    picks = pair_blocks((lists_ref[0], lists_ref[1]), is_odd())
    for pick, out_ref in zip(picks, (near_ref, far_ref)):
        start = pl.multiple_of(jnp.minimum(pick, rows // BLOCK - 1) * BLOCK, BLOCK)
        out_ref[:width, :] = x_ref[:, pl.ds(start, BLOCK)]
        out_ref[width:, :] = g_ref[:, pl.ds(start, BLOCK)]
    for side in range(2):
        lists_out[side] = jnp.full(lists_out.shape[1:], lists_ref[side], jnp.int32)
    for copy in copies[3:]:
        copy.wait()


def fill_halo(table_ref, near_ref, far_ref, odd, blocks):
    near, far = near_ref[...], far_ref[...]
    table_ref[blocks] = jnp.where(odd, near, far)
    table_ref[blocks + 1] = jnp.where(odd, far, near)


def one_hot(rows, line):
    return (rows == line).astype(F32).astype(BF16)


def select_rows(table, rows, local):
    found = []
    for j in range(0, local.shape[0], 2):
        lines = [local[i : i + 1] for i in range(j, min(j + 2, local.shape[0]))]
        choice = jnp.concatenate([one_hot(rows, line) for line in lines], axis=1)
        both = jnp.dot(table, choice, preferred_element_type=F32).astype(BF16)
        found += [both[:, i * BLOCK : (i + 1) * BLOCK] for i in range(len(lines))]
    return found


def gather(table_ref, rule_ref, first_ref, second_ref, blocks):
    offsets = rule_ref.shape[0]
    group = offsets // 3
    sources, channels, _ = table_ref.shape
    width = channels // 2
    source_rows = lax.broadcasted_iota(jnp.int32, (BLOCK, BLOCK), 0)

    def store(k, low, high, found, mirrored):
        first_ref[k * width : (k + 1) * width, low:high] = found[:width]
        second_ref[mirrored * width : (mirrored + 1) * width, low:high] = found[width:]

    strays = jnp.zeros((group, BLOCK), jnp.int32)
    for block in range(blocks):
        low, high = block * BLOCK, (block + 1) * BLOCK
        for side in range(3):
            entries = rule_ref[side * group : (side + 1) * group, low:high]
            if side == 1:
                source = block
            else:
                least = jnp.min(entries.astype(F32)).astype(jnp.int32)
                source = jnp.minimum(least // BLOCK, sources - 1)
            local = entries - source * BLOCK
            named = entries < sources * BLOCK
            strays = strays | (
                named & ((local < 0) | (local >= BLOCK))
            ).astype(jnp.int32)
            for j, found in enumerate(select_rows(table_ref[source], source_rows, local)):
                k = side * group + j
                store(k, low, high, found, offsets - 1 - k)

    @pl.when(jnp.max(strays.astype(F32)) > 0)
    def _():
        rows = rule_ref.shape[1]
        every_row = lax.broadcasted_iota(jnp.int32, (BLOCK, rows), 0)

        def one(k, carry):
            line = rule_ref[pl.ds(k, 1), :]
            found = jnp.zeros((channels, rows), F32)
            for source in range(sources):
                choice = one_hot(every_row, line - source * BLOCK)
                found += jnp.dot(table_ref[source], choice, preferred_element_type=F32)
            here = pl.multiple_of(k * width, width)
            there = pl.multiple_of((offsets - 1 - k) * width, width)
            first_ref[pl.ds(here, width), :] = found[:width].astype(BF16)
            second_ref[pl.ds(there, width), :] = found[width:].astype(BF16)
            return carry

        lax.fori_loop(0, offsets, one, 0)


def turn(weight_ref, turned_ref):
    width, depth = weight_ref.shape
    offsets = depth // width
    for k in range(0, offsets, 2):
        count = min(2, offsets - k)
        block = weight_ref[:, k * width : (k + count) * width].astype(F32).T
        pieces = [block[i * width : (i + 1) * width] for i in range(count)]
        joined = pieces[0] if count == 1 else jnp.concatenate(pieces, axis=1)
        turned_ref[:, k * width : (k + count) * width] = joined.astype(BF16)


def own_kernel(
    rule_ref, x_ref, g_ref, w2_ref, w1_hbm,
    xs_ref, gs_ref, pre_ref, d_hidden_ref, turned_ref, w1_ref,
    table_ref, sems,
):
    copies = fetch((w1_hbm,), (w1_ref,), sems)
    width, rows = x_ref.shape
    blocks = rows // BLOCK
    for block in range(blocks):
        low, high = block * BLOCK, (block + 1) * BLOCK
        table_ref[block, :width] = x_ref[:, low:high]
        table_ref[block, width:] = g_ref[:, low:high]
    table_ref[blocks:] = jnp.zeros_like(table_ref[blocks:])
    gather(table_ref, rule_ref, xs_ref, gs_ref, blocks)
    turn(w2_ref, turned_ref)
    d_hidden_ref[...] = jnp.dot(turned_ref[...], gs_ref[...], preferred_element_type=F32)
    for copy in copies:
        copy.wait()
    pre_ref[...] = jnp.dot(w1_ref[...], xs_ref[...], preferred_element_type=F32)


def packed_rows(offsets, width):
    return offsets * width * width // BLOCK


def pack(out_ref, pair, pieces):
    width = pieces[0].shape[0]
    if len(pieces) == 1:
        pieces = [pieces[0][: width // 2], pieces[0][width // 2 :]]
    joined = jnp.concatenate(pieces, axis=1)
    row = pair * width
    out_ref[row : row + joined.shape[0]] = joined.astype(out_ref.dtype)


def first_terms(state_ref, xs_ref, out_ref):
    blocks = state_ref.shape[0]
    width = state_ref.shape[1] // 2
    depth = xs_ref.shape[0]
    d_pre = jnp.concatenate([state_ref[block, width:] for block in range(blocks)], axis=1)
    for low in range(0, depth, 8 * width):
        high = min(depth, low + 8 * width)
        terms = lax.dot_general(d_pre, xs_ref[low:high], NT, preferred_element_type=F32)
        for at in range(low, high, 2 * width):
            end = min(high, at + 2 * width)
            pair = terms[:, at - low : end - low]
            if end - at == BLOCK:
                row = at // BLOCK * width
                out_ref[row : row + width] = pair.astype(out_ref.dtype)
            else:
                pack(out_ref, at // BLOCK, [pair])


def second_terms(state_ref, gs_ref, out_ref):
    blocks = state_ref.shape[0]
    width = state_ref.shape[1] // 2
    depth = gs_ref.shape[0]
    hidden = jnp.concatenate([state_ref[block, :width] for block in range(blocks)], axis=1)
    for low in range(0, depth, 4 * width):
        high = min(depth, low + 4 * width)
        terms = lax.dot_general(gs_ref[low:high], hidden, NT, preferred_element_type=F32)
        for at in range(low, high, 2 * width):
            pieces = [
                terms[i - low : i - low + width] for i in range(at, min(high, at + 2 * width), width)
            ]
            pack(out_ref, at // BLOCK, pieces)


def rim_kernel(
    lists_ref, near_ref, far_ref, pre_in, d_hidden_in, rule_ref, w1_ref, turned_ref, xs_in, gs_in,
    state_ref, near_out, far_out, send_ref, xs_ref, gs_ref,
    pre_ref, d_hidden_ref, rim_ref,
):
    width, rows = pre_in.shape
    blocks = rows // BLOCK
    offsets = rule_ref.shape[0]
    group = offsets // 3
    odd = is_odd()
    listed = [jnp.max(lists_ref[side].astype(F32)).astype(jnp.int32) for side in range(2)]
    near, far = near_ref[...], far_ref[...]
    tables = (jnp.where(odd, near, far), jnp.where(odd, far, near))
    pre_ref[...] = pre_in[...]
    d_hidden_ref[...] = d_hidden_in[...]
    source_rows = lax.broadcasted_iota(jnp.int32, (BLOCK, BLOCK), 0)
    sides = []
    for side in range(2):
        columns = pl.ds(pl.multiple_of(jnp.minimum(listed[side], blocks - 1) * BLOCK, BLOCK), BLOCK)
        start = 2 * side * group
        mirrored = offsets - group - start
        span = slice(start * width, (start + group) * width)
        mirror_span = slice(mirrored * width, (mirrored + group) * width)
        sides.append((listed[side] < blocks, columns, span, mirror_span))
        local = rule_ref[start : start + group, columns] - (blocks + side) * BLOCK
        for j, found in enumerate(select_rows(tables[side], source_rows, local)):
            rim_ref[2 * side, j * width : (j + 1) * width] = found[:width]
            place = (group - 1 - j) * width
            rim_ref[2 * side + 1, place : place + width] = found[width:]
    for side, (named, columns, span, mirror_span) in enumerate(sides):
        rim_x, rim_g = rim_ref[2 * side], rim_ref[2 * side + 1]
        pre_ref[:, columns] += jnp.dot(w1_ref[:, span], rim_x, preferred_element_type=F32)
        d_hidden_ref[:, columns] += jnp.dot(
            turned_ref[:, mirror_span], rim_g, preferred_element_type=F32
        )
        xs_ref[span, columns] = jnp.where(named, rim_x, xs_ref[span, columns])
        gs_ref[mirror_span, columns] = jnp.where(named, rim_g, gs_ref[mirror_span, columns])
    pre = pre_ref[...]
    sigma = jax.nn.sigmoid(pre)
    hidden = (pre * sigma).astype(BF16)
    d_pre = (d_hidden_ref[...] * sigma * (1.0 + pre * (1.0 - sigma))).astype(BF16)
    for block in range(blocks):
        low, high = block * BLOCK, (block + 1) * BLOCK
        state_ref[block, :width] = hidden[:, low:high]
        state_ref[block, width:] = d_pre[:, low:high]
    for pick, out_ref in zip(pair_blocks(listed, odd), (near_out, far_out)):
        out_ref[...] = state_ref[jnp.minimum(pick, blocks - 1)]

    @pl.when(odd)
    def _():
        first_terms(state_ref, xs_ref, send_ref)

    @pl.when(jnp.logical_not(odd))
    def _():
        second_terms(state_ref, gs_ref, send_ref)


def keep_kernel(state_ref, xs_ref, gs_ref, keep_ref):
    odd = is_odd()

    @pl.when(odd)
    def _():
        second_terms(state_ref, gs_ref, keep_ref)

    @pl.when(jnp.logical_not(odd))
    def _():
        first_terms(state_ref, xs_ref, keep_ref)


def put(source_ref, for_odd, for_even, staging_ref, sems):
    width, depth = staging_ref.shape
    pairs = depth // BLOCK
    cuts = [0, pairs // 3 * BLOCK, 2 * pairs // 3 * BLOCK, depth]

    def unpack(low, high):
        for at in range(low, high, BLOCK):
            row = at // BLOCK * width
            if at + BLOCK <= high:
                staging_ref[:, at : at + BLOCK] = source_ref[row : row + width].astype(F32)
            else:
                half = width // 2
                block = source_ref[row : row + half].astype(F32)
                staging_ref[:half, at:high] = block[:, :width]
                staging_ref[half:, at:high] = block[:, width:]

    odd = is_odd()
    for chosen, target in ((odd, for_odd), (jnp.logical_not(odd), for_even)):

        @pl.when(chosen)
        def _():
            copies = []
            for i, (low, high) in enumerate(zip(cuts, cuts[1:])):
                unpack(low, high)
                place = pl.ds(low, high - low)
                copies.append(
                    pltpu.make_async_copy(staging_ref.at[:, place], target.at[:, place], sems.at[i])
                )
                copies[-1].start()
            for copy in copies:
                copy.wait()


def put_own_kernel(own_ref, first_hbm, second_hbm, staging_ref, sems):
    put(own_ref, second_hbm, first_hbm, staging_ref, sems)


def put_other_kernel(other_ref, first_in, second_in, first_hbm, second_hbm, staging_ref, sems):
    put(other_ref, first_hbm, second_hbm, staging_ref, sems)


def second_kernel(
    near_ref, far_ref, state_ref, rule_ref, x_ref, g_ref, w1_ref, w2_ref,
    out_ref, dx_ref,
    table_ref, hs_ref, ds_ref, turned_ref,
):
    _, rows = x_ref.shape
    blocks = rows // BLOCK
    odd = is_odd()
    for block in range(blocks):
        table_ref[block] = state_ref[block]
    fill_halo(table_ref, near_ref, far_ref, odd, blocks)
    gather(table_ref, rule_ref, hs_ref, ds_ref, blocks)
    turn(w1_ref, turned_ref)
    second = jnp.dot(w2_ref[...], hs_ref[...], preferred_element_type=F32)
    out_ref[...] = (second + x_ref[...].astype(F32)).astype(BF16)
    d_input = jnp.dot(turned_ref[...], ds_ref[...], preferred_element_type=F32)
    dx_ref[...] = (d_input + g_ref[...].astype(F32)).astype(BF16)


def neighbour_pairs(groups, count):
    near = [(i, i ^ 1) for i in range(groups * count)]
    far = []
    for group in range(groups):
        for i in range(count):
            other, tile = group, i + 1 if i % 2 else i - 1
            if not 0 <= tile < count:
                other, tile = (group + 1) % groups, i
            far.append((group * count + i, other * count + tile))
    return near, far


def total_over_tiles(keep, send, scale, shape):
    count = lax.axis_size("tile")
    cores = [(i, i ^ 1) for i in range(count)]
    received = lax.ppermute(send, "tile", cores)
    total = keep + received.astype(F32)
    bits = [1 << b for b in range(1, count.bit_length() - 1)]
    for step, (even_bit, odd_bit) in enumerate(zip(bits, bits[-1:] + bits[:-1])):
        wire = BF16 if step >= len(bits) - 3 else F32
        pairs = [(i, i ^ (odd_bit if i % 2 else even_bit)) for i in range(count)]
        sent = total.astype(wire)
        received = lax.ppermute(sent, "tile", pairs)
        total = sent.astype(F32) + received.astype(F32)
    total = (total * scale).astype(BF16)
    other = lax.ppermute(total, "tile", cores)
    result = jax.ShapeDtypeStruct(shape, F32)
    staging = [pltpu.VMEM(shape, F32), pltpu.SemaphoreType.DMA((3,))]
    put_own = pl.pallas_call(
        put_own_kernel,
        out_shape=(result, result),
        in_specs=[VMEM],
        out_specs=(HBM, HBM),
        scratch_shapes=staging,
        compiler_params=MEDIUM,
    )
    half = put_own(total)
    return pl.pallas_call(
        put_other_kernel,
        out_shape=(result, result),
        in_specs=[VMEM, HBM, HBM],
        out_specs=(HBM, HBM),
        scratch_shapes=staging,
        input_output_aliases={1: 0, 2: 1},
        compiler_params=MEDIUM,
    )(other, *half)


def body(features, rulebook, send_lists, weight_first, weight_second, cotangent):
    width, rows = features.shape
    offsets = rulebook.shape[0]
    blocks = rows // BLOCK
    count = lax.axis_size("tile")
    near_pairs, far_pairs = neighbour_pairs(lax.axis_size("groups"), count)
    axes = ("groups", "tile")
    send_lists = send_lists.reshape(2)
    features, cotangent, rulebook, weight_first, weight_second, send_lists = (
        pltpu.with_memory_space_constraint(array, pltpu.HBM)
        for array in (features, cotangent, rulebook, weight_first, weight_second, send_lists)
    )
    shape = jax.ShapeDtypeStruct
    rim = shape((2 * width, BLOCK), BF16)
    values = shape((width, rows), BF16)
    sums = shape((width, rows), F32)
    gathered = shape((offsets * width, rows), BF16)
    weight = shape((width, offsets * width), BF16)
    packed = (packed_rows(offsets, width), BLOCK)
    state_shape = shape((blocks, 2 * width, BLOCK), BF16)
    table = pltpu.VMEM((blocks + 2, 2 * width, BLOCK), BF16)

    near, far, lists, x, g, rule, w2 = pl.pallas_call(
        load_kernel,
        out_shape=(
            rim, rim, shape((2, 8, BLOCK), jnp.int32), values, values,
            shape(rulebook.shape, jnp.int32), weight,
        ),
        in_specs=[HBM] * 5,
        out_specs=(VMEM,) * 7,
        scratch_shapes=[pltpu.SMEM((2,), jnp.int32), pltpu.SemaphoreType.DMA((5,))],
        compiler_params=MEDIUM,
    )(send_lists, features, cotangent, rulebook, weight_second)
    far = lax.ppermute(far, axes, far_pairs)
    near = lax.ppermute(near, axes, near_pairs)

    work = pl.CostEstimate(
        flops=2 * 2 * width * offsets * rows * (width + BLOCK),
        bytes_accessed=4 * offsets * width * rows,
        transcendentals=0,
    )
    own_phase = pl.pallas_call(
        own_kernel,
        out_shape=(gathered, gathered, sums, sums, weight, weight),
        in_specs=[VMEM] * 4 + [HBM],
        out_specs=(VMEM,) * 6,
        scratch_shapes=[table, pltpu.SemaphoreType.DMA((1,))],
        compiler_params=MEDIUM,
        cost_estimate=work,
    )
    xs, gs, pre, d_hidden, turned, w1 = own_phase(rule, x, g, w2, weight_first)
    state, near, far, send, xs, gs = pl.pallas_call(
        rim_kernel,
        out_shape=(state_shape, rim, rim, shape(packed, BF16), gathered, gathered),
        in_specs=[VMEM] * 10,
        out_specs=(VMEM,) * 6,
        scratch_shapes=[
            pltpu.VMEM((width, rows), F32),
            pltpu.VMEM((width, rows), F32),
            pltpu.VMEM((4, offsets // 3 * width, BLOCK), BF16),
        ],
        input_output_aliases={8: 4, 9: 5},
        compiler_params=MEDIUM,
    )(lists, near, far, pre, d_hidden, rule, w1, turned, xs, gs)
    keep_terms = pl.pallas_call(
        keep_kernel,
        out_shape=shape(packed, F32),
        in_specs=[VMEM] * 3,
        out_specs=VMEM,
        compiler_params=MEDIUM,
    )
    keep = keep_terms(state, xs, gs)

    near = lax.ppermute(near, axes, near_pairs)
    far = lax.ppermute(far, axes, far_pairs)
    second_phase = pl.pallas_call(
        second_kernel,
        out_shape=(values, values),
        in_specs=[VMEM] * 8,
        out_specs=(VMEM, VMEM),
        scratch_shapes=[
            table,
            pltpu.VMEM((offsets * width, rows), BF16),
            pltpu.VMEM((offsets * width, rows), BF16),
            pltpu.VMEM((width, offsets * width), BF16),
        ],
        compiler_params=MEDIUM,
        cost_estimate=work,
    )
    out_features, d_features = second_phase(near, far, state, rule, x, g, w1, w2)

    scale = 1.0 / math.sqrt(rows * count)
    grad_first, grad_second = total_over_tiles(keep, send, scale, weight.shape)
    return out_features, d_features, grad_first, grad_second


def solution(mesh):
    tiles = P(None, ("groups", "tile"))
    return jax.shard_map(
        body,
        mesh=mesh,
        in_specs=(tiles, tiles, tiles, P(), P(), tiles),
        out_specs=(tiles, tiles, P("groups", None), P("groups", None)),
        check_vma=False,
    )
```

```python
import math

import jax
import jax.numpy as jnp
from jax import lax
from jax.experimental import pallas as pl
from jax.experimental.pallas import tpu as pltpu
from jax.sharding import PartitionSpec as P


BLOCK = 128
F32, BF16 = jnp.float32, jnp.bfloat16
HBM = pl.BlockSpec(memory_space=pltpu.HBM)
MEDIUM = pltpu.CompilerParams(vmem_limit_bytes=20 << 20)
VMEM = pl.BlockSpec(memory_space=pltpu.VMEM)
NT = (((1,), (1,)), ((), ()))


def is_odd():
    return lax.axis_index("tile") % 2 == 1


def pair_blocks(listed, odd):
    lower, upper = listed
    return jnp.where(odd, lower, upper), jnp.where(odd, upper, lower)


def fetch(sources, targets, sems):
    copies = [
        pltpu.make_async_copy(source, target, sems.at[i])
        for i, (source, target) in enumerate(zip(sources, targets))
    ]
    for copy in copies:
        copy.start()
    return copies


def load_kernel(
    lists_hbm, x_hbm, g_hbm, rule_hbm, w2_hbm,
    near_ref, far_ref, lists_out, x_ref, g_ref, rule_ref, w2_ref,
    lists_ref, sems,
):
    width, rows = x_ref.shape
    copies = fetch(
        (lists_hbm, x_hbm, g_hbm, rule_hbm, w2_hbm),
        (lists_ref, x_ref, g_ref, rule_ref, w2_ref),
        sems,
    )
    for copy in copies[:3]:
        copy.wait()
    picks = pair_blocks((lists_ref[0], lists_ref[1]), is_odd())
    for pick, out_ref in zip(picks, (near_ref, far_ref)):
        start = pl.multiple_of(jnp.minimum(pick, rows // BLOCK - 1) * BLOCK, BLOCK)
        out_ref[:width, :] = x_ref[:, pl.ds(start, BLOCK)]
        out_ref[width:, :] = g_ref[:, pl.ds(start, BLOCK)]
    for side in range(2):
        lists_out[side] = jnp.full(lists_out.shape[1:], lists_ref[side], jnp.int32)
    for copy in copies[3:]:
        copy.wait()


def fill_halo(table_ref, near_ref, far_ref, odd, blocks):
    near, far = near_ref[...], far_ref[...]
    table_ref[blocks] = jnp.where(odd, near, far)
    table_ref[blocks + 1] = jnp.where(odd, far, near)


def one_hot(rows, line):
    return (rows == line).astype(F32).astype(BF16)


def select_rows(table, rows, local):
    found = []
    for j in range(0, local.shape[0], 2):
        lines = [local[i : i + 1] for i in range(j, min(j + 2, local.shape[0]))]
        choice = jnp.concatenate([one_hot(rows, line) for line in lines], axis=1)
        both = jnp.dot(table, choice, preferred_element_type=F32).astype(BF16)
        found += [both[:, i * BLOCK : (i + 1) * BLOCK] for i in range(len(lines))]
    return found


def gather(table_ref, rule_ref, first_ref, second_ref, blocks):
    offsets = rule_ref.shape[0]
    group = offsets // 3
    sources, channels, _ = table_ref.shape
    width = channels // 2
    source_rows = lax.broadcasted_iota(jnp.int32, (BLOCK, BLOCK), 0)

    def store(k, low, high, found, mirrored):
        first_ref[k * width : (k + 1) * width, low:high] = found[:width]
        second_ref[mirrored * width : (mirrored + 1) * width, low:high] = found[width:]

    strays = jnp.zeros((group, BLOCK), jnp.int32)
    for block in range(blocks):
        low, high = block * BLOCK, (block + 1) * BLOCK
        for side in range(3):
            entries = rule_ref[side * group : (side + 1) * group, low:high]
            if side == 1:
                source = block
            else:
                least = jnp.min(entries.astype(F32)).astype(jnp.int32)
                source = jnp.minimum(least // BLOCK, sources - 1)
            local = entries - source * BLOCK
            named = entries < sources * BLOCK
            strays = strays | (
                named & ((local < 0) | (local >= BLOCK))
            ).astype(jnp.int32)
            for j, found in enumerate(select_rows(table_ref[source], source_rows, local)):
                k = side * group + j
                store(k, low, high, found, offsets - 1 - k)

    @pl.when(jnp.max(strays.astype(F32)) > 0)
    def _():
        rows = rule_ref.shape[1]
        every_row = lax.broadcasted_iota(jnp.int32, (BLOCK, rows), 0)

        def one(k, carry):
            line = rule_ref[pl.ds(k, 1), :]
            found = jnp.zeros((channels, rows), F32)
            for source in range(sources):
                choice = one_hot(every_row, line - source * BLOCK)
                found += jnp.dot(table_ref[source], choice, preferred_element_type=F32)
            here = pl.multiple_of(k * width, width)
            there = pl.multiple_of((offsets - 1 - k) * width, width)
            first_ref[pl.ds(here, width), :] = found[:width].astype(BF16)
            second_ref[pl.ds(there, width), :] = found[width:].astype(BF16)
            return carry

        lax.fori_loop(0, offsets, one, 0)


def turn(weight_ref, turned_ref):
    width, depth = weight_ref.shape
    offsets = depth // width
    for k in range(0, offsets, 2):
        count = min(2, offsets - k)
        block = weight_ref[:, k * width : (k + count) * width].astype(F32).T
        pieces = [block[i * width : (i + 1) * width] for i in range(count)]
        joined = pieces[0] if count == 1 else jnp.concatenate(pieces, axis=1)
        turned_ref[:, k * width : (k + count) * width] = joined.astype(BF16)


def own_kernel(
    rule_ref, x_ref, g_ref, w2_ref, w1_hbm,
    xs_ref, gs_ref, pre_ref, d_hidden_ref, turned_ref, w1_ref,
    table_ref, sems,
):
    copies = fetch((w1_hbm,), (w1_ref,), sems)
    width, rows = x_ref.shape
    blocks = rows // BLOCK
    for block in range(blocks):
        low, high = block * BLOCK, (block + 1) * BLOCK
        table_ref[block, :width] = x_ref[:, low:high]
        table_ref[block, width:] = g_ref[:, low:high]
    table_ref[blocks:] = jnp.zeros_like(table_ref[blocks:])
    gather(table_ref, rule_ref, xs_ref, gs_ref, blocks)
    turn(w2_ref, turned_ref)
    d_hidden_ref[...] = jnp.dot(turned_ref[...], gs_ref[...], preferred_element_type=F32)
    for copy in copies:
        copy.wait()
    pre_ref[...] = jnp.dot(w1_ref[...], xs_ref[...], preferred_element_type=F32)


def packed_rows(offsets, width):
    return offsets * width * width // BLOCK


def pack(out_ref, pair, pieces):
    width = pieces[0].shape[0]
    if len(pieces) == 1:
        pieces = [pieces[0][: width // 2], pieces[0][width // 2 :]]
    joined = jnp.concatenate(pieces, axis=1)
    row = pair * width
    out_ref[row : row + joined.shape[0]] = joined.astype(out_ref.dtype)


def first_terms(state_ref, xs_ref, out_ref):
    blocks = state_ref.shape[0]
    width = state_ref.shape[1] // 2
    depth = xs_ref.shape[0]
    d_pre = jnp.concatenate([state_ref[block, width:] for block in range(blocks)], axis=1)
    for low in range(0, depth, 8 * width):
        high = min(depth, low + 8 * width)
        terms = lax.dot_general(d_pre, xs_ref[low:high], NT, preferred_element_type=F32)
        for at in range(low, high, 2 * width):
            end = min(high, at + 2 * width)
            pair = terms[:, at - low : end - low]
            if end - at == BLOCK:
                row = at // BLOCK * width
                out_ref[row : row + width] = pair.astype(out_ref.dtype)
            else:
                pack(out_ref, at // BLOCK, [pair])


def second_terms(state_ref, gs_ref, out_ref):
    blocks = state_ref.shape[0]
    width = state_ref.shape[1] // 2
    depth = gs_ref.shape[0]
    hidden = jnp.concatenate([state_ref[block, :width] for block in range(blocks)], axis=1)
    for low in range(0, depth, 4 * width):
        high = min(depth, low + 4 * width)
        terms = lax.dot_general(gs_ref[low:high], hidden, NT, preferred_element_type=F32)
        for at in range(low, high, 2 * width):
            pieces = [
                terms[i - low : i - low + width] for i in range(at, min(high, at + 2 * width), width)
            ]
            pack(out_ref, at // BLOCK, pieces)


def rim_kernel(
    lists_ref, near_ref, far_ref, pre_in, d_hidden_in, rule_ref, w1_ref, turned_ref, xs_in, gs_in,
    state_ref, near_out, far_out, send_ref, xs_ref, gs_ref,
    pre_ref, d_hidden_ref, rim_ref,
):
    width, rows = pre_in.shape
    blocks = rows // BLOCK
    offsets = rule_ref.shape[0]
    group = offsets // 3
    odd = is_odd()
    listed = [jnp.max(lists_ref[side].astype(F32)).astype(jnp.int32) for side in range(2)]
    near, far = near_ref[...], far_ref[...]
    tables = (jnp.where(odd, near, far), jnp.where(odd, far, near))
    pre_ref[...] = pre_in[...]
    d_hidden_ref[...] = d_hidden_in[...]
    source_rows = lax.broadcasted_iota(jnp.int32, (BLOCK, BLOCK), 0)
    sides = []
    for side in range(2):
        columns = pl.ds(pl.multiple_of(jnp.minimum(listed[side], blocks - 1) * BLOCK, BLOCK), BLOCK)
        start = 2 * side * group
        mirrored = offsets - group - start
        span = slice(start * width, (start + group) * width)
        mirror_span = slice(mirrored * width, (mirrored + group) * width)
        sides.append((listed[side] < blocks, columns, span, mirror_span))
        local = rule_ref[start : start + group, columns] - (blocks + side) * BLOCK
        for j, found in enumerate(select_rows(tables[side], source_rows, local)):
            rim_ref[2 * side, j * width : (j + 1) * width] = found[:width]
            place = (group - 1 - j) * width
            rim_ref[2 * side + 1, place : place + width] = found[width:]
    for side, (named, columns, span, mirror_span) in enumerate(sides):
        rim_x, rim_g = rim_ref[2 * side], rim_ref[2 * side + 1]
        pre_ref[:, columns] += jnp.dot(w1_ref[:, span], rim_x, preferred_element_type=F32)
        d_hidden_ref[:, columns] += jnp.dot(
            turned_ref[:, mirror_span], rim_g, preferred_element_type=F32
        )
        xs_ref[span, columns] = jnp.where(named, rim_x, xs_ref[span, columns])
        gs_ref[mirror_span, columns] = jnp.where(named, rim_g, gs_ref[mirror_span, columns])
    pre = pre_ref[...]
    sigma = jax.nn.sigmoid(pre)
    hidden = (pre * sigma).astype(BF16)
    d_pre = (d_hidden_ref[...] * sigma * (1.0 + pre * (1.0 - sigma))).astype(BF16)
    for block in range(blocks):
        low, high = block * BLOCK, (block + 1) * BLOCK
        state_ref[block, :width] = hidden[:, low:high]
        state_ref[block, width:] = d_pre[:, low:high]
    for pick, out_ref in zip(pair_blocks(listed, odd), (near_out, far_out)):
        out_ref[...] = state_ref[jnp.minimum(pick, blocks - 1)]

    @pl.when(odd)
    def _():
        first_terms(state_ref, xs_ref, send_ref)

    @pl.when(jnp.logical_not(odd))
    def _():
        second_terms(state_ref, gs_ref, send_ref)


def keep_kernel(state_ref, xs_ref, gs_ref, keep_ref):
    odd = is_odd()

    @pl.when(odd)
    def _():
        second_terms(state_ref, gs_ref, keep_ref)

    @pl.when(jnp.logical_not(odd))
    def _():
        first_terms(state_ref, xs_ref, keep_ref)


def put(source_ref, for_odd, for_even, staging_ref, sems):
    width, depth = staging_ref.shape
    pairs = depth // BLOCK
    cuts = [0, pairs // 3 * BLOCK, 2 * pairs // 3 * BLOCK, depth]

    def unpack(low, high):
        for at in range(low, high, BLOCK):
            row = at // BLOCK * width
            if at + BLOCK <= high:
                staging_ref[:, at : at + BLOCK] = source_ref[row : row + width].astype(F32)
            else:
                half = width // 2
                block = source_ref[row : row + half].astype(F32)
                staging_ref[:half, at:high] = block[:, :width]
                staging_ref[half:, at:high] = block[:, width:]

    odd = is_odd()
    for chosen, target in ((odd, for_odd), (jnp.logical_not(odd), for_even)):

        @pl.when(chosen)
        def _():
            copies = []
            for i, (low, high) in enumerate(zip(cuts, cuts[1:])):
                unpack(low, high)
                place = pl.ds(low, high - low)
                copies.append(
                    pltpu.make_async_copy(staging_ref.at[:, place], target.at[:, place], sems.at[i])
                )
                copies[-1].start()
            for copy in copies:
                copy.wait()


def put_own_kernel(own_ref, first_hbm, second_hbm, staging_ref, sems):
    put(own_ref, second_hbm, first_hbm, staging_ref, sems)


def put_other_kernel(other_ref, first_in, second_in, first_hbm, second_hbm, staging_ref, sems):
    put(other_ref, first_hbm, second_hbm, staging_ref, sems)


def second_kernel(
    near_ref, far_ref, state_ref, rule_ref, x_ref, g_ref, w1_ref, w2_ref,
    out_ref, dx_ref,
    table_ref, hs_ref, ds_ref, turned_ref,
):
    _, rows = x_ref.shape
    blocks = rows // BLOCK
    odd = is_odd()
    for block in range(blocks):
        table_ref[block] = state_ref[block]
    fill_halo(table_ref, near_ref, far_ref, odd, blocks)
    gather(table_ref, rule_ref, hs_ref, ds_ref, blocks)
    turn(w1_ref, turned_ref)
    second = jnp.dot(w2_ref[...], hs_ref[...], preferred_element_type=F32)
    out_ref[...] = (second + x_ref[...].astype(F32)).astype(BF16)
    d_input = jnp.dot(turned_ref[...], ds_ref[...], preferred_element_type=F32)
    dx_ref[...] = (d_input + g_ref[...].astype(F32)).astype(BF16)


def neighbour_pairs(groups, count):
    near = [(i, i ^ 1) for i in range(groups * count)]
    far = []
    for group in range(groups):
        for i in range(count):
            other, tile = group, i + 1 if i % 2 else i - 1
            if not 0 <= tile < count:
                other, tile = (group + 1) % groups, i
            far.append((group * count + i, other * count + tile))
    return near, far


def total_over_tiles(keep, send, scale, shape):
    count = lax.axis_size("tile")
    cores = [(i, i ^ 1) for i in range(count)]
    received = lax.ppermute(send, "tile", cores)
    total = keep + received.astype(F32)
    index = lax.axis_index("tile")
    bits = [1 << b for b in range(1, count.bit_length() - 1)]
    routes = list(zip(bits, bits[-1:] + bits[:-1]))
    exchanges = [[(i, i ^ route[i % 2]) for i in range(count)] for route in routes]
    high = jnp.where(index % 2 == 1, index // routes[0][1], index // routes[0][0]) % 2 == 1
    half = total.shape[0] // 2
    for step, pairs in enumerate(exchanges):
        wire = BF16 if step >= len(bits) - 3 else F32
        if step == 0:
            sent = jnp.where(high, total[:half], total[half:]).astype(wire)
            total = jnp.where(high, total[half:], total[:half])
        else:
            sent = total.astype(wire)
            total = sent.astype(F32)
        received = lax.ppermute(sent, "tile", pairs)
        total = total + received.astype(F32)
    total = (total * scale).astype(BF16)
    rest = lax.ppermute(total, "tile", exchanges[0])
    total = jnp.where(high, jnp.concatenate([rest, total]), jnp.concatenate([total, rest]))
    other = lax.ppermute(total, "tile", cores)
    result = jax.ShapeDtypeStruct(shape, F32)
    staging = [pltpu.VMEM(shape, F32), pltpu.SemaphoreType.DMA((3,))]
    put_own = pl.pallas_call(
        put_own_kernel,
        out_shape=(result, result),
        in_specs=[VMEM],
        out_specs=(HBM, HBM),
        scratch_shapes=staging,
        compiler_params=MEDIUM,
    )
    half = put_own(total)
    return pl.pallas_call(
        put_other_kernel,
        out_shape=(result, result),
        in_specs=[VMEM, HBM, HBM],
        out_specs=(HBM, HBM),
        scratch_shapes=staging,
        input_output_aliases={1: 0, 2: 1},
        compiler_params=MEDIUM,
    )(other, *half)


def body(features, rulebook, send_lists, weight_first, weight_second, cotangent):
    width, rows = features.shape
    offsets = rulebook.shape[0]
    blocks = rows // BLOCK
    count = lax.axis_size("tile")
    near_pairs, far_pairs = neighbour_pairs(lax.axis_size("groups"), count)
    axes = ("groups", "tile")
    send_lists = send_lists.reshape(2)
    features, cotangent, rulebook, weight_first, weight_second, send_lists = (
        pltpu.with_memory_space_constraint(array, pltpu.HBM)
        for array in (features, cotangent, rulebook, weight_first, weight_second, send_lists)
    )
    shape = jax.ShapeDtypeStruct
    rim = shape((2 * width, BLOCK), BF16)
    values = shape((width, rows), BF16)
    sums = shape((width, rows), F32)
    gathered = shape((offsets * width, rows), BF16)
    weight = shape((width, offsets * width), BF16)
    packed = (packed_rows(offsets, width), BLOCK)
    state_shape = shape((blocks, 2 * width, BLOCK), BF16)
    table = pltpu.VMEM((blocks + 2, 2 * width, BLOCK), BF16)

    near, far, lists, x, g, rule, w2 = pl.pallas_call(
        load_kernel,
        out_shape=(
            rim, rim, shape((2, 8, BLOCK), jnp.int32), values, values,
            shape(rulebook.shape, jnp.int32), weight,
        ),
        in_specs=[HBM] * 5,
        out_specs=(VMEM,) * 7,
        scratch_shapes=[pltpu.SMEM((2,), jnp.int32), pltpu.SemaphoreType.DMA((5,))],
        compiler_params=MEDIUM,
    )(send_lists, features, cotangent, rulebook, weight_second)
    far = lax.ppermute(far, axes, far_pairs)
    near = lax.ppermute(near, axes, near_pairs)

    work = pl.CostEstimate(
        flops=2 * 2 * width * offsets * rows * (width + BLOCK),
        bytes_accessed=4 * offsets * width * rows,
        transcendentals=0,
    )
    own_phase = pl.pallas_call(
        own_kernel,
        out_shape=(gathered, gathered, sums, sums, weight, weight),
        in_specs=[VMEM] * 4 + [HBM],
        out_specs=(VMEM,) * 6,
        scratch_shapes=[table, pltpu.SemaphoreType.DMA((1,))],
        compiler_params=MEDIUM,
        cost_estimate=work,
    )
    xs, gs, pre, d_hidden, turned, w1 = own_phase(rule, x, g, w2, weight_first)
    state, near, far, send, xs, gs = pl.pallas_call(
        rim_kernel,
        out_shape=(state_shape, rim, rim, shape(packed, BF16), gathered, gathered),
        in_specs=[VMEM] * 10,
        out_specs=(VMEM,) * 6,
        scratch_shapes=[
            pltpu.VMEM((width, rows), F32),
            pltpu.VMEM((width, rows), F32),
            pltpu.VMEM((4, offsets // 3 * width, BLOCK), BF16),
        ],
        input_output_aliases={8: 4, 9: 5},
        compiler_params=MEDIUM,
    )(lists, near, far, pre, d_hidden, rule, w1, turned, xs, gs)
    keep_terms = pl.pallas_call(
        keep_kernel,
        out_shape=shape(packed, F32),
        in_specs=[VMEM] * 3,
        out_specs=VMEM,
        compiler_params=MEDIUM,
    )
    keep = keep_terms(state, xs, gs)

    near = lax.ppermute(near, axes, near_pairs)
    far = lax.ppermute(far, axes, far_pairs)
    second_phase = pl.pallas_call(
        second_kernel,
        out_shape=(values, values),
        in_specs=[VMEM] * 8,
        out_specs=(VMEM, VMEM),
        scratch_shapes=[
            table,
            pltpu.VMEM((offsets * width, rows), BF16),
            pltpu.VMEM((offsets * width, rows), BF16),
            pltpu.VMEM((width, offsets * width), BF16),
        ],
        compiler_params=MEDIUM,
        cost_estimate=work,
    )
    out_features, d_features = second_phase(near, far, state, rule, x, g, w1, w2)

    scale = 1.0 / math.sqrt(rows * count)
    grad_first, grad_second = total_over_tiles(keep, send, scale, weight.shape)
    return out_features, d_features, grad_first, grad_second


def solution(mesh):
    tiles = P(None, ("groups", "tile"))
    return jax.shard_map(
        body,
        mesh=mesh,
        in_specs=(tiles, tiles, tiles, P(), P(), tiles),
        out_specs=(tiles, tiles, P("groups", None), P("groups", None)),
        check_vma=False,
    )
```

```python
import math

import jax
import jax.numpy as jnp
from jax import lax
from jax.experimental import pallas as pl
from jax.experimental.pallas import tpu as pltpu
from jax.sharding import PartitionSpec as P


BLOCK = 128
F32, BF16 = jnp.float32, jnp.bfloat16
HBM = pl.BlockSpec(memory_space=pltpu.HBM)
MEDIUM = pltpu.CompilerParams(vmem_limit_bytes=20 << 20)
VMEM = pl.BlockSpec(memory_space=pltpu.VMEM)
NT = (((1,), (1,)), ((), ()))


def is_odd():
    return lax.axis_index("tile") % 2 == 1


def pair_blocks(listed, odd):
    lower, upper = listed
    return jnp.where(odd, lower, upper), jnp.where(odd, upper, lower)


def fetch(sources, targets, sems):
    copies = [
        pltpu.make_async_copy(source, target, sems.at[i])
        for i, (source, target) in enumerate(zip(sources, targets))
    ]
    for copy in copies:
        copy.start()
    return copies


def load_kernel(
    lists_hbm, x_hbm, g_hbm, rule_hbm, w2_hbm,
    near_ref, far_ref, lists_out, x_ref, g_ref, rule_ref, w2_ref,
    lists_ref, sems,
):
    width, rows = x_ref.shape
    copies = fetch(
        (lists_hbm, x_hbm, g_hbm, rule_hbm, w2_hbm),
        (lists_ref, x_ref, g_ref, rule_ref, w2_ref),
        sems,
    )
    for copy in copies[:3]:
        copy.wait()
    picks = pair_blocks((lists_ref[0], lists_ref[1]), is_odd())
    for pick, out_ref in zip(picks, (near_ref, far_ref)):
        start = pl.multiple_of(jnp.minimum(pick, rows // BLOCK - 1) * BLOCK, BLOCK)
        out_ref[:width, :] = x_ref[:, pl.ds(start, BLOCK)]
        out_ref[width:, :] = g_ref[:, pl.ds(start, BLOCK)]
    for side in range(2):
        lists_out[side] = jnp.full(lists_out.shape[1:], lists_ref[side], jnp.int32)
    for copy in copies[3:]:
        copy.wait()


def fill_halo(table_ref, near_ref, far_ref, odd, blocks):
    near, far = near_ref[...], far_ref[...]
    table_ref[blocks] = jnp.where(odd, near, far)
    table_ref[blocks + 1] = jnp.where(odd, far, near)


def one_hot(rows, line):
    return (rows == line).astype(F32).astype(BF16)


def select_rows(table, rows, local):
    found = []
    for j in range(0, local.shape[0], 2):
        lines = [local[i : i + 1] for i in range(j, min(j + 2, local.shape[0]))]
        choice = jnp.concatenate([one_hot(rows, line) for line in lines], axis=1)
        both = jnp.dot(table, choice, preferred_element_type=F32).astype(BF16)
        found += [both[:, i * BLOCK : (i + 1) * BLOCK] for i in range(len(lines))]
    return found


def gather(table_ref, rule_ref, first_ref, second_ref, blocks):
    offsets = rule_ref.shape[0]
    group = offsets // 3
    sources, channels, _ = table_ref.shape
    width = channels // 2
    source_rows = lax.broadcasted_iota(jnp.int32, (BLOCK, BLOCK), 0)

    def store(k, low, high, found, mirrored):
        first_ref[k * width : (k + 1) * width, low:high] = found[:width]
        second_ref[mirrored * width : (mirrored + 1) * width, low:high] = found[width:]

    strays = jnp.zeros((group, BLOCK), jnp.int32)
    for block in range(blocks):
        low, high = block * BLOCK, (block + 1) * BLOCK
        for side in range(3):
            entries = rule_ref[side * group : (side + 1) * group, low:high]
            if side == 1:
                source = block
            else:
                least = jnp.min(entries.astype(F32)).astype(jnp.int32)
                source = jnp.minimum(least // BLOCK, sources - 1)
            local = entries - source * BLOCK
            named = entries < sources * BLOCK
            strays = strays | (
                named & ((local < 0) | (local >= BLOCK))
            ).astype(jnp.int32)
            for j, found in enumerate(select_rows(table_ref[source], source_rows, local)):
                k = side * group + j
                store(k, low, high, found, offsets - 1 - k)

    @pl.when(jnp.max(strays.astype(F32)) > 0)
    def _():
        rows = rule_ref.shape[1]
        every_row = lax.broadcasted_iota(jnp.int32, (BLOCK, rows), 0)

        def one(k, carry):
            line = rule_ref[pl.ds(k, 1), :]
            found = jnp.zeros((channels, rows), F32)
            for source in range(sources):
                choice = one_hot(every_row, line - source * BLOCK)
                found += jnp.dot(table_ref[source], choice, preferred_element_type=F32)
            here = pl.multiple_of(k * width, width)
            there = pl.multiple_of((offsets - 1 - k) * width, width)
            first_ref[pl.ds(here, width), :] = found[:width].astype(BF16)
            second_ref[pl.ds(there, width), :] = found[width:].astype(BF16)
            return carry

        lax.fori_loop(0, offsets, one, 0)


def turn(weight_ref, turned_ref):
    width, depth = weight_ref.shape
    offsets = depth // width
    for k in range(0, offsets, 2):
        count = min(2, offsets - k)
        block = weight_ref[:, k * width : (k + count) * width].astype(F32).T
        pieces = [block[i * width : (i + 1) * width] for i in range(count)]
        joined = pieces[0] if count == 1 else jnp.concatenate(pieces, axis=1)
        turned_ref[:, k * width : (k + count) * width] = joined.astype(BF16)


def listed_blocks(lists_ref):
    return [jnp.max(lists_ref[side].astype(F32)).astype(jnp.int32) for side in range(2)]


def halo_rows(side, listed, table, rule_ref, blocks):
    width = table.shape[0] // 2
    offsets = rule_ref.shape[0]
    group = offsets // 3
    upper = side == 1
    block = jnp.where(upper, listed[1], listed[0])
    columns = pl.ds(pl.multiple_of(jnp.minimum(block, blocks - 1) * BLOCK, BLOCK), BLOCK)
    far_start = (offsets - group) * width
    start = pl.multiple_of(jnp.where(upper, far_start, 0), BLOCK)
    mirrored = pl.multiple_of(jnp.where(upper, 0, far_start), BLOCK)
    lines = jnp.where(
        upper, rule_ref[offsets - group : offsets, columns], rule_ref[:group, columns]
    )
    local = lines - (blocks + side) * BLOCK
    found = select_rows(table, lax.broadcasted_iota(jnp.int32, (BLOCK, BLOCK), 0), local)
    first = [rows[:width] for rows in found]
    second = [rows[width:] for rows in found[::-1]]
    depth = group * width
    return block < blocks, columns, pl.ds(start, depth), pl.ds(mirrored, depth), first, second


def own_gather_kernel(
    rule_ref, x_ref, g_ref, w1_hbm, xs_ref, gs_ref, w1_ref, table_ref, sems
):
    copies = fetch((w1_hbm,), (w1_ref,), sems)
    width, rows = x_ref.shape
    blocks = rows // BLOCK
    for block in range(blocks):
        low, high = block * BLOCK, (block + 1) * BLOCK
        table_ref[block, :width] = x_ref[:, low:high]
        table_ref[block, width:] = g_ref[:, low:high]
    table_ref[blocks:] = jnp.zeros_like(table_ref[blocks:])
    gather(table_ref, rule_ref, xs_ref, gs_ref, blocks)
    for copy in copies:
        copy.wait()


def insert_rows(target_ref, span, columns, named, pieces):
    width = pieces[0].shape[0]
    for i, piece in enumerate(pieces):
        place = pl.ds(pl.multiple_of(span.start + i * width, width), width)
        target_ref[place, columns] = jnp.where(named, piece, target_ref[place, columns])


def own_conv_kernel(
    lists_ref, near_ref, rule_ref, w1_ref, w2_ref, xs_in, gs_in,
    pre_ref, d_hidden_ref, turned_ref, xs_ref, gs_ref,
):
    blocks = pre_ref.shape[1] // BLOCK
    turn(w2_ref, turned_ref)
    side = jnp.where(is_odd(), 0, 1)
    named, columns, span, mirror_span, first, second = halo_rows(
        side, listed_blocks(lists_ref), near_ref[...], rule_ref, blocks
    )
    insert_rows(xs_ref, span, columns, named, first)
    insert_rows(gs_ref, mirror_span, columns, named, second)
    d_hidden_ref[...] = jnp.dot(turned_ref[...], gs_ref[...], preferred_element_type=F32)
    pre_ref[...] = jnp.dot(w1_ref[...], xs_ref[...], preferred_element_type=F32)


def packed_rows(offsets, width):
    return offsets * width * width // BLOCK


def pack(out_ref, pair, pieces):
    width = pieces[0].shape[0]
    if len(pieces) == 1:
        pieces = [pieces[0][: width // 2], pieces[0][width // 2 :]]
    joined = jnp.concatenate(pieces, axis=1)
    row = pair * width
    out_ref[row : row + joined.shape[0]] = joined.astype(out_ref.dtype)


def first_terms(state_ref, xs_ref, out_ref):
    blocks = state_ref.shape[0]
    width = state_ref.shape[1] // 2
    depth = xs_ref.shape[0]
    d_pre = jnp.concatenate([state_ref[block, width:] for block in range(blocks)], axis=1)
    for low in range(0, depth, 8 * width):
        high = min(depth, low + 8 * width)
        terms = lax.dot_general(d_pre, xs_ref[low:high], NT, preferred_element_type=F32)
        for at in range(low, high, 2 * width):
            end = min(high, at + 2 * width)
            pair = terms[:, at - low : end - low]
            if end - at == BLOCK:
                row = at // BLOCK * width
                out_ref[row : row + width] = pair.astype(out_ref.dtype)
            else:
                pack(out_ref, at // BLOCK, [pair])


def second_terms(state_ref, gs_ref, out_ref):
    blocks = state_ref.shape[0]
    width = state_ref.shape[1] // 2
    depth = gs_ref.shape[0]
    hidden = jnp.concatenate([state_ref[block, :width] for block in range(blocks)], axis=1)
    for low in range(0, depth, 4 * width):
        high = min(depth, low + 4 * width)
        terms = lax.dot_general(gs_ref[low:high], hidden, NT, preferred_element_type=F32)
        for at in range(low, high, 2 * width):
            pieces = [
                terms[i - low : i - low + width] for i in range(at, min(high, at + 2 * width), width)
            ]
            pack(out_ref, at // BLOCK, pieces)


def rim_kernel(
    lists_ref, far_ref, pre_in, d_hidden_in, rule_ref, w1_ref, turned_ref, xs_in, gs_in,
    state_ref, near_out, far_out, send_ref, xs_ref, gs_ref,
    pre_ref, d_hidden_ref, rim_ref,
):
    width, rows = pre_in.shape
    blocks = rows // BLOCK
    odd = is_odd()
    listed = listed_blocks(lists_ref)
    named, columns, span, mirror_span, first, second = halo_rows(
        jnp.where(odd, 1, 0), listed, far_ref[...], rule_ref, blocks
    )
    pre_ref[...] = pre_in[...]
    d_hidden_ref[...] = d_hidden_in[...]
    for i, (x_rows, g_rows) in enumerate(zip(first, second)):
        rim_ref[0, i * width : (i + 1) * width] = x_rows
        rim_ref[1, i * width : (i + 1) * width] = g_rows
    pre_ref[:, columns] += jnp.dot(w1_ref[:, span], rim_ref[0], preferred_element_type=F32)
    d_hidden_ref[:, columns] += jnp.dot(
        turned_ref[:, mirror_span], rim_ref[1], preferred_element_type=F32
    )
    insert_rows(xs_ref, span, columns, named, first)
    insert_rows(gs_ref, mirror_span, columns, named, second)
    pre = pre_ref[...]
    sigma = jax.nn.sigmoid(pre)
    hidden = (pre * sigma).astype(BF16)
    d_pre = (d_hidden_ref[...] * sigma * (1.0 + pre * (1.0 - sigma))).astype(BF16)
    for block in range(blocks):
        low, high = block * BLOCK, (block + 1) * BLOCK
        state_ref[block, :width] = hidden[:, low:high]
        state_ref[block, width:] = d_pre[:, low:high]
    for pick, out_ref in zip(pair_blocks(listed, odd), (near_out, far_out)):
        out_ref[...] = state_ref[jnp.minimum(pick, blocks - 1)]

    @pl.when(odd)
    def _():
        first_terms(state_ref, xs_ref, send_ref)

    @pl.when(jnp.logical_not(odd))
    def _():
        second_terms(state_ref, gs_ref, send_ref)


def keep_kernel(state_ref, xs_ref, gs_ref, keep_ref):
    odd = is_odd()

    @pl.when(odd)
    def _():
        second_terms(state_ref, gs_ref, keep_ref)

    @pl.when(jnp.logical_not(odd))
    def _():
        first_terms(state_ref, xs_ref, keep_ref)


def put(source_ref, for_odd, for_even, staging_ref, sems):
    width, depth = staging_ref.shape
    pairs = depth // BLOCK
    cuts = [0, pairs // 3 * BLOCK, 2 * pairs // 3 * BLOCK, depth]

    def unpack(low, high):
        for at in range(low, high, BLOCK):
            row = at // BLOCK * width
            if at + BLOCK <= high:
                staging_ref[:, at : at + BLOCK] = source_ref[row : row + width].astype(F32)
            else:
                half = width // 2
                block = source_ref[row : row + half].astype(F32)
                staging_ref[:half, at:high] = block[:, :width]
                staging_ref[half:, at:high] = block[:, width:]

    odd = is_odd()
    for chosen, target in ((odd, for_odd), (jnp.logical_not(odd), for_even)):

        @pl.when(chosen)
        def _():
            copies = []
            for i, (low, high) in enumerate(zip(cuts, cuts[1:])):
                unpack(low, high)
                place = pl.ds(low, high - low)
                copies.append(
                    pltpu.make_async_copy(staging_ref.at[:, place], target.at[:, place], sems.at[i])
                )
                copies[-1].start()
            for copy in copies:
                copy.wait()


def put_own_kernel(own_ref, first_hbm, second_hbm, staging_ref, sems):
    put(own_ref, second_hbm, first_hbm, staging_ref, sems)


def put_other_kernel(other_ref, first_in, second_in, first_hbm, second_hbm, staging_ref, sems):
    put(other_ref, first_hbm, second_hbm, staging_ref, sems)


def second_kernel(
    near_ref, far_ref, state_ref, rule_ref, x_ref, g_ref, w1_ref, w2_ref,
    out_ref, dx_ref,
    table_ref, hs_ref, ds_ref, turned_ref,
):
    _, rows = x_ref.shape
    blocks = rows // BLOCK
    odd = is_odd()
    for block in range(blocks):
        table_ref[block] = state_ref[block]
    fill_halo(table_ref, near_ref, far_ref, odd, blocks)
    gather(table_ref, rule_ref, hs_ref, ds_ref, blocks)
    turn(w1_ref, turned_ref)
    second = jnp.dot(w2_ref[...], hs_ref[...], preferred_element_type=F32)
    out_ref[...] = (second + x_ref[...].astype(F32)).astype(BF16)
    d_input = jnp.dot(turned_ref[...], ds_ref[...], preferred_element_type=F32)
    dx_ref[...] = (d_input + g_ref[...].astype(F32)).astype(BF16)


def neighbour_pairs(groups, count):
    near = [(i, i ^ 1) for i in range(groups * count)]
    far = []
    for group in range(groups):
        for i in range(count):
            other, tile = group, i + 1 if i % 2 else i - 1
            if not 0 <= tile < count:
                other, tile = (group + 1) % groups, i
            far.append((group * count + i, other * count + tile))
    return near, far


def total_over_tiles(keep, send, scale, shape):
    count = lax.axis_size("tile")
    cores = [(i, i ^ 1) for i in range(count)]
    received = lax.ppermute(send, "tile", cores)
    total = keep + received.astype(F32)
    bits = [1 << b for b in range(1, count.bit_length() - 1)]
    for step, (even_bit, odd_bit) in enumerate(zip(bits, bits[-1:] + bits[:-1])):
        wire = BF16 if step >= len(bits) - 3 else F32
        pairs = [(i, i ^ (odd_bit if i % 2 else even_bit)) for i in range(count)]
        sent = total.astype(wire)
        received = lax.ppermute(sent, "tile", pairs)
        total = sent.astype(F32) + received.astype(F32)
    total = (total * scale).astype(BF16)
    other = lax.ppermute(total, "tile", cores)
    result = jax.ShapeDtypeStruct(shape, F32)
    staging = [pltpu.VMEM(shape, F32), pltpu.SemaphoreType.DMA((3,))]
    put_own = pl.pallas_call(
        put_own_kernel,
        out_shape=(result, result),
        in_specs=[VMEM],
        out_specs=(HBM, HBM),
        scratch_shapes=staging,
        compiler_params=MEDIUM,
    )
    half = put_own(total)
    return pl.pallas_call(
        put_other_kernel,
        out_shape=(result, result),
        in_specs=[VMEM, HBM, HBM],
        out_specs=(HBM, HBM),
        scratch_shapes=staging,
        input_output_aliases={1: 0, 2: 1},
        compiler_params=MEDIUM,
    )(other, *half)


def body(features, rulebook, send_lists, weight_first, weight_second, cotangent):
    width, rows = features.shape
    offsets = rulebook.shape[0]
    blocks = rows // BLOCK
    count = lax.axis_size("tile")
    near_pairs, far_pairs = neighbour_pairs(lax.axis_size("groups"), count)
    axes = ("groups", "tile")
    send_lists = send_lists.reshape(2)
    features, cotangent, rulebook, weight_first, weight_second, send_lists = (
        pltpu.with_memory_space_constraint(array, pltpu.HBM)
        for array in (features, cotangent, rulebook, weight_first, weight_second, send_lists)
    )
    shape = jax.ShapeDtypeStruct
    rim = shape((2 * width, BLOCK), BF16)
    values = shape((width, rows), BF16)
    sums = shape((width, rows), F32)
    gathered = shape((offsets * width, rows), BF16)
    weight = shape((width, offsets * width), BF16)
    packed = (packed_rows(offsets, width), BLOCK)
    state_shape = shape((blocks, 2 * width, BLOCK), BF16)
    table = pltpu.VMEM((blocks + 2, 2 * width, BLOCK), BF16)

    near, far, lists, x, g, rule, w2 = pl.pallas_call(
        load_kernel,
        out_shape=(
            rim, rim, shape((2, 8, BLOCK), jnp.int32), values, values,
            shape(rulebook.shape, jnp.int32), weight,
        ),
        in_specs=[HBM] * 5,
        out_specs=(VMEM,) * 7,
        scratch_shapes=[pltpu.SMEM((2,), jnp.int32), pltpu.SemaphoreType.DMA((5,))],
        compiler_params=MEDIUM,
    )(send_lists, features, cotangent, rulebook, weight_second)
    far = lax.ppermute(far, axes, far_pairs)
    near = lax.ppermute(near, axes, near_pairs)

    work = pl.CostEstimate(
        flops=2 * 2 * width * offsets * rows * (width + BLOCK),
        bytes_accessed=4 * offsets * width * rows,
        transcendentals=0,
    )
    own_gather = pl.pallas_call(
        own_gather_kernel,
        out_shape=(gathered, gathered, weight),
        in_specs=[VMEM] * 3 + [HBM],
        out_specs=(VMEM,) * 3,
        scratch_shapes=[table, pltpu.SemaphoreType.DMA((1,))],
        compiler_params=MEDIUM,
        cost_estimate=work,
    )
    xs, gs, w1 = own_gather(rule, x, g, weight_first)
    own_conv = pl.pallas_call(
        own_conv_kernel,
        out_shape=(sums, sums, weight, gathered, gathered),
        in_specs=[VMEM] * 7,
        out_specs=(VMEM,) * 5,
        input_output_aliases={5: 3, 6: 4},
        compiler_params=MEDIUM,
        cost_estimate=work,
    )
    pre, d_hidden, turned, xs, gs = own_conv(lists, near, rule, w1, w2, xs, gs)
    state, near, far, send, xs, gs = pl.pallas_call(
        rim_kernel,
        out_shape=(state_shape, rim, rim, shape(packed, BF16), gathered, gathered),
        in_specs=[VMEM] * 9,
        out_specs=(VMEM,) * 6,
        scratch_shapes=[
            pltpu.VMEM((width, rows), F32),
            pltpu.VMEM((width, rows), F32),
            pltpu.VMEM((2, offsets // 3 * width, BLOCK), BF16),
        ],
        input_output_aliases={7: 4, 8: 5},
        compiler_params=MEDIUM,
    )(lists, far, pre, d_hidden, rule, w1, turned, xs, gs)
    keep_terms = pl.pallas_call(
        keep_kernel,
        out_shape=shape(packed, F32),
        in_specs=[VMEM] * 3,
        out_specs=VMEM,
        compiler_params=MEDIUM,
    )
    keep = keep_terms(state, xs, gs)

    near = lax.ppermute(near, axes, near_pairs)
    far = lax.ppermute(far, axes, far_pairs)
    second_phase = pl.pallas_call(
        second_kernel,
        out_shape=(values, values),
        in_specs=[VMEM] * 8,
        out_specs=(VMEM, VMEM),
        scratch_shapes=[
            table,
            pltpu.VMEM((offsets * width, rows), BF16),
            pltpu.VMEM((offsets * width, rows), BF16),
            pltpu.VMEM((width, offsets * width), BF16),
        ],
        compiler_params=MEDIUM,
        cost_estimate=work,
    )
    out_features, d_features = second_phase(near, far, state, rule, x, g, w1, w2)

    scale = 1.0 / math.sqrt(rows * count)
    grad_first, grad_second = total_over_tiles(keep, send, scale, weight.shape)
    return out_features, d_features, grad_first, grad_second


def solution(mesh):
    tiles = P(None, ("groups", "tile"))
    return jax.shard_map(
        body,
        mesh=mesh,
        in_specs=(tiles, tiles, tiles, P(), P(), tiles),
        out_specs=(tiles, tiles, P("groups", None), P("groups", None)),
        check_vma=False,
    )
```

```python
import math

import jax
import jax.numpy as jnp
from jax import lax
from jax.experimental import pallas as pl
from jax.experimental.pallas import tpu as pltpu
from jax.sharding import PartitionSpec as P


BLOCK = 128
F32, BF16 = jnp.float32, jnp.bfloat16
HBM = pl.BlockSpec(memory_space=pltpu.HBM)
MEDIUM = pltpu.CompilerParams(vmem_limit_bytes=20 << 20)
VMEM = pl.BlockSpec(memory_space=pltpu.VMEM)
NT = (((1,), (1,)), ((), ()))


def is_odd():
    return lax.axis_index("tile") % 2 == 1


def pair_blocks(listed, odd):
    lower, upper = listed
    return jnp.where(odd, lower, upper), jnp.where(odd, upper, lower)


def fetch(sources, targets, sems):
    copies = [
        pltpu.make_async_copy(source, target, sems.at[i])
        for i, (source, target) in enumerate(zip(sources, targets))
    ]
    for copy in copies:
        copy.start()
    return copies


def load_kernel(
    lists_hbm, x_hbm, g_hbm, rule_hbm,
    near_ref, far_ref, lists_out, x_ref, g_ref, rule_ref,
    lists_ref, sems,
):
    width, rows = x_ref.shape
    copies = fetch(
        (lists_hbm, x_hbm, g_hbm, rule_hbm), (lists_ref, x_ref, g_ref, rule_ref), sems
    )
    for copy in copies[:3]:
        copy.wait()
    picks = pair_blocks((lists_ref[0], lists_ref[1]), is_odd())
    for pick, out_ref in zip(picks, (near_ref, far_ref)):
        start = pl.multiple_of(jnp.minimum(pick, rows // BLOCK - 1) * BLOCK, BLOCK)
        out_ref[:width, :] = x_ref[:, pl.ds(start, BLOCK)]
        out_ref[width:, :] = g_ref[:, pl.ds(start, BLOCK)]
    for side in range(2):
        lists_out[side] = jnp.full(lists_out.shape[1:], lists_ref[side], jnp.int32)
    for copy in copies[3:]:
        copy.wait()


def fill_halo(table_ref, near_ref, far_ref, odd, blocks):
    near, far = near_ref[...], far_ref[...]
    table_ref[blocks] = jnp.where(odd, near, far)
    table_ref[blocks + 1] = jnp.where(odd, far, near)


def one_hot(rows, line):
    return (rows == line).astype(F32).astype(BF16)


def select_rows(table, rows, local):
    found = []
    for j in range(0, local.shape[0], 2):
        lines = [local[i : i + 1] for i in range(j, min(j + 2, local.shape[0]))]
        choice = jnp.concatenate([one_hot(rows, line) for line in lines], axis=1)
        both = jnp.dot(table, choice, preferred_element_type=F32).astype(BF16)
        found += [both[:, i * BLOCK : (i + 1) * BLOCK] for i in range(len(lines))]
    return found


def gather(table_ref, rule_ref, first_ref, second_ref, blocks):
    offsets = rule_ref.shape[0]
    group = offsets // 3
    sources, channels, _ = table_ref.shape
    width = channels // 2
    source_rows = lax.broadcasted_iota(jnp.int32, (BLOCK, BLOCK), 0)

    def store(k, low, high, found, mirrored):
        first_ref[k * width : (k + 1) * width, low:high] = found[:width]
        second_ref[mirrored * width : (mirrored + 1) * width, low:high] = found[width:]

    strays = jnp.zeros((group, BLOCK), jnp.int32)
    for block in range(blocks):
        low, high = block * BLOCK, (block + 1) * BLOCK
        for side in range(3):
            entries = rule_ref[side * group : (side + 1) * group, low:high]
            if side == 1:
                source = block
            else:
                least = jnp.min(entries.astype(F32)).astype(jnp.int32)
                source = jnp.minimum(least // BLOCK, sources - 1)
            local = entries - source * BLOCK
            named = entries < sources * BLOCK
            strays = strays | (
                named & ((local < 0) | (local >= BLOCK))
            ).astype(jnp.int32)
            for j, found in enumerate(select_rows(table_ref[source], source_rows, local)):
                k = side * group + j
                store(k, low, high, found, offsets - 1 - k)

    @pl.when(jnp.max(strays.astype(F32)) > 0)
    def _():
        rows = rule_ref.shape[1]
        every_row = lax.broadcasted_iota(jnp.int32, (BLOCK, rows), 0)

        def one(k, carry):
            line = rule_ref[pl.ds(k, 1), :]
            found = jnp.zeros((channels, rows), F32)
            for source in range(sources):
                choice = one_hot(every_row, line - source * BLOCK)
                found += jnp.dot(table_ref[source], choice, preferred_element_type=F32)
            here = pl.multiple_of(k * width, width)
            there = pl.multiple_of((offsets - 1 - k) * width, width)
            first_ref[pl.ds(here, width), :] = found[:width].astype(BF16)
            second_ref[pl.ds(there, width), :] = found[width:].astype(BF16)
            return carry

        lax.fori_loop(0, offsets, one, 0)


def turn(weight_ref, turned_ref):
    width, depth = weight_ref.shape
    offsets = depth // width
    for k in range(0, offsets, 2):
        count = min(2, offsets - k)
        block = weight_ref[:, k * width : (k + count) * width].astype(F32).T
        pieces = [block[i * width : (i + 1) * width] for i in range(count)]
        joined = pieces[0] if count == 1 else jnp.concatenate(pieces, axis=1)
        turned_ref[:, k * width : (k + count) * width] = joined.astype(BF16)


def listed_blocks(lists_ref):
    return [jnp.max(lists_ref[side].astype(F32)).astype(jnp.int32) for side in range(2)]


def halo_rows(side, listed, table, rule_ref, blocks):
    width = table.shape[0] // 2
    offsets = rule_ref.shape[0]
    group = offsets // 3
    upper = side == 1
    block = jnp.where(upper, listed[1], listed[0])
    columns = pl.ds(pl.multiple_of(jnp.minimum(block, blocks - 1) * BLOCK, BLOCK), BLOCK)
    far_start = (offsets - group) * width
    start = pl.multiple_of(jnp.where(upper, far_start, 0), BLOCK)
    mirrored = pl.multiple_of(jnp.where(upper, 0, far_start), BLOCK)
    lines = jnp.where(
        upper, rule_ref[offsets - group : offsets, columns], rule_ref[:group, columns]
    )
    local = lines - (blocks + side) * BLOCK
    found = select_rows(table, lax.broadcasted_iota(jnp.int32, (BLOCK, BLOCK), 0), local)
    first = [rows[:width] for rows in found]
    second = [rows[width:] for rows in found[::-1]]
    depth = group * width
    return block < blocks, columns, pl.ds(start, depth), pl.ds(mirrored, depth), first, second


def own_gather_kernel(
    rule_ref, x_ref, g_ref, w2_hbm, w1_hbm,
    xs_ref, gs_ref, w2_ref, w1_ref,
    table_ref, sems,
):
    copies = fetch((w2_hbm, w1_hbm), (w2_ref, w1_ref), sems)
    width, rows = x_ref.shape
    blocks = rows // BLOCK
    for block in range(blocks):
        low, high = block * BLOCK, (block + 1) * BLOCK
        table_ref[block, :width] = x_ref[:, low:high]
        table_ref[block, width:] = g_ref[:, low:high]
    table_ref[blocks:] = jnp.zeros_like(table_ref[blocks:])
    gather(table_ref, rule_ref, xs_ref, gs_ref, blocks)
    for copy in copies:
        copy.wait()


def insert_rows(target_ref, span, columns, named, pieces):
    width = pieces[0].shape[0]
    for i, piece in enumerate(pieces):
        place = pl.ds(pl.multiple_of(span.start + i * width, width), width)
        target_ref[place, columns] = jnp.where(named, piece, target_ref[place, columns])


def own_conv_kernel(
    lists_ref, near_ref, rule_ref, w1_ref, w2_ref, xs_in, gs_in,
    pre_ref, d_hidden_ref, turned_ref, xs_ref, gs_ref,
):
    blocks = pre_ref.shape[1] // BLOCK
    turn(w2_ref, turned_ref)
    side = jnp.where(is_odd(), 0, 1)
    named, columns, span, mirror_span, first, second = halo_rows(
        side, listed_blocks(lists_ref), near_ref[...], rule_ref, blocks
    )
    insert_rows(xs_ref, span, columns, named, first)
    insert_rows(gs_ref, mirror_span, columns, named, second)
    d_hidden_ref[...] = jnp.dot(turned_ref[...], gs_ref[...], preferred_element_type=F32)
    pre_ref[...] = jnp.dot(w1_ref[...], xs_ref[...], preferred_element_type=F32)


def packed_rows(offsets, width):
    return offsets * width * width // BLOCK


def pack(out_ref, pair, pieces):
    width = pieces[0].shape[0]
    if len(pieces) == 1:
        pieces = [pieces[0][: width // 2], pieces[0][width // 2 :]]
    joined = jnp.concatenate(pieces, axis=1)
    row = pair * width
    out_ref[row : row + joined.shape[0]] = joined.astype(out_ref.dtype)


def first_terms(state_ref, xs_ref, out_ref):
    blocks = state_ref.shape[0]
    width = state_ref.shape[1] // 2
    depth = xs_ref.shape[0]
    d_pre = jnp.concatenate([state_ref[block, width:] for block in range(blocks)], axis=1)
    for low in range(0, depth, 8 * width):
        high = min(depth, low + 8 * width)
        terms = lax.dot_general(d_pre, xs_ref[low:high], NT, preferred_element_type=F32)
        for at in range(low, high, 2 * width):
            end = min(high, at + 2 * width)
            pair = terms[:, at - low : end - low]
            if end - at == BLOCK:
                row = at // BLOCK * width
                out_ref[row : row + width] = pair.astype(out_ref.dtype)
            else:
                pack(out_ref, at // BLOCK, [pair])


def second_terms(state_ref, gs_ref, out_ref):
    blocks = state_ref.shape[0]
    width = state_ref.shape[1] // 2
    depth = gs_ref.shape[0]
    hidden = jnp.concatenate([state_ref[block, :width] for block in range(blocks)], axis=1)
    for low in range(0, depth, 4 * width):
        high = min(depth, low + 4 * width)
        terms = lax.dot_general(gs_ref[low:high], hidden, NT, preferred_element_type=F32)
        for at in range(low, high, 2 * width):
            pieces = [
                terms[i - low : i - low + width] for i in range(at, min(high, at + 2 * width), width)
            ]
            pack(out_ref, at // BLOCK, pieces)


def rim_kernel(
    lists_ref, far_ref, pre_in, d_hidden_in, rule_ref, w1_ref, turned_ref, xs_in, gs_in,
    state_ref, near_out, far_out, send_ref, xs_ref, gs_ref,
    pre_ref, d_hidden_ref, rim_ref,
):
    width, rows = pre_in.shape
    blocks = rows // BLOCK
    odd = is_odd()
    listed = listed_blocks(lists_ref)
    named, columns, span, mirror_span, first, second = halo_rows(
        jnp.where(odd, 1, 0), listed, far_ref[...], rule_ref, blocks
    )
    pre_ref[...] = pre_in[...]
    d_hidden_ref[...] = d_hidden_in[...]
    for i, (x_rows, g_rows) in enumerate(zip(first, second)):
        rim_ref[0, i * width : (i + 1) * width] = x_rows
        rim_ref[1, i * width : (i + 1) * width] = g_rows
    pre_ref[:, columns] += jnp.dot(w1_ref[:, span], rim_ref[0], preferred_element_type=F32)
    d_hidden_ref[:, columns] += jnp.dot(
        turned_ref[:, mirror_span], rim_ref[1], preferred_element_type=F32
    )
    insert_rows(xs_ref, span, columns, named, first)
    insert_rows(gs_ref, mirror_span, columns, named, second)
    pre = pre_ref[...]
    sigma = jax.nn.sigmoid(pre)
    hidden = (pre * sigma).astype(BF16)
    d_pre = (d_hidden_ref[...] * sigma * (1.0 + pre * (1.0 - sigma))).astype(BF16)
    for block in range(blocks):
        low, high = block * BLOCK, (block + 1) * BLOCK
        state_ref[block, :width] = hidden[:, low:high]
        state_ref[block, width:] = d_pre[:, low:high]
    for pick, out_ref in zip(pair_blocks(listed, odd), (near_out, far_out)):
        out_ref[...] = state_ref[jnp.minimum(pick, blocks - 1)]

    @pl.when(odd)
    def _():
        first_terms(state_ref, xs_ref, send_ref)

    @pl.when(jnp.logical_not(odd))
    def _():
        second_terms(state_ref, gs_ref, send_ref)


def keep_kernel(state_ref, xs_ref, gs_ref, keep_ref):
    odd = is_odd()

    @pl.when(odd)
    def _():
        second_terms(state_ref, gs_ref, keep_ref)

    @pl.when(jnp.logical_not(odd))
    def _():
        first_terms(state_ref, xs_ref, keep_ref)


def put(source_ref, for_odd, for_even, staging_ref, sems):
    width, depth = staging_ref.shape
    pairs = depth // BLOCK
    cuts = [0, pairs // 2 * BLOCK, 6 * pairs // 7 * BLOCK, depth]

    def unpack(low, high):
        for at in range(low, high, BLOCK):
            row = at // BLOCK * width
            if at + BLOCK <= high:
                staging_ref[:, at : at + BLOCK] = source_ref[row : row + width].astype(F32)
            else:
                half = width // 2
                block = source_ref[row : row + half].astype(F32)
                staging_ref[:half, at:high] = block[:, :width]
                staging_ref[half:, at:high] = block[:, width:]

    odd = is_odd()
    for chosen, target in ((odd, for_odd), (jnp.logical_not(odd), for_even)):

        @pl.when(chosen)
        def _():
            copies = []
            for i, (low, high) in enumerate(zip(cuts, cuts[1:])):
                unpack(low, high)
                place = pl.ds(low, high - low)
                copies.append(
                    pltpu.make_async_copy(staging_ref.at[:, place], target.at[:, place], sems.at[i])
                )
                copies[-1].start()
            for copy in copies:
                copy.wait()


def put_own_kernel(own_ref, first_hbm, second_hbm, staging_ref, sems):
    put(own_ref, second_hbm, first_hbm, staging_ref, sems)


def put_other_kernel(other_ref, first_in, second_in, first_hbm, second_hbm, staging_ref, sems):
    put(other_ref, first_hbm, second_hbm, staging_ref, sems)


def second_kernel(
    near_ref, far_ref, state_ref, rule_ref, x_ref, g_ref, w1_ref, w2_ref,
    out_ref, dx_ref,
    table_ref, hs_ref, ds_ref, turned_ref,
):
    _, rows = x_ref.shape
    blocks = rows // BLOCK
    odd = is_odd()
    for block in range(blocks):
        table_ref[block] = state_ref[block]
    fill_halo(table_ref, near_ref, far_ref, odd, blocks)
    gather(table_ref, rule_ref, hs_ref, ds_ref, blocks)
    turn(w1_ref, turned_ref)
    second = jnp.dot(w2_ref[...], hs_ref[...], preferred_element_type=F32)
    out_ref[...] = (second + x_ref[...].astype(F32)).astype(BF16)
    d_input = jnp.dot(turned_ref[...], ds_ref[...], preferred_element_type=F32)
    dx_ref[...] = (d_input + g_ref[...].astype(F32)).astype(BF16)


def neighbour_pairs(groups, count):
    near = [(i, i ^ 1) for i in range(groups * count)]
    far = []
    for group in range(groups):
        for i in range(count):
            other, tile = group, i + 1 if i % 2 else i - 1
            if not 0 <= tile < count:
                other, tile = (group + 1) % groups, i
            far.append((group * count + i, other * count + tile))
    return near, far


def total_over_tiles(keep, send, scale, shape):
    count = lax.axis_size("tile")
    cores = [(i, i ^ 1) for i in range(count)]
    received = lax.ppermute(send, "tile", cores)
    total = keep + received.astype(F32)
    bits = [1 << b for b in range(1, count.bit_length() - 1)]
    for step, (even_bit, odd_bit) in enumerate(zip(bits[-1:] + bits[:-1], bits[-2:] + bits[:-2])):
        wire = BF16 if step >= len(bits) - 3 else F32
        pairs = [(i, i ^ (odd_bit if i % 2 else even_bit)) for i in range(count)]
        sent = total.astype(wire)
        received = lax.ppermute(sent, "tile", pairs)
        total = sent.astype(F32) + received.astype(F32)
    total = (total * scale).astype(BF16)
    other = lax.ppermute(total, "tile", cores)
    result = jax.ShapeDtypeStruct(shape, F32)
    staging = [pltpu.VMEM(shape, F32), pltpu.SemaphoreType.DMA((3,))]
    put_own = pl.pallas_call(
        put_own_kernel,
        out_shape=(result, result),
        in_specs=[VMEM],
        out_specs=(HBM, HBM),
        scratch_shapes=staging,
        compiler_params=MEDIUM,
    )
    half = put_own(total)
    return pl.pallas_call(
        put_other_kernel,
        out_shape=(result, result),
        in_specs=[VMEM, HBM, HBM],
        out_specs=(HBM, HBM),
        scratch_shapes=staging,
        input_output_aliases={1: 0, 2: 1},
        compiler_params=MEDIUM,
    )(other, *half)


def body(features, rulebook, send_lists, weight_first, weight_second, cotangent):
    width, rows = features.shape
    offsets = rulebook.shape[0]
    blocks = rows // BLOCK
    count = lax.axis_size("tile")
    near_pairs, far_pairs = neighbour_pairs(lax.axis_size("groups"), count)
    axes = ("groups", "tile")
    send_lists = send_lists.reshape(2)
    features, cotangent, rulebook, weight_first, weight_second, send_lists = (
        pltpu.with_memory_space_constraint(array, pltpu.HBM)
        for array in (features, cotangent, rulebook, weight_first, weight_second, send_lists)
    )
    shape = jax.ShapeDtypeStruct
    rim = shape((2 * width, BLOCK), BF16)
    values = shape((width, rows), BF16)
    sums = shape((width, rows), F32)
    gathered = shape((offsets * width, rows), BF16)
    weight = shape((width, offsets * width), BF16)
    packed = (packed_rows(offsets, width), BLOCK)
    state_shape = shape((blocks, 2 * width, BLOCK), BF16)
    table = pltpu.VMEM((blocks + 2, 2 * width, BLOCK), BF16)

    near, far, lists, x, g, rule = pl.pallas_call(
        load_kernel,
        out_shape=(
            rim, rim, shape((2, 8, BLOCK), jnp.int32), values, values,
            shape(rulebook.shape, jnp.int32),
        ),
        in_specs=[HBM] * 4,
        out_specs=(VMEM,) * 6,
        scratch_shapes=[pltpu.SMEM((2,), jnp.int32), pltpu.SemaphoreType.DMA((4,))],
        compiler_params=MEDIUM,
    )(send_lists, features, cotangent, rulebook)
    far = lax.ppermute(far, axes, far_pairs)
    near = lax.ppermute(near, axes, near_pairs)

    work = pl.CostEstimate(
        flops=2 * 2 * width * offsets * rows * (width + BLOCK),
        bytes_accessed=4 * offsets * width * rows,
        transcendentals=0,
    )
    own_gather = pl.pallas_call(
        own_gather_kernel,
        out_shape=(gathered, gathered, weight, weight),
        in_specs=[VMEM] * 3 + [HBM] * 2,
        out_specs=(VMEM,) * 4,
        scratch_shapes=[table, pltpu.SemaphoreType.DMA((2,))],
        compiler_params=MEDIUM,
        cost_estimate=work,
    )
    xs, gs, w2, w1 = own_gather(rule, x, g, weight_second, weight_first)
    own_conv = pl.pallas_call(
        own_conv_kernel,
        out_shape=(sums, sums, weight, gathered, gathered),
        in_specs=[VMEM] * 7,
        out_specs=(VMEM,) * 5,
        input_output_aliases={5: 3, 6: 4},
        compiler_params=MEDIUM,
        cost_estimate=work,
    )
    pre, d_hidden, turned, xs, gs = own_conv(lists, near, rule, w1, w2, xs, gs)
    state, near, far, send, xs, gs = pl.pallas_call(
        rim_kernel,
        out_shape=(state_shape, rim, rim, shape(packed, BF16), gathered, gathered),
        in_specs=[VMEM] * 9,
        out_specs=(VMEM,) * 6,
        scratch_shapes=[
            pltpu.VMEM((width, rows), F32),
            pltpu.VMEM((width, rows), F32),
            pltpu.VMEM((2, offsets // 3 * width, BLOCK), BF16),
        ],
        input_output_aliases={7: 4, 8: 5},
        compiler_params=MEDIUM,
    )(lists, far, pre, d_hidden, rule, w1, turned, xs, gs)
    keep_terms = pl.pallas_call(
        keep_kernel,
        out_shape=shape(packed, F32),
        in_specs=[VMEM] * 3,
        out_specs=VMEM,
        compiler_params=MEDIUM,
    )
    keep = keep_terms(state, xs, gs)

    near = lax.ppermute(near, axes, near_pairs)
    far = lax.ppermute(far, axes, far_pairs)
    second_phase = pl.pallas_call(
        second_kernel,
        out_shape=(values, values),
        in_specs=[VMEM] * 8,
        out_specs=(VMEM, VMEM),
        scratch_shapes=[
            table,
            pltpu.VMEM((offsets * width, rows), BF16),
            pltpu.VMEM((offsets * width, rows), BF16),
            pltpu.VMEM((width, offsets * width), BF16),
        ],
        compiler_params=MEDIUM,
        cost_estimate=work,
    )
    out_features, d_features = second_phase(near, far, state, rule, x, g, w1, w2)

    scale = 1.0 / math.sqrt(rows * count)
    grad_first, grad_second = total_over_tiles(keep, send, scale, weight.shape)
    return out_features, d_features, grad_first, grad_second


def solution(mesh):
    tiles = P(None, ("groups", "tile"))
    return jax.shard_map(
        body,
        mesh=mesh,
        in_specs=(tiles, tiles, tiles, P(), P(), tiles),
        out_specs=(tiles, tiles, P("groups", None), P("groups", None)),
        check_vma=False,
    )
```
